32 devices in a mesh: fsdp: 2 (over y), ctx: 4 (over z), tp: 4 (over x, core).
Axes of the slice: x: 2, y: 2, z: 4, core: 2. Of those that a mesh axis runs over, the one named last changes fastest.
Arguments:
- tokens: bfloat16 [8, 1024, 1024], P('fsdp', 'ctx'), may hold values from -6 to 6
- first_values: bfloat16 [8, 1024, 1024], P('fsdp', 'ctx', 'tp'), may hold values from -6 to 6
- out_grad: bfloat16 [8, 1024, 1024], P('fsdp', 'ctx'), may hold values from -6 to 6
- w_qkv: bfloat16 [1024, 3, 1024], P('fsdp', None, 'tp'), may hold values from -0.1875 to 0.1875
- output_weight: bfloat16 [1024, 1024], P('tp', 'fsdp'), may hold values from -1.5 to 1.5
- w_gate: bfloat16 [1024, 2816], P('fsdp', 'tp'), may hold values from -0.1875 to 0.1875
- w_up: bfloat16 [1024, 2816], P('fsdp', 'tp'), may hold values from -0.1875 to 0.1875
- w_down: bfloat16 [2816, 1024], P('tp', 'fsdp'), may hold values from -0.109375 to 0.109375
- gain_attn: bfloat16 [1024], P('fsdp'), may hold values from 0.5 to 1.5
- gain_mlp: bfloat16 [1024], P('fsdp'), may hold values from 0.5 to 1.5
- mix: float32 [16], P('tp'), may hold values from 0.3 to 0.7
Outputs:
- output: bfloat16 [8, 1024, 1024], P('fsdp', 'ctx')
- grad_tokens: float32 [8, 1024, 1024], P('fsdp', 'ctx')
- grad_first: float32 [8, 1024, 1024], P('fsdp', 'ctx', 'tp')
- grad_w_qkv: float32 [1024, 3, 1024], P('fsdp', None, 'tp')
- grad_w_out: float32 [1024, 1024], P('tp', 'fsdp')
- grad_w_gate: float32 [1024, 2816], P('fsdp', 'tp')
- grad_w_up: float32 [1024, 2816], P('fsdp', 'tp')
- grad_w_down: float32 [2816, 1024], P('tp', 'fsdp')
- grad_gain_attn: float32 [1024], P('fsdp')
- grad_gain_mlp: float32 [1024], P('fsdp')
- grad_mix: float32 [16], P('tp')
The draws below stay inside these ranges and needn't reach their ends.
All inputs are finite; a program needn't handle non-finite values.
Results may differ from the reference program's by a relative error of at most 0.019.
Values may be sent and summed in bfloat16 or wider, within the bound.
No kernel may reach another device: no remote copies, remote signals or barrier semaphores. Data moves between devices by JAX's collectives and lax.ppermute only.
A program may use at most 128 MiB of HBM per device.

```python
import jax
import jax.numpy as jnp
from jax import lax

D = 1024
HEADS = 16
HEAD = 64
FF = 2816
BLOCK = 256
SEQ_DEV = 4
SEQ_LEN = 1024
SEQS = 8


def with_spikes(values, own_key, source, target, shards_of, factor):
    owner, partner = [(jnp.arange(values.shape[axis_at]) // (values.shape[axis_at] // shards_of)).reshape([-1 if axis == axis_at else 1 for axis in range(values.ndim)]) for axis_at in (source, target)]
    chosen = jax.random.permutation(own_key, shards_of)[partner]
    strong = (owner == chosen) | (owner == (partner + shards_of // 2) % shards_of)
    return jnp.where(strong, factor * values, values)


def block_levels(rng, dims, pieces, least, top_value):
    factor_of = 1.0
    for axis_at, shards_of in pieces:
        draws = jax.random.uniform(jax.random.fold_in(jax.random.fold_in(rng, 6), axis_at), (shards_of,), jnp.float32, least / len(pieces), top_value / len(pieces))
        factor_of = factor_of * jnp.repeat(jnp.exp(draws), dims[axis_at] // shards_of).reshape((-1,) + (1,) * (len(dims) - 1 - axis_at))
    return factor_of


def normal_values(own_key, shape, spread, reach, shards=(), held_as=jnp.bfloat16):
    array = jax.random.normal(own_key, shape, jnp.float32) * spread
    if len(shards) > 0:
        array = block_levels(own_key, shape, shards, -0.22, 0.18) * array
    return jnp.clip(array, min=-reach, max=reach).astype(held_as)


def heavy_noise(stream_key, extent, deviation, limit, pieces, heavy, held_as=jnp.bfloat16):
    entries = deviation * jax.random.normal(stream_key, extent, jnp.float32)
    if pieces:
        entries = entries * block_levels(stream_key, extent, pieces, -0.22, 0.18)
    return jnp.clip(with_spikes(entries, jax.random.fold_in(stream_key, 3), *heavy), -limit, limit).astype(held_as)


def setup_inputs(seed: int = 0) -> dict:
    arg_keys = jax.random.split(jax.random.key(seed), 12)
    return {
        "tokens": normal_values(arg_keys[0], (SEQS, SEQ_LEN, D), 1.0, 6.0, ((0, 2), (1, 4))),
        "first_values": normal_values(arg_keys[1], (SEQS, SEQ_LEN, D), 1.0, 6.0, ((0, 2), (1, 4), (2, 4))),
        "out_grad": heavy_noise(arg_keys[2], (SEQS, SEQ_LEN, D), 1.0, 6.0, ((0, 2), (1, 4)), (0, 2, 2, 2.0)),
        "w_qkv": normal_values(arg_keys[3], (D, 3, D), D ** -0.5, 0.1875, ((0, 2), (2, 4))),
        "output_weight": normal_values(arg_keys[4], (D, D), (max(D // 64, 1)) ** -0.5, 1.5, ((0, 4), (1, 2))),
        "w_gate": normal_values(arg_keys[5], (D, FF), D ** -0.5, 0.1875, ((0, 2), (1, 4))),
        "w_up": normal_values(arg_keys[6], (D, FF), D ** -0.5, 0.1875, ((0, 2), (1, 4))),
        "w_down": normal_values(arg_keys[7], (FF, D), FF ** -0.5, 0.109375, ((0, 4), (1, 2))),
        "gain_attn": jnp.clip(1.0 + 0.1 * jax.random.normal(arg_keys[8], (D,), jnp.float32), 0.5, 1.5).astype(jnp.bfloat16),
        "gain_mlp": jnp.clip(1.0 + 0.1 * jax.random.normal(arg_keys[9], (D,), jnp.float32), 0.5, 1.5).astype(jnp.bfloat16),
        "mix": jnp.clip(0.3 + 0.39999998 * jax.random.uniform(arg_keys[10], (HEADS,), jnp.float32) ** block_levels(arg_keys[10], (HEADS,), ((0, 4),), -0.2, 0.2), 0.3, 0.7),
    }


EPSILON = 1e-06
SCORE_SCALE = 0.125
MASKED = -1e+30
FULL_PRECISION = lax.Precision.HIGHEST

@jax.custom_vjp
def low(v):
    return lax.optimization_barrier(v.astype(jnp.bfloat16)).astype(jnp.float32)

@jax.custom_vjp
def reduced_backward(v):
    return v

def low_keep(v):
    return (low(v), None)

def low_pass(kept, grad):
    return (grad,)

def back_keep(v):
    return (v, None)

def back_low(kept, grad):
    return (low(grad),)
low.defvjp(low_keep, low_pass)
reduced_backward.defvjp(back_keep, back_low)

def norm_rows(values, gain_vec):
    return values * lax.rsqrt(lax.optimization_barrier(jnp.mean(values * values, axis=-1, keepdims=True)) + EPSILON) * gain_vec

def angle_tables(count):
    half_size = HEAD // 2
    positions = jnp.arange(count).astype(jnp.float32)
    frequency = 10000.0 ** (-jnp.arange(half_size).astype(jnp.float32) / half_size)
    table = positions[:, None] * frequency[None, :]
    return (jnp.cos(table)[None, :, None, :], jnp.sin(table)[None, :, None, :])

def rotate(values, cosine, sine_table):
    half_size = values.shape[-1] // 2
    first_half, second_half = (values[..., :half_size], values[..., half_size:])
    return jnp.concatenate([first_half * cosine - second_half * sine_table, second_half * cosine + first_half * sine_table], axis=-1)

def attend_one(operands):
    query_seq, key_seq, value_seq = operands
    scores = reduced_backward(jnp.einsum('qhc,khc->hqk', query_seq, key_seq, precision=FULL_PRECISION) * SCORE_SCALE)
    block_ids = jnp.arange(SEQ_LEN) // BLOCK
    visible = block_ids[None, :] <= block_ids[:, None]
    scores = jnp.where(visible[None], scores, MASKED)
    attn_probs = jax.nn.softmax(scores, axis=-1)
    return jnp.einsum('hqk,khc->qhc', low(attn_probs), value_seq, precision=FULL_PRECISION)

def layer(tokens, first_values, w_qkv, output_weight, w_gate, w_up, w_down, gain_attn, gain_mlp, mix):
    group_size = tokens.shape[0]
    shape_heads = (group_size, SEQ_LEN, HEADS, HEAD)
    normed = low(norm_rows(tokens, gain_attn))
    projected = jnp.einsum('gld,dkc->glkc', normed, w_qkv, precision=FULL_PRECISION)
    query_raw = reduced_backward(projected[:, :, 0]).reshape(shape_heads)
    key_raw = reduced_backward(projected[:, :, 1]).reshape(shape_heads)
    value_raw = reduced_backward(projected[:, :, 2]).reshape(shape_heads)
    cosine, sine_table = angle_tables(SEQ_LEN)
    queries = low(rotate(query_raw, cosine, sine_table))
    key_rows = low(rotate(key_raw, cosine, sine_table))
    mixture_portion = mix[None, None, :, None]
    value_rows = low(mixture_portion * value_raw + (1.0 - mixture_portion) * first_values.reshape(shape_heads))
    attention_result = lax.map(jax.checkpoint(attend_one), (queries, key_rows, value_rows))
    attention_result = low(reduced_backward(attention_result)).reshape(group_size, SEQ_LEN, D)
    branch_output = reduced_backward(jnp.einsum('sbm,mj->sbj', attention_result, output_weight, precision=FULL_PRECISION))
    residual = tokens + branch_output
    normed_mlp = low(norm_rows(residual, gain_mlp))
    gate_proj = reduced_backward(jnp.einsum('gld,df->glf', normed_mlp, w_gate, precision=FULL_PRECISION))
    up_proj = reduced_backward(jnp.einsum('gld,df->glf', normed_mlp, w_up, precision=FULL_PRECISION))
    hidden = low(jax.nn.silu(gate_proj) * up_proj)
    return residual + jnp.einsum('glf,fd->gld', hidden, w_down, precision=FULL_PRECISION)

def reference(tokens, first_values, out_grad, w_qkv, output_weight, w_gate, w_up, w_down, gain_attn, gain_mlp, mix):
    params = tuple((item.astype(jnp.float32) for item in (w_qkv, output_weight, w_gate, w_up, w_down, gain_attn, gain_mlp))) + (mix,)

    def step(running_totals, index):
        begin = index * SEQ_DEV
        piece_x = lax.dynamic_slice_in_dim(tokens, begin, SEQ_DEV, 0).astype(jnp.float32)
        piece_v = lax.dynamic_slice_in_dim(first_values, begin, SEQ_DEV, 0).astype(jnp.float32)
        piece_g = lax.dynamic_slice_in_dim(out_grad, begin, SEQ_DEV, 0).astype(jnp.float32)
        result, pull = jax.vjp(layer, piece_x, piece_v, *params)
        grads = pull(piece_g)
        running_totals = tuple((left_sum + right_sum for left_sum, right_sum in zip(running_totals, grads[2:])))
        return (running_totals, (result.astype(jnp.bfloat16), grads[0], grads[1]))
    zeros = tuple((jnp.zeros_like(item) for item in params))
    running_totals, stacked = lax.scan(step, zeros, jnp.arange(SEQS // SEQ_DEV, dtype=jnp.int32))
    outputs, grad_inputs, grad_firsts = stacked
    return (outputs.reshape(SEQS, SEQ_LEN, D), grad_inputs.reshape(SEQS, SEQ_LEN, D), grad_firsts.reshape(SEQS, SEQ_LEN, D), running_totals[0], running_totals[1], running_totals[2], running_totals[3], running_totals[4], running_totals[5], running_totals[6], running_totals[7])
```

```python
import functools

import jax
import jax.numpy as jnp
from jax import lax
from jax.experimental import pallas as pl
from jax.experimental.pallas import tpu as pltpu
from jax.sharding import PartitionSpec as P

EPSILON = 1e-06
SCALE = 0.125
BF = jnp.bfloat16
F32 = jnp.float32
NN = (((1,), (0,)), ((), ()))
NT = (((1,), (1,)), ((), ()))
TN = (((0,), (0,)), ((), ()))


def dot(a, b, dims=NN):
    return lax.dot_general(a, b, dims, preferred_element_type=F32)


def full(shape):
    return pl.BlockSpec(shape, lambda *_: (0,) * len(shape))


def call(kernel, out_shapes, *args, grid=None, in_specs=None, out_specs=None, scratch=(), flops=0, name=None):
    moved = sum(a.size * a.dtype.itemsize for a in args)
    moved += sum(o.size * o.dtype.itemsize for o in out_shapes)
    keywords = {}
    if grid is not None:
        keywords = dict(grid=grid, in_specs=in_specs, out_specs=out_specs)
    elif in_specs is not None:
        keywords = dict(in_specs=in_specs)
    return pl.pallas_call(
        kernel,
        out_shape=out_shapes,
        scratch_shapes=list(scratch),
        cost_estimate=pl.CostEstimate(flops=flops, bytes_accessed=moved, transcendentals=0),
        compiler_params=pltpu.CompilerParams(vmem_limit_bytes=60 << 20),
        name=name,
        **keywords,
    )(*args)


def shape_of(dims, dtype):
    return jax.ShapeDtypeStruct(dims, dtype)


def half_swap(values, lane):
    width = values.shape[-1]
    ahead = pltpu.roll(values, width - 32, 1)
    behind = pltpu.roll(values, 32, 1)
    return jnp.where(lane % 64 < 32, ahead, behind)


def signed_tables(cos_ref, sin_ref, index, width, lane):
    cosine = jnp.concatenate([cos_ref[index]] * (width // 128), axis=1)
    sine = jnp.concatenate([sin_ref[index]] * (width // 128), axis=1)
    return cosine, jnp.where(lane % 64 < 32, -sine, sine)


def qkv_kernel(seg, p0, p1, p2, p3, gain, wa, wb, fv, cos, sin, mix, normed_o, q_o, k_o, v_o, diff_o):
    x = jnp.concatenate([p0[0], p1[0], p2[0], p3[0]], axis=0).astype(F32)
    half = wa.shape[1]
    inverse = lax.rsqrt(jnp.mean(x * x, axis=-1, keepdims=True) + EPSILON)
    normed = (x * inverse * gain[...]).astype(BF)
    normed_o[0] = normed
    width = wa.shape[2]
    lane = lax.broadcasted_iota(jnp.int32, (1, width), 1)
    cosine, sine = signed_tables(cos, sin, 0, width, lane)
    na, nb = normed[:, :half], normed[:, half:]
    raw = [dot(na, wa[i]) + dot(nb, wb[i]) for i in range(3)]
    q_o[0] = (raw[0] * cosine + half_swap(raw[0], lane) * sine).astype(BF)
    k_o[0] = (raw[1] * cosine + half_swap(raw[1], lane) * sine).astype(BF)
    first = jnp.concatenate([fv[0, seg[r]] for r in range(4)], axis=0).astype(F32)
    v_o[0] = (mix[...] * raw[2] + (1.0 - mix[...]) * first).astype(BF)
    diff_o[0] = (raw[2] - first).astype(BF)


def attend_kernel(q, k, v, woa, wob, att_o, lse_o, keep_o, send_o, v_t, o_t):
    blocks, rows, width = q.shape
    heads = width // 64
    for b in range(blocks):
        v_t[:, b * rows:(b + 1) * rows] = v[b].astype(F32).T.astype(BF)
    lane = lax.broadcasted_iota(jnp.int32, (1, width), 1) // 64

    def head(h, carry):
        own = lane == h
        for qb in range(blocks):
            qm = jnp.where(own, q[qb], jnp.zeros_like(q[qb]))
            scores = [dot(k[kb], qm, NT) * SCALE for kb in range(qb + 1)]
            top = functools.reduce(jnp.maximum, [jnp.max(s, axis=0, keepdims=True) for s in scores])
            total = jnp.zeros((1, rows), F32)
            out = jnp.zeros((64, rows), F32)
            for kb in range(qb + 1):
                e = jnp.exp(scores[kb] - top)
                total = total + jnp.sum(e, axis=0, keepdims=True)
                out = out + dot(v_t[pl.ds(pl.multiple_of(h * 64, 64), 64), kb * rows:(kb + 1) * rows], e.astype(BF))
            o_t[qb, pl.ds(pl.multiple_of(h * 64, 64), 64), :] = out / total
            lse_o[h, qb:qb + 1, :] = top + jnp.log(total)
        return carry

    lax.fori_loop(0, heads, head, 0)
    half = woa.shape[1]
    quarter = rows // 4
    for qb in range(blocks):
        att = o_t[qb].T.astype(BF)
        att_o[qb] = att
        for lo, w in ((0, woa), (half, wob)):
            part = dot(att, w[...])
            for p in range(2):
                keep_o[p, qb, :, lo:lo + half] = part[p * quarter:(p + 1) * quarter]
                send_o[p, qb, :, lo:lo + half] = part[(2 + p) * quarter:(3 + p) * quarter].astype(BF)


def residual_kernel(x, keep, got_core, got_x, gain, residual_o, normed_o):
    residual = (
        x[0].astype(F32) + keep[0, 0] + got_core[0, 0].astype(F32) + got_x[0].astype(F32)
    )
    inverse = lax.rsqrt(jnp.mean(residual * residual, axis=-1, keepdims=True) + EPSILON)
    residual_o[0] = residual
    normed_o[0] = (residual * inverse * gain[...]).astype(BF)


def mlp_kernel(
    n0, n1, n2, n3, g0, g1, g2, g3, ga, gb, ua, ub, da, db,
    normed_o, grad_o, hidden_o, dgate_o, dup_o, keep_o, send_o,
):
    n = jnp.concatenate([n0[0], n1[0], n2[0], n3[0]], axis=0)
    g = jnp.concatenate([g0[0], g1[0], g2[0], g3[0]], axis=0)
    normed_o[0] = n
    grad_o[0] = g
    half = ga.shape[1]
    na, nb = n[:, :half], n[:, half:]
    gate = dot(na, ga[...], NT) + dot(nb, gb[...], NT)
    up = dot(na, ua[...], NT) + dot(nb, ub[...], NT)
    grad_hidden = dot(g[:, :half], da[...], NT) + dot(g[:, half:], db[...], NT)
    s = jax.nn.sigmoid(gate)
    active = gate * s
    hidden_o[0] = (active * up).astype(BF)
    dgate = (grad_hidden * up * s * (1.0 + gate * (1.0 - s))).astype(BF)
    dup = (grad_hidden * active).astype(BF)
    dgate_o[0] = dgate
    dup_o[0] = dup
    quarter = n.shape[0] // 4
    for lo, wg, wu in ((0, ga, ua), (half, gb, ub)):
        part = dot(dgate, wg[...]) + dot(dup, wu[...])
        for p in range(2):
            keep_o[p, 0, :, lo:lo + half] = part[p * quarter:(p + 1) * quarter]
            send_o[p, 0, :, lo:lo + half] = part[(2 + p) * quarter:(3 + p) * quarter].astype(BF)


def down_kernel(hidden, da, db, keep_o, send_o):
    half = da.shape[1]
    quarter = hidden.shape[1] // 4
    for lo, w in ((0, da), (half, db)):
        part = dot(hidden[0], w[...])
        for p in range(2):
            keep_o[p, 0, :, lo:lo + half] = part[p * quarter:(p + 1) * quarter]
            send_o[p, 0, :, lo:lo + half] = part[(2 + p) * quarter:(3 + p) * quarter].astype(BF)


def norm_back_kernel(direct, keep, got_core, got_x, values, gain, grad_o, low_o, gain_o):
    @pl.when(pl.program_id(0) == 0)
    def _():
        gain_o[...] = jnp.zeros_like(gain_o)

    grad = keep[0, 0] + got_core[0, 0].astype(F32) + got_x[0].astype(F32)
    x = values[0].astype(F32)
    inverse = lax.rsqrt(jnp.mean(x * x, axis=-1, keepdims=True) + EPSILON)
    weighted = grad * gain[...]
    gain_o[...] += jnp.sum(grad * x * inverse, axis=0, keepdims=True)
    out = direct[0].astype(F32) + (
        inverse * weighted
        - x * (inverse * inverse * inverse) * jnp.mean(weighted * x, axis=-1, keepdims=True)
    )
    grad_o[0] = out
    low_o[0] = out.astype(BF)


def attend_back_kernel(
    seg, b0, b1, b2, b3, woa, wob, q, k, v, att, lse, cos, sin, mix, diff,
    gb_o, gq_o, gk_o, gv_o, gf_o, dmix_o,
    gat, dmat, k_t, dk, dv, dq_t,
):
    blocks, rows, width = q.shape
    heads = width // 64
    half = woa.shape[1]
    lane_full = lax.broadcasted_iota(jnp.int32, (1, width), 1)
    lane = lane_full // 64
    pick = (
        lax.broadcasted_iota(jnp.int32, (8, width), 0)
        == lax.broadcasted_iota(jnp.int32, (8, width), 1) // 64
    ).astype(F32)
    for b in range(blocks):
        g = jnp.concatenate([b0[b], b1[b], b2[b], b3[b]], axis=0)
        gb_o[b] = g
        ga = (dot(g[:, :half], woa[...], NT) + dot(g[:, half:], wob[...], NT)).astype(BF)
        gat[b] = ga
        prod = ga.astype(F32) * att[b].astype(F32)
        dmat[b] = lax.dot_general(pick, prod, NT, precision=lax.Precision.HIGHEST, preferred_element_type=F32)
        k_t[:, b * rows:(b + 1) * rows] = k[b].astype(F32).T.astype(BF)
    dk[...] = jnp.zeros_like(dk)
    dv[...] = jnp.zeros_like(dv)

    def head(h, carry):
        own = lane == h
        for qb in range(blocks):
            qm = jnp.where(own, q[qb], jnp.zeros_like(q[qb]))
            gm = jnp.where(own, gat[qb], jnp.zeros_like(gat[qb]))
            log_total = lse[h, qb:qb + 1, :]
            row_dot = dmat[qb, pl.ds(h, 1), :]
            acc = jnp.zeros((64, rows), F32)
            for kb in range(qb + 1):
                prob = jnp.exp(dot(k[kb], qm, NT) * SCALE - log_total)
                dprob = dot(v[kb], gm, NT)
                ds = (prob * (dprob - row_dot)).astype(BF)
                dv[kb] += dot(prob.astype(BF), gm)
                dk[kb] += dot(ds, qm)
                acc = acc + dot(k_t[pl.ds(pl.multiple_of(h * 64, 64), 64), kb * rows:(kb + 1) * rows], ds)
            dq_t[qb, pl.ds(pl.multiple_of(h * 64, 64), 64), :] = acc
        return carry

    lax.fori_loop(0, heads, head, 0)
    quarter = rows // 4
    total = jnp.zeros((1, width), F32)
    for b in range(blocks):
        cosine, sine = signed_tables(cos, sin, b, width, lane_full)
        gq = dq_t[b].T * SCALE
        gk = dk[b] * SCALE
        gv = dv[b]
        gq_o[b] = (gq * cosine - half_swap(gq, lane_full) * sine).astype(BF)
        gk_o[b] = (gk * cosine - half_swap(gk, lane_full) * sine).astype(BF)
        gv_o[b] = (mix[...] * gv).astype(BF)
        gf = ((1.0 - mix[...]) * gv).astype(BF)
        for r in range(4):
            gf_o[b, seg[r]] = gf[r * quarter:(r + 1) * quarter]
        total = total + jnp.sum(gv * diff[b].astype(F32), axis=0, keepdims=True)
    dmix_o[...] = total


def grad_normed_kernel(gq, gk, gv, wa, wb, keep_o, send_o):
    half = wa.shape[1]
    quarter = gq.shape[1] // 4
    for lo, w in ((0, wa), (half, wb)):
        part = dot(gq[0], w[0], NT) + dot(gk[0], w[1], NT) + dot(gv[0], w[2], NT)
        for p in range(2):
            keep_o[p, 0, :, lo:lo + half] = part[p * quarter:(p + 1) * quarter]
            send_o[p, 0, :, lo:lo + half] = part[(2 + p) * quarter:(3 + p) * quarter].astype(BF)


def place_kernel(where, roll, *refs):
    pieces, out = refs[:-1], refs[-1]
    width = out.shape[-1]
    half = width // 2
    for r, piece in enumerate(pieces):
        value = piece[0]
        low, high = value[:, :half], value[:, half:]
        swap = roll[0] == 1
        out[0, where[r], :, :half] = jnp.where(swap, high, low).astype(out.dtype)
        out[0, where[r], :, half:] = jnp.where(swap, low, high).astype(out.dtype)


def first_kernel(got, out):
    out[...] = got[...].astype(out.dtype)


def on_device(
    fsdp, ctx, tp,
    tokens, first_values, out_grad, w_qkv, output_weight, w_gate, w_up, w_down, gain_attn, gain_mlp, mix,
):
    seqs, block, width = tokens.shape
    local = w_qkv.shape[2]
    hidden_width = w_gate.shape[1]
    quarter = block // tp
    half = width // 2
    pair = fsdp == 2
    assert seqs == ctx and ctx == 4 and tp == 4
    y = lax.axis_index("fsdp")
    z = lax.axis_index("ctx")
    t = lax.axis_index("tp")
    swap_y = [(0, 1), (1, 0)]
    by_core = [(i, i ^ 1) for i in range(tp)]
    by_x = [(i, i ^ 2) for i in range(tp)]

    def core(value):
        return lax.ppermute(value, "tp", by_core)

    def across(value):
        return lax.ppermute(value, "tp", by_x)

    def other_half(value, axis):
        if pair:
            return value, lax.ppermute(value, "fsdp", swap_y)
        whole = lax.all_gather(value, "fsdp", axis=axis, tiled=True)
        return tuple(lax.slice_in_dim(whole, i * half, (i + 1) * half, axis=axis) for i in range(2))

    def gather(own):
        second = across(own)
        return own, second, core(own), core(second)

    def own_rows(value):
        part = lax.dynamic_slice_in_dim(value, t * quarter, quarter, axis=1)
        if pair:
            part = jnp.where(y == 1, jnp.roll(part, half, axis=-1), part)
        return lax.all_to_all(part, "ctx", 0, 0)

    x_own = own_rows(tokens)
    x_pieces = gather(x_own)
    qkv_own = jnp.transpose(w_qkv, (1, 0, 2))
    qkv_a, qkv_b = other_half(qkv_own, 1)
    gains = other_half(jnp.stack([gain_attn, gain_mlp]), 1)
    gains = jnp.concatenate(gains, axis=1).astype(F32)
    gain_first, gain_second = gains[0:1], gains[1:2]
    fv = lax.all_to_all(first_values, "ctx", 0, 0).reshape(ctx, tp, quarter, local)
    out_a, out_b = other_half(output_weight, 1)
    g_own = own_rows(out_grad)
    g_pieces = gather(g_own)
    gate_a, gate_b = other_half(w_gate.T, 1)
    up_a, up_b = other_half(w_up.T, 1)
    down_a, down_b = other_half(w_down, 1)

    seg = jnp.stack([t, t ^ 2, t ^ 1, t ^ 3]).astype(jnp.int32)
    roll = jnp.reshape(y if pair else y * 0, (1,)).astype(jnp.int32)
    place = (seg[:, None] * quarter + jnp.arange(quarter)[None, :]).reshape(block)
    positions = (jnp.arange(ctx)[:, None] * block + place[None, :]).astype(F32)
    lanes = (jnp.arange(128) % 32).astype(F32)
    table = positions[:, :, None] * (10000.0 ** (-lanes / 32.0))[None, None, :]
    cosine, sine = jnp.cos(table), jnp.sin(table)
    mix_row = jnp.repeat(mix, local // mix.shape[0])[None, :]

    rows = ctx * block
    smem = pl.BlockSpec(memory_space=pltpu.SMEM)
    piece_spec = pl.BlockSpec((1, quarter, width), lambda b: (b, 0, 0))
    block_local = pl.BlockSpec((1, block, local), lambda b: (b, 0, 0))
    block_width = pl.BlockSpec((1, block, width), lambda b: (b, 0, 0))
    block_hidden = pl.BlockSpec((1, block, hidden_width), lambda b: (b, 0, 0))
    block_table = pl.BlockSpec((1, block, 128), lambda b: (b, 0, 0))
    part_spec = pl.BlockSpec((2, 1, quarter, width), lambda b: (0, b, 0, 0))
    first_part = pl.BlockSpec((1, 1, quarter, width), lambda b: (0, b, 0, 0))
    keep_shape = shape_of((2, ctx, quarter, width), F32)
    send_shape = shape_of((2, ctx, quarter, width), BF)
    own_f32 = shape_of((ctx, quarter, width), F32)
    own_low = shape_of((ctx, quarter, width), BF)
    rows_local = shape_of((ctx, block, local), BF)
    rows_width = shape_of((ctx, block, width), BF)
    rows_hidden = shape_of((ctx, block, hidden_width), BF)
    gain_spec = full((1, width))

    normed, queries, keys, values, diff = call(
        qkv_kernel,
        [rows_width, rows_local, rows_local, rows_local, rows_local],
        seg, *x_pieces, gain_first, qkv_a, qkv_b, fv, cosine, sine, mix_row,
        grid=(ctx,),
        in_specs=[smem] + [piece_spec] * 4 + [
            gain_spec, full((3, half, local)), full((3, half, local)),
            pl.BlockSpec((1, tp, quarter, local), lambda b: (b, 0, 0, 0)),
            block_table, block_table, full((1, local)),
        ],
        out_specs=[block_width] + [block_local] * 4,
        flops=2 * rows * width * 3 * local,
        name="norm_qkv",
    )
    attended, log_total, keep, send = call(
        attend_kernel,
        [rows_local, shape_of((mix.shape[0], ctx, block), F32), keep_shape, send_shape],
        queries, keys, values, out_a, out_b,
        scratch=[pltpu.VMEM((local, rows), BF), pltpu.VMEM((ctx, local, block), F32)],
        flops=6 * rows * rows * local,
        name="attend",
    )

    def reduce_rows(keep, send):
        got_core = core(send)
        onward = (keep[1] + got_core[1].astype(F32)).astype(BF)
        return got_core, across(onward)

    got_core, got_x = reduce_rows(keep, send)
    residual, normed_own = call(
        residual_kernel,
        [own_f32, own_low],
        x_own, keep, got_core, got_x, gain_second,
        grid=(ctx,),
        in_specs=[piece_spec, first_part, first_part, piece_spec, gain_spec],
        out_specs=[piece_spec, piece_spec],
        name="residual_norm",
    )
    n_pieces = gather(normed_own)
    normed_mlp, grad_rows, hidden, grad_gate, grad_up, keep, send = call(
        mlp_kernel,
        [rows_width, rows_width, rows_hidden, rows_hidden, rows_hidden, keep_shape, send_shape],
        *n_pieces, *g_pieces, gate_a, gate_b, up_a, up_b, down_a, down_b,
        grid=(ctx,),
        in_specs=[piece_spec] * 8 + [full((hidden_width, half))] * 6,
        out_specs=[block_width] * 2 + [block_hidden] * 3 + [part_spec] * 2,
        flops=10 * rows * width * hidden_width,
        name="mlp",
    )
    got_core, got_x = reduce_rows(keep, send)
    grad_residual, branch_own, gain_sum_second = call(
        norm_back_kernel,
        [own_f32, own_low, shape_of((1, width), F32)],
        g_own, keep, got_core, got_x, residual, gain_second,
        grid=(ctx,),
        in_specs=[piece_spec, first_part, first_part, piece_spec, piece_spec, gain_spec],
        out_specs=[piece_spec, piece_spec, gain_spec],
        name="norm_back_mlp",
    )
    b_pieces = gather(branch_own)

    down_keep, down_send = call(
        down_kernel,
        [keep_shape, send_shape],
        hidden, down_a, down_b,
        grid=(ctx,),
        in_specs=[block_hidden, full((hidden_width, half)), full((hidden_width, half))],
        out_specs=[part_spec, part_spec],
        flops=2 * rows * width * hidden_width,
        name="down",
    )

    def weight_grad(left, right):
        return lax.dot_general(
            left.reshape(rows, -1), right.reshape(rows, -1), TN, preferred_element_type=F32
        )

    def owned(grad, axis):
        first, second = (lax.slice_in_dim(grad, i * half, (i + 1) * half, axis=axis) for i in range(2))
        if pair:
            shard = first + lax.ppermute(second.astype(BF), "fsdp", swap_y).astype(F32)
        else:
            shard = lax.psum_scatter(
                grad.astype(BF), "fsdp", scatter_dimension=axis, tiled=True
            ).astype(F32)
        toward = lax.ppermute(shard.astype(BF), "ctx", [(0, 1), (3, 2)])
        shard = (shard + toward.astype(F32)).astype(BF)
        meet = lax.ppermute(shard, "ctx", [(1, 2), (2, 1)])
        shard = (shard.astype(F32) + meet.astype(F32)).astype(BF)
        back = lax.ppermute(shard, "ctx", [(1, 0), (2, 3)])
        return jnp.where((z == 0) | (z == 3), back, shard).astype(F32)

    grad_w_down = owned(weight_grad(hidden, grad_rows), 1)
    grad_w_gate = owned(weight_grad(grad_gate, normed_mlp), 1).T
    grad_w_up = owned(weight_grad(grad_up, normed_mlp), 1).T

    branch_rows, gq, gk, gv, gf, mix_sum = call(
        attend_back_kernel,
        [
            rows_width, rows_local, rows_local, rows_local,
            shape_of((ctx, tp, quarter, local), BF), shape_of((1, local), F32),
        ],
        seg, *b_pieces, out_a, out_b, queries, keys, values, attended, log_total, cosine, sine, mix_row, diff,
        in_specs=[smem] + [pl.BlockSpec(memory_space=pltpu.VMEM)] * 15,
        scratch=[
            pltpu.VMEM((ctx, block, local), BF),
            pltpu.VMEM((ctx, 8, block), F32),
            pltpu.VMEM((local, rows), BF),
            pltpu.VMEM((ctx, block, local), F32),
            pltpu.VMEM((ctx, block, local), F32),
            pltpu.VMEM((ctx, local, block), F32),
        ],
        flops=14 * rows * rows * local,
        name="attend_back",
    )
    keep, send = call(
        grad_normed_kernel,
        [keep_shape, send_shape],
        gq, gk, gv, qkv_a, qkv_b,
        grid=(ctx,),
        in_specs=[block_local] * 3 + [full((3, half, local))] * 2,
        out_specs=[part_spec, part_spec],
        flops=6 * rows * width * local,
        name="grad_normed",
    )
    got_core, got_x = reduce_rows(keep, send)
    grad_w_qkv = owned(
        jnp.stack([weight_grad(normed, item) for item in (gq, gk, gv)]), 1
    )
    grad_w_qkv = jnp.transpose(grad_w_qkv, (1, 0, 2))
    grad_w_out = owned(weight_grad(attended, branch_rows), 1)

    _, tokens_own, gain_sum_first = call(
        norm_back_kernel,
        [own_f32, own_low, shape_of((1, width), F32)],
        grad_residual, keep, got_core, got_x, x_own, gain_first,
        grid=(ctx,),
        in_specs=[piece_spec, first_part, first_part, piece_spec, piece_spec, gain_spec],
        out_specs=[piece_spec, piece_spec, gain_spec],
        name="norm_back_attn",
    )

    got_core, got_x = reduce_rows(down_keep, down_send)
    output_own = (
        residual + down_keep[0] + got_core[0].astype(F32) + got_x.astype(F32)
    ).astype(BF)

    def home(own, dtype):
        pieces = gather(lax.all_to_all(own, "ctx", 0, 0))
        placed = call(
            place_kernel,
            [shape_of((seqs, tp, quarter, width), dtype)],
            seg, roll, *pieces,
            grid=(seqs,),
            in_specs=[smem, smem] + [piece_spec] * 4,
            out_specs=[pl.BlockSpec((1, tp, quarter, width), lambda b: (b, 0, 0, 0))],
            name="place",
        )[0]
        return placed.reshape(seqs, block, width)

    output = home(output_own, BF)
    grad_tokens = home(tokens_own, F32)
    grad_first = lax.all_to_all(gf, "ctx", 0, 0).reshape(seqs, block, local).astype(F32)

    small = jnp.concatenate([gain_sum_first, gain_sum_second, mix_sum], axis=1)
    for step in (1, 2):
        small = small + lax.ppermute(small, "ctx", [(i, i ^ step) for i in range(ctx)])
    mixed = small[:, 2 * width:]
    first_gain, second_gain = small[:, :width], small[:, width:2 * width]
    if pair:
        outgoing = jnp.concatenate([first_gain[:, half:], second_gain[:, half:], mixed], axis=1)
        incoming = lax.ppermute(outgoing, "fsdp", swap_y)
        gains_here = jnp.concatenate([first_gain[:, :half], second_gain[:, :half]], axis=1)
        gains_here = gains_here + incoming[:, :2 * half]
        mixed = mixed + incoming[:, 2 * half:]
    else:
        mixed = lax.psum(mixed, "fsdp")
        gains_here = jnp.concatenate(
            [
                lax.psum_scatter(item, "fsdp", scatter_dimension=1, tiled=True)
                for item in (first_gain, second_gain)
            ],
            axis=1,
        )
    for perm in (by_core, by_x):
        gains_here = gains_here + lax.ppermute(gains_here, "tp", perm)
    share = gain_attn.shape[0]
    grad_mix = jnp.sum(mixed.reshape(mix.shape[0], -1), axis=1)
    return (
        output, grad_tokens, grad_first, grad_w_qkv, grad_w_out, grad_w_gate, grad_w_up, grad_w_down,
        gains_here[0, :share], gains_here[0, share:], grad_mix,
    )


def solution(mesh):
    rows = P("fsdp", "ctx", None)
    in_specs = (
        rows, P("fsdp", "ctx", "tp"), rows, P("fsdp", None, "tp"), P("tp", "fsdp"), P("fsdp", "tp"),
        P("fsdp", "tp"), P("tp", "fsdp"), P("fsdp"), P("fsdp"), P("tp"),
    )
    out_specs = (
        rows, rows, P("fsdp", "ctx", "tp"), P("fsdp", None, "tp"), P("tp", "fsdp"), P("fsdp", "tp"),
        P("fsdp", "tp"), P("tp", "fsdp"), P("fsdp"), P("fsdp"), P("tp"),
    )
    sizes = [mesh.shape[name] for name in ("fsdp", "ctx", "tp")]
    return jax.shard_map(
        functools.partial(on_device, *sizes), mesh=mesh, in_specs=in_specs, out_specs=out_specs,
        check_vma=False,
    )
```

```python
import functools

import jax
import jax.numpy as jnp
from jax import lax
from jax.experimental import pallas as pl
from jax.experimental.pallas import tpu as pltpu
from jax.sharding import PartitionSpec as P

EPSILON = 1e-06
SCALE = 0.125
BF = jnp.bfloat16
F32 = jnp.float32
NN = (((1,), (0,)), ((), ()))
NT = (((1,), (1,)), ((), ()))
TN = (((0,), (0,)), ((), ()))


def dot(a, b, dims=NN):
    return lax.dot_general(a, b, dims, preferred_element_type=F32)


def full(shape):
    return pl.BlockSpec(shape, lambda *_: (0,) * len(shape))


def call(kernel, out_shapes, *args, grid=None, in_specs=None, out_specs=None, scratch=(), us=0, name=None, vmem=16):
    moved = sum(a.size * a.dtype.itemsize for a in args)
    moved += sum(o.size * o.dtype.itemsize for o in out_shapes)
    keywords = {}
    if grid is not None:
        keywords = dict(grid=grid, in_specs=in_specs, out_specs=out_specs)
    elif in_specs is not None:
        keywords = dict(in_specs=in_specs)
    return pl.pallas_call(
        kernel,
        out_shape=out_shapes,
        scratch_shapes=list(scratch),
        cost_estimate=pl.CostEstimate(flops=0, bytes_accessed=int(us * 3.4e6), transcendentals=0),
        compiler_params=pltpu.CompilerParams(vmem_limit_bytes=vmem << 20),
        name=name,
        **keywords,
    )(*args)


def shape_of(dims, dtype):
    return jax.ShapeDtypeStruct(dims, dtype)


def own_kernel(place, tokens, grads, x_o, g_o, sems):
    half = x_o.shape[2] // 2
    copies = []
    for h in range(2):
        start = pl.multiple_of(place[2 + h] * half, half)
        lanes = slice(h * half, (h + 1) * half)
        pairs = [
            (tokens.at[:, place[0], :, pl.ds(start, half)], x_o.at[:, :, lanes]),
            (grads.at[:, place[0], :, pl.ds(start, half)], g_o.at[:, 0, :, lanes]),
            (grads.at[:, place[1], :, pl.ds(start, half)], g_o.at[:, 1, :, lanes]),
        ]
        for source, out in pairs:
            copies.append(pltpu.make_async_copy(source, out, sems.at[len(copies)]))
    for copy in copies:
        copy.start()
    for copy in copies:
        copy.wait()


def half_swap(values, lane):
    width = values.shape[-1]
    ahead = pltpu.roll(values, width - 32, 1)
    behind = pltpu.roll(values, 32, 1)
    return jnp.where(lane % 64 < 32, ahead, behind)


def signed_tables(cos_ref, sin_ref, index, width, lane):
    cosine = jnp.concatenate([cos_ref[index]] * (width // 128), axis=1)
    sine = jnp.concatenate([sin_ref[index]] * (width // 128), axis=1)
    return cosine, jnp.where(lane % 64 < 32, -sine, sine)


def qkv_kernel(p0, p1, p2, p3, gain, wa, wb, cos, sin, na_o, nb_o, q_o, k_o, v_o):
    x = jnp.concatenate([p0[0], p1[0], p2[0], p3[0]], axis=0).astype(F32)
    half = wa.shape[1]
    inverse = lax.rsqrt(jnp.mean(x * x, axis=-1, keepdims=True) + EPSILON)
    normed = (x * inverse * gain[...]).astype(BF)
    width = wa.shape[2]
    lane = lax.broadcasted_iota(jnp.int32, (1, width), 1)
    cosine, sine = signed_tables(cos, sin, 0, width, lane)
    na, nb = normed[:, :half], normed[:, half:]
    na_o[0] = na
    nb_o[0] = nb
    raw = [dot(na, wa[i]) + dot(nb, wb[i]) for i in range(3)]
    q_o[0] = (raw[0] * cosine + half_swap(raw[0], lane) * sine).astype(BF)
    k_o[0] = (raw[1] * cosine + half_swap(raw[1], lane) * sine).astype(BF)
    v_o[0] = raw[2]


def attend_kernel(seg, q, k, raw, fv, mix, woa, wob, v_o, att_o, lse_o, keep_o, send_o, v_t, o_t):
    blocks, rows, width = q.shape
    heads = width // 64
    for b in range(blocks):
        first = jnp.concatenate([fv[b, seg[r]] for r in range(4)], axis=0).astype(F32)
        value = mix[...] * raw[b] + (1.0 - mix[...]) * first
        v_o[b] = value.astype(BF)
        v_t[:, b * rows:(b + 1) * rows] = value.T.astype(BF)
    lane = lax.broadcasted_iota(jnp.int32, (1, width), 1) // 64

    def head(h, carry):
        own = lane == h
        for qb in range(blocks):
            qm = jnp.where(own, q[qb], jnp.zeros_like(q[qb]))
            scores = [dot(k[kb], qm, NT) * SCALE for kb in range(qb + 1)]
            top = functools.reduce(jnp.maximum, [jnp.max(s, axis=0, keepdims=True) for s in scores])
            total = jnp.zeros((1, rows), F32)
            out = jnp.zeros((64, rows), F32)
            for kb in range(qb + 1):
                e = jnp.exp(scores[kb] - top)
                total = total + jnp.sum(e, axis=0, keepdims=True)
                out = out + dot(v_t[pl.ds(pl.multiple_of(h * 64, 64), 64), kb * rows:(kb + 1) * rows], e.astype(BF))
            o_t[qb, pl.ds(pl.multiple_of(h * 64, 64), 64), :] = out / total
            lse_o[h, qb:qb + 1, :] = top + jnp.log(total)
        return carry

    lax.fori_loop(0, heads, head, 0)
    half = woa.shape[1]
    quarter = rows // 4
    for qb in range(blocks):
        att = o_t[qb].T.astype(BF)
        att_o[qb] = att
        for lo, w in ((0, woa), (half, wob)):
            part = dot(att, w[...])
            for p in range(2):
                keep_o[p, qb, :, lo:lo + half] = part[p * quarter:(p + 1) * quarter]
                send_o[p, qb, :, lo:lo + half] = part[(2 + p) * quarter:(3 + p) * quarter].astype(BF)


def residual_kernel(x, keep, got_core, got_x, gain, residual_o, normed_o):
    residual = (
        x[0].astype(F32) + keep[0, 0] + got_core[0, 0].astype(F32) + got_x[0].astype(F32)
    )
    inverse = lax.rsqrt(jnp.mean(residual * residual, axis=-1, keepdims=True) + EPSILON)
    residual_o[0] = residual
    normed_o[0] = (residual * inverse * gain[...]).astype(BF)


def mlp_kernel(
    n0, n1, n2, n3, g0, g1, ga, gb, ua, ub, da, db,
    na_o, nb_o, la_o, lb_o, hidden_o, dgate_o, dup_o, keep_o, send_o,
):
    n = jnp.concatenate([n0[0], n1[0], n2[0], n3[0]], axis=0)
    g = jnp.concatenate([g0[0, 0], g0[0, 1], g1[0, 0], g1[0, 1]], axis=0)
    half = ga.shape[1]
    na, nb = n[:, :half], n[:, half:]
    na_o[0] = na
    nb_o[0] = nb
    la_o[0] = g[:, :half]
    lb_o[0] = g[:, half:]
    gate = dot(na, ga[...], NT) + dot(nb, gb[...], NT)
    up = dot(na, ua[...], NT) + dot(nb, ub[...], NT)
    grad_hidden = dot(g[:, :half], da[...], NT) + dot(g[:, half:], db[...], NT)
    s = jax.nn.sigmoid(gate)
    active = gate * s
    hidden_o[0] = (active * up).astype(BF)
    dgate = (grad_hidden * up * s * (1.0 + gate * (1.0 - s))).astype(BF)
    dup = (grad_hidden * active).astype(BF)
    dgate_o[0] = dgate
    dup_o[0] = dup
    quarter = n.shape[0] // 4
    for lo, wg, wu in ((0, ga, ua), (half, gb, ub)):
        part = dot(dgate, wg[...]) + dot(dup, wu[...])
        for p in range(2):
            keep_o[p, 0, :, lo:lo + half] = part[p * quarter:(p + 1) * quarter]
            send_o[p, 0, :, lo:lo + half] = part[(2 + p) * quarter:(3 + p) * quarter].astype(BF)


def down_kernel(hidden, da, db, keep_o, send_o):
    half = da.shape[1]
    quarter = hidden.shape[1] // 4
    for lo, w in ((0, da), (half, db)):
        part = dot(hidden[0], w[...])
        for p in range(2):
            keep_o[p, 0, :, lo:lo + half] = part[p * quarter:(p + 1) * quarter]
            send_o[p, 0, :, lo:lo + half] = part[(2 + p) * quarter:(3 + p) * quarter].astype(BF)


def norm_back_kernel(direct, keep, got_core, got_x, values, gain, grad_o, low_o, gain_o):
    @pl.when(pl.program_id(0) == 0)
    def _():
        gain_o[...] = jnp.zeros_like(gain_o)

    grad = keep[0, 0] + got_core[0, 0].astype(F32) + got_x[0].astype(F32)
    x = values[0].astype(F32)
    inverse = lax.rsqrt(jnp.mean(x * x, axis=-1, keepdims=True) + EPSILON)
    weighted = grad * gain[...]
    gain_o[...] += jnp.sum(grad * x * inverse, axis=0, keepdims=True)
    out = direct[0].astype(F32) + (
        inverse * weighted
        - x * (inverse * inverse * inverse) * jnp.mean(weighted * x, axis=-1, keepdims=True)
    )
    grad_o[0] = out
    low_o[0] = out.astype(BF)


def attend_back_kernel(
    seg, b0, b1, b2, b3, woa, wob, q, k, v, att, lse, cos, sin, mix, raw, fv,
    p0, p1, p2, p3, wa, wb, gain_in,
    g_o, gf_o, keep_o, send_o, own_o, other_o,
    gat, dmat, k_t, dk, dv, dq_t, og,
):
    blocks, rows, width = q.shape
    heads = width // 64
    half = woa.shape[1]
    lane_full = lax.broadcasted_iota(jnp.int32, (1, width), 1)
    lane = lane_full // 64
    pick = (
        lax.broadcasted_iota(jnp.int32, (8, width), 0)
        == lax.broadcasted_iota(jnp.int32, (8, width), 1) // 64
    ).astype(F32)
    og[...] = jnp.zeros_like(og)
    for b in range(blocks):
        g = jnp.concatenate([b0[b], b1[b], b2[b], b3[b]], axis=0)
        og[...] += dot(att[b], g, TN)
        ga = (dot(g[:, :half], woa[...], NT) + dot(g[:, half:], wob[...], NT)).astype(BF)
        gat[b] = ga
        prod = ga.astype(F32) * att[b].astype(F32)
        dmat[b] = lax.dot_general(pick, prod, NT, precision=lax.Precision.HIGHEST, preferred_element_type=F32)
        k_t[:, b * rows:(b + 1) * rows] = k[b].astype(F32).T.astype(BF)
    dk[...] = jnp.zeros_like(dk)
    dv[...] = jnp.zeros_like(dv)

    def head(h, carry):
        own = lane == h
        for qb in range(blocks):
            qm = jnp.where(own, q[qb], jnp.zeros_like(q[qb]))
            gm = jnp.where(own, gat[qb], jnp.zeros_like(gat[qb]))
            log_total = lse[h, qb:qb + 1, :]
            row_dot = dmat[qb, pl.ds(h, 1), :]
            acc = jnp.zeros((64, rows), F32)
            for kb in range(qb + 1):
                prob = jnp.exp(dot(k[kb], qm, NT) * SCALE - log_total)
                dprob = dot(v[kb], gm, NT)
                ds = (prob * (dprob - row_dot)).astype(BF)
                dv[kb] += dot(prob.astype(BF), gm)
                dk[kb] += dot(ds, qm)
                acc = acc + dot(k_t[pl.ds(pl.multiple_of(h * 64, 64), 64), kb * rows:(kb + 1) * rows], ds)
            dq_t[qb, pl.ds(pl.multiple_of(h * 64, 64), 64), :] = acc
        return carry

    lax.fori_loop(0, heads, head, 0)
    quarter = rows // 4
    total = jnp.zeros((1, width), F32)
    gains = [jnp.zeros((1, half), F32) for _ in range(2)]
    for b in range(blocks):
        cosine, sine = signed_tables(cos, sin, b, width, lane_full)
        gq = dq_t[b].T * SCALE
        gk = dk[b] * SCALE
        gv = dv[b]
        grads = [
            (gq * cosine - half_swap(gq, lane_full) * sine).astype(BF),
            (gk * cosine - half_swap(gk, lane_full) * sine).astype(BF),
            (mix[...] * gv).astype(BF),
        ]
        for i, grad in enumerate(grads):
            g_o[b, :, i * width:(i + 1) * width] = grad
        x = jnp.concatenate([p0[b], p1[b], p2[b], p3[b]], axis=0).astype(F32)
        x = x * lax.rsqrt(jnp.mean(x * x, axis=-1, keepdims=True) + EPSILON)
        for i, w in enumerate((wa, wb)):
            lanes = slice(i * half, (i + 1) * half)
            part = sum(dot(grad, w[j], NT) for j, grad in enumerate(grads))
            gains[i] = gains[i] + jnp.sum(part * x[:, lanes], axis=0, keepdims=True)
            for p in range(2):
                keep_o[p, b, :, lanes] = part[p * quarter:(p + 1) * quarter]
                send_o[p, b, :, lanes] = part[(2 + p) * quarter:(3 + p) * quarter].astype(BF)
        gf = ((1.0 - mix[...]) * gv).astype(BF)
        for r in range(4):
            gf_o[b, seg[r]] = gf[r * quarter:(r + 1) * quarter]
        first = jnp.concatenate([fv[b, seg[r]] for r in range(4)], axis=0).astype(F32)
        total = total + jnp.sum(gv * (raw[b] - first), axis=0, keepdims=True)
    row = lax.broadcasted_iota(jnp.int32, (16, half), 0)
    mixed = jnp.concatenate([total, jnp.zeros((1, half - width), F32)], axis=1)
    for i, out in enumerate((own_o, other_o)):
        lanes = slice(i * half, (i + 1) * half)
        extra = jnp.where(row == 0, gains[i], jnp.where(row == 1, gain_in[:, lanes], jnp.where(row == 2, mixed, 0.0)))
        out[:width] = og[:, lanes].astype(out.dtype)
        out[width:] = extra.astype(out.dtype)


def place_kernel(where, roll, *refs):
    pieces, out = refs[:-1], refs[-1]
    width = out.shape[-1]
    half = width // 2
    for r, piece in enumerate(pieces):
        value = piece[0]
        low, high = value[:, :half], value[:, half:]
        swap = roll[0] == 1
        out[0, where[r], :, :half] = jnp.where(swap, high, low).astype(out.dtype)
        out[0, where[r], :, half:] = jnp.where(swap, low, high).astype(out.dtype)


def first_kernel(got, out):
    out[...] = got[...].astype(out.dtype)


def on_device(
    fsdp, ctx, tp,
    tokens, first_values, out_grad, w_qkv, output_weight, w_gate, w_up, w_down, gain_attn, gain_mlp, mix,
):
    seqs, block, width = tokens.shape
    local = w_qkv.shape[2]
    hidden_width = w_gate.shape[1]
    quarter = block // tp
    half = width // 2
    pair = fsdp == 2
    assert seqs == ctx and ctx == 4 and tp == 4 and local <= half
    y = lax.axis_index("fsdp")
    z = lax.axis_index("ctx")
    t = lax.axis_index("tp")
    swap_y = [(0, 1), (1, 0)]
    by_core = [(i, i ^ 1) for i in range(tp)]
    by_x = [(i, i ^ 2) for i in range(tp)]

    def tie(*values):
        return lax.optimization_barrier(values)

    def core(value):
        return lax.ppermute(value, "tp", by_core)

    def across(value):
        return lax.ppermute(value, "tp", by_x)

    def other_half(value, axis):
        if pair:
            return value, lax.ppermute(value, "fsdp", swap_y)
        whole = lax.all_gather(value, "fsdp", axis=axis, tiled=True)
        return tuple(lax.slice_in_dim(whole, i * half, (i + 1) * half, axis=axis) for i in range(2))

    def added(keep, got, i):
        return keep[i] + got[i].astype(F32)

    rows = ctx * block
    smem = pl.BlockSpec(memory_space=pltpu.SMEM)
    piece_spec = pl.BlockSpec((1, quarter, width), lambda b: (b, 0, 0))
    pair_spec = pl.BlockSpec((1, 2, quarter, width), lambda b: (b, 0, 0, 0))
    pair_first = pl.BlockSpec((1, None, quarter, width), lambda b: (b, 0, 0, 0))
    block_local = pl.BlockSpec((1, block, local), lambda b: (b, 0, 0))
    block_half = pl.BlockSpec((1, block, half), lambda b: (b, 0, 0))
    block_hidden = pl.BlockSpec((1, block, hidden_width), lambda b: (b, 0, 0))
    block_table = pl.BlockSpec((1, block, 128), lambda b: (b, 0, 0))
    part_spec = pl.BlockSpec((2, 1, quarter, width), lambda b: (0, b, 0, 0))
    first_part = pl.BlockSpec((1, 1, quarter, width), lambda b: (0, b, 0, 0))
    gain_spec = full((1, width))
    keep_shape = shape_of((2, ctx, quarter, width), F32)
    send_shape = shape_of((2, ctx, quarter, width), BF)
    own_f32 = shape_of((ctx, quarter, width), F32)
    own_low = shape_of((ctx, quarter, width), BF)
    rows_local = shape_of((ctx, block, local), BF)
    rows_half = shape_of((ctx, block, half), BF)
    rows_hidden = shape_of((ctx, block, hidden_width), BF)
    gain_row = shape_of((1, width), F32)

    seg = jnp.stack([t, t ^ 2, t ^ 1, t ^ 3]).astype(jnp.int32)
    turn = y if pair else y * 0
    roll = jnp.reshape(turn, (1,)).astype(jnp.int32)
    x_part, g_part = call(
        own_kernel,
        [shape_of((seqs, quarter, width), BF), shape_of((seqs, 2, quarter, width), BF)],
        jnp.stack([t, t ^ 2, turn, 1 - turn]).astype(jnp.int32),
        tokens.reshape(seqs, tp, quarter, width), out_grad.reshape(seqs, tp, quarter, width),
        in_specs=[smem] + [pl.BlockSpec(memory_space=pltpu.HBM)] * 2,
        scratch=[pltpu.SemaphoreType.DMA((6,))],
        name="own", vmem=4,
    )
    place = (seg[:, None] * quarter + jnp.arange(quarter)[None, :]).reshape(block)
    positions = (jnp.arange(ctx)[:, None] * block + place[None, :]).astype(F32)
    lanes = (jnp.arange(128) % 32).astype(F32)
    table = positions[:, :, None] * (10000.0 ** (-lanes / 32.0))[None, None, :]
    cosine, sine = jnp.cos(table), jnp.sin(table)
    mix_row = jnp.repeat(mix, local // mix.shape[0])[None, :]

    qkv_a, qkv_b = other_half(jnp.transpose(w_qkv, (1, 0, 2)), 1)
    out_a, out_b = other_half(
        jnp.concatenate([output_weight, jnp.stack([gain_attn, gain_mlp])], axis=0), 1
    )
    gate_a, gate_b = other_half(w_gate.T, 1)
    up_a, up_b = other_half(w_up.T, 1)
    down_a, down_b = other_half(w_down, 1)

    x_own = lax.all_to_all(x_part, "ctx", 0, 0)
    x_own, qkv_b, cosine, sine, mix_row = tie(x_own, qkv_b, cosine, sine, mix_row)
    x_second = across(x_own)
    fv = lax.all_to_all(first_values, "ctx", 0, 0).reshape(ctx, tp, quarter, local)
    x_second, out_b = tie(x_second, out_b)
    x_pieces = (x_own, x_second, core(x_own), core(x_second))
    gains = jnp.concatenate([out_a[local:], out_b[local:]], axis=1).astype(F32)
    out_a, out_b = out_a[:local], out_b[:local]
    gain_first, gain_second = gains[0:1], gains[1:2]

    norm_a, norm_b, queries, keys, raw = call(
        qkv_kernel,
        [rows_half, rows_half, rows_local, rows_local, shape_of((ctx, block, local), F32)],
        *x_pieces, gain_first, qkv_a, qkv_b, cosine, sine,
        grid=(ctx,),
        in_specs=[piece_spec] * 4 + [
            gain_spec, full((3, half, local)), full((3, half, local)), block_table, block_table,
        ],
        out_specs=[block_half] * 2 + [block_local] * 3,
        name="norm_qkv",
    )
    values, attended, log_total, keep, send = call(
        attend_kernel,
        [rows_local, rows_local, shape_of((mix.shape[0], ctx, block), F32), keep_shape, send_shape],
        seg, queries, keys, raw, fv, mix_row, out_a, out_b,
        in_specs=[smem] + [pl.BlockSpec(memory_space=pltpu.VMEM)] * 7,
        scratch=[pltpu.VMEM((local, rows), BF), pltpu.VMEM((ctx, local, block), F32)],
        name="attend",
    )
    send, gate_b = tie(send, gate_b)
    got_core = core(send)
    got_x = across(added(keep, got_core, 1).astype(BF))
    g_first = lax.all_to_all(g_part, "ctx", 0, 0)
    got_x, up_b, g_first = tie(got_x, up_b, g_first)
    residual, normed_own = call(
        residual_kernel,
        [own_f32, own_low],
        x_own, keep, got_core, got_x, gain_second,
        grid=(ctx,),
        in_specs=[piece_spec, first_part, first_part, piece_spec, gain_spec],
        out_specs=[piece_spec, piece_spec],
        name="residual_norm", vmem=6,
    )
    n_second = across(normed_own)
    g_second = core(g_first)
    n_second, down_b, g_second = tie(n_second, down_b, g_second)
    mlp_a, mlp_b, last_a, last_b, hidden, grad_gate, grad_up, keep, send = call(
        mlp_kernel,
        [rows_half] * 4 + [rows_hidden] * 3 + [keep_shape, send_shape],
        normed_own, n_second, core(normed_own), core(n_second), g_first, g_second,
        gate_a, gate_b, up_a, up_b, down_a, down_b,
        grid=(ctx,),
        in_specs=[piece_spec] * 4 + [pair_spec] * 2 + [full((hidden_width, half))] * 6,
        out_specs=[block_half] * 4 + [block_hidden] * 3 + [part_spec] * 2,
        name="mlp", vmem=24,
    )

    def weight_grad(left, right):
        return lax.dot_general(
            left.reshape(rows, -1), right.reshape(rows, -1), TN, preferred_element_type=F32
        )

    def exchange(first, second, axis=1):
        if pair:
            return lax.ppermute(second, "fsdp", swap_y)
        return lax.psum_scatter(
            jnp.concatenate([first.astype(BF), second], axis=axis), "fsdp", scatter_dimension=axis, tiled=True
        )

    def joined(first, received):
        return (first + received.astype(F32)).astype(BF) if pair else received

    def plus(shard, received):
        return (shard.astype(F32) + received.astype(F32)).astype(BF)

    def toward(shard):
        return lax.ppermute(shard, "ctx", [(0, 1), (3, 2)])

    def meet(shard):
        return lax.ppermute(shard, "ctx", [(1, 2), (2, 1)])

    def back(shard):
        return lax.ppermute(shard, "ctx", [(1, 0), (2, 3)])

    def settled(shard, received):
        return jnp.where((z == 0) | (z == 3), received, shard).astype(F32)

    got_core = core(send)
    gate_first = weight_grad(grad_gate, mlp_a)
    gate_second = weight_grad(grad_gate, mlp_b).astype(BF)
    onward = added(keep, got_core, 1).astype(BF)

    onward, gate_first, gate_second, grad_up, hidden = tie(onward, gate_first, gate_second, grad_up, hidden)
    got_x = across(onward)
    gate_got = exchange(gate_first, gate_second)
    up_first = weight_grad(grad_up, mlp_a)
    up_second = weight_grad(grad_up, mlp_b).astype(BF)
    down_first = weight_grad(hidden, last_a)
    down_second = weight_grad(hidden, last_b).astype(BF)
    grad_residual, branch_own, gain_sum_second = call(
        norm_back_kernel,
        [own_f32, own_low, gain_row],
        g_first, keep, got_core, got_x, residual, gain_second,
        grid=(ctx,),
        in_specs=[pair_first, first_part, first_part, piece_spec, piece_spec, gain_spec],
        out_specs=[piece_spec, piece_spec, gain_spec],
        name="norm_back_mlp", vmem=6, us=10,
    )
    (
        branch_own, grad_residual, gate_got, gate_first, up_first, up_second, down_first, down_second, hidden,
    ) = tie(branch_own, grad_residual, gate_got, gate_first, up_first, up_second, down_first, down_second, hidden)

    b_second = across(branch_own)
    b_core = core(branch_own)
    b_both = core(b_second)
    up_got = exchange(up_first, up_second)
    gate_shard = joined(gate_first, gate_got)
    gate_more = toward(gate_shard)
    down_keep, down_send = call(
        down_kernel,
        [keep_shape, send_shape],
        hidden, down_a, down_b,
        grid=(ctx,),
        in_specs=[block_hidden, full((hidden_width, half)), full((hidden_width, half))],
        out_specs=[part_spec, part_spec],
        name="down", vmem=12,
    )
    down_core = core(down_send)
    down_onward = added(down_keep, down_core, 1).astype(BF)
    output_own = residual + added(down_keep, down_core, 0)
    (
        b_second, b_core, b_both, up_got, gate_shard, gate_more, down_onward, output_own, down_second,
    ) = tie(b_second, b_core, b_both, up_got, gate_shard, gate_more, down_onward, output_own, down_second)

    down_x = across(down_onward)
    down_got = exchange(down_first, down_second)
    gate_shard = plus(gate_shard, gate_more)
    gate_more = meet(gate_shard)
    up_shard = joined(up_first, up_got)
    up_more = toward(up_shard)
    payload = shape_of((local + 16, half), F32), shape_of((local + 16, half), BF)
    grads, gf, keep, send, out_first, out_second = call(
        attend_back_kernel,
        [shape_of((ctx, block, 3 * local), BF), shape_of((ctx, tp, quarter, local), BF), keep_shape, send_shape, *payload],
        seg, branch_own, b_second, b_core, b_both, out_a, out_b,
        queries, keys, values, attended, log_total, cosine, sine, mix_row, raw, fv,
        *x_pieces, qkv_a, qkv_b, gain_sum_second,
        in_specs=[smem] + [pl.BlockSpec(memory_space=pltpu.VMEM)] * 23,
        scratch=[
            pltpu.VMEM((ctx, block, local), BF),
            pltpu.VMEM((ctx, 8, block), F32),
            pltpu.VMEM((local, rows), BF),
            pltpu.VMEM((ctx, block, local), F32),
            pltpu.VMEM((ctx, block, local), F32),
            pltpu.VMEM((ctx, local, block), F32),
            pltpu.VMEM((local, width), F32),
        ],
        name="attend_back", vmem=36,
    )
    got_core = core(send)
    onward = added(keep, got_core, 1).astype(BF)
    (
        onward, grads, out_second, down_got, gate_shard, gate_more, up_shard, up_more, down_x,
    ) = tie(onward, grads, out_second, down_got, gate_shard, gate_more, up_shard, up_more, down_x)

    got_x = across(onward)
    gate_shard = plus(gate_shard, gate_more)
    gate_more = back(gate_shard)
    up_shard = plus(up_shard, up_more)
    up_more = meet(up_shard)
    down_shard = joined(down_first, down_got)
    down_more = toward(down_shard)
    out_got = exchange(out_first, out_second)
    qkv_first = weight_grad(norm_a, grads)
    qkv_second = weight_grad(norm_b, grads).astype(BF)
    qkv_got = exchange(qkv_first, qkv_second, 0)
    output_own = (output_own + down_x.astype(F32)).astype(BF)
    _, tokens_own, _ = call(
        norm_back_kernel,
        [own_f32, own_low, gain_row],
        grad_residual, keep, got_core, got_x, x_own, gain_first,
        grid=(ctx,),
        in_specs=[piece_spec, first_part, first_part, piece_spec, piece_spec, gain_spec],
        out_specs=[piece_spec, piece_spec, gain_spec],
        name="norm_back_attn", vmem=6, us=10,
    )
    (
        tokens_own, output_own, gate_shard, gate_more, up_shard, up_more, down_shard, down_more,
    ) = tie(tokens_own, output_own, gate_shard, gate_more, up_shard, up_more, down_shard, down_more)

    tokens_home = lax.all_to_all(tokens_own, "ctx", 0, 0)
    grad_w_gate = settled(gate_shard, gate_more).T
    up_shard = plus(up_shard, up_more)
    down_shard = plus(down_shard, down_more)
    (
        tokens_home, output_own, gf, up_shard, down_shard, out_got, qkv_got,
    ) = tie(tokens_home, output_own, gf, up_shard, down_shard, out_got, qkv_got)
    tokens_second = across(tokens_home)
    output_home = lax.all_to_all(output_own, "ctx", 0, 0)
    up_more = back(up_shard)
    down_more = meet(down_shard)
    out_shard = joined(out_first, out_got)
    out_more = toward(out_shard)
    qkv_shard = joined(qkv_first, qkv_got)
    qkv_more = toward(qkv_shard)
    (
        tokens_second, output_home, gf, up_more, down_more, out_more, qkv_more,
    ) = tie(tokens_second, output_home, gf, up_more, down_more, out_more, qkv_more)
    output_second = across(output_home)
    first_home = lax.all_to_all(gf, "ctx", 0, 0)
    grad_w_up = settled(up_shard, up_more).T
    down_shard = plus(down_shard, down_more)
    down_more = back(down_shard)
    out_shard = plus(out_shard, out_more)
    out_more = meet(out_shard)
    qkv_shard = plus(qkv_shard, qkv_more)
    qkv_more = meet(qkv_shard)
    (
        output_second, first_home, down_more, out_more, qkv_more,
    ) = tie(output_second, first_home, down_more, out_more, qkv_more)
    grad_w_down = settled(down_shard, down_more)
    out_shard = plus(out_shard, out_more)
    qkv_shard = plus(qkv_shard, qkv_more)
    out_full = settled(out_shard, back(out_shard))
    qkv_full = settled(qkv_shard, back(qkv_shard))
    grad_w_qkv = qkv_full.reshape(-1, 3, local)
    grad_w_out = out_full[:local]

    def placed(own, second, dtype):
        return call(
            place_kernel,
            [shape_of((seqs, tp, quarter, width), dtype)],
            seg, roll, own, second, core(own), core(second),
            grid=(seqs,),
            in_specs=[smem, smem] + [piece_spec] * 4,
            out_specs=[pl.BlockSpec((1, tp, quarter, width), lambda b: (b, 0, 0, 0))],
            name="place", vmem=6,
        )[0].reshape(seqs, block, width)

    grad_tokens = placed(tokens_home, tokens_second, F32)
    output = placed(output_home, output_second, BF)
    grad_first = first_home.reshape(seqs, block, local).astype(F32)

    share = gain_attn.shape[0]
    gain_grads = out_full[local:local + 2]
    for move in (core, across):
        gain_grads = gain_grads + move(gain_grads)
    mixed = out_full[local + 2:local + 3]
    if not pair:
        mixed = lax.all_gather(mixed, "fsdp", axis=1, tiled=True)
    mixed = mixed[:, :local]
    grad_mix = jnp.sum(mixed.reshape(mix.shape[0], -1), axis=1)
    return (
        output, grad_tokens, grad_first, grad_w_qkv, grad_w_out, grad_w_gate, grad_w_up, grad_w_down,
        gain_grads[0, :share], gain_grads[1, :share], grad_mix,
    )


def solution(mesh):
    rows = P("fsdp", "ctx", None)
    in_specs = (
        rows, P("fsdp", "ctx", "tp"), rows, P("fsdp", None, "tp"), P("tp", "fsdp"), P("fsdp", "tp"),
        P("fsdp", "tp"), P("tp", "fsdp"), P("fsdp"), P("fsdp"), P("tp"),
    )
    out_specs = (
        rows, rows, P("fsdp", "ctx", "tp"), P("fsdp", None, "tp"), P("tp", "fsdp"), P("fsdp", "tp"),
        P("fsdp", "tp"), P("tp", "fsdp"), P("fsdp"), P("fsdp"), P("tp"),
    )
    sizes = [mesh.shape[name] for name in ("fsdp", "ctx", "tp")]
    return jax.shard_map(
        functools.partial(on_device, *sizes), mesh=mesh, in_specs=in_specs, out_specs=out_specs,
        check_vma=False,
    )
```

```python
import functools

import jax
import jax.numpy as jnp
from jax import lax
from jax.experimental import pallas as pl
from jax.experimental.pallas import tpu as pltpu
from jax.sharding import PartitionSpec as P

EPSILON = 1e-06
SCALE = 0.125
BF = jnp.bfloat16
F32 = jnp.float32
NN = (((1,), (0,)), ((), ()))
NT = (((1,), (1,)), ((), ()))
TN = (((0,), (0,)), ((), ()))


def dot(a, b, dims=NN):
    return lax.dot_general(a, b, dims, preferred_element_type=F32)


def away(item):
    return pltpu.HBM(item.shape, item.dtype)


def full(shape):
    return pl.BlockSpec(shape, lambda *_: (0,) * len(shape))


def call(kernel, out_shapes, *args, grid=None, in_specs=None, out_specs=None, scratch=(), us=0, name=None, vmem=16):
    keywords = {}
    if grid is not None:
        keywords = dict(grid=grid, in_specs=in_specs, out_specs=out_specs)
    elif in_specs is not None:
        keywords = dict(in_specs=in_specs)
    return pl.pallas_call(
        kernel,
        out_shape=out_shapes,
        scratch_shapes=list(scratch),
        cost_estimate=pl.CostEstimate(flops=int(us * 1e9), bytes_accessed=int(us * 3.4e6), transcendentals=0),
        compiler_params=pltpu.CompilerParams(vmem_limit_bytes=vmem << 20),
        name=name,
        **keywords,
    )(*args)


def shape_of(dims, dtype):
    return jax.ShapeDtypeStruct(dims, dtype)


def own_kernel(count, place, source, *refs):
    outs, sems = refs[:count], refs[count]
    half = outs[0].shape[2] // 2
    copies = []
    for p, out in enumerate(outs):
        for h in range(2):
            copies.append(
                pltpu.make_async_copy(
                    source.at[:, place[p], :, pl.ds(pl.multiple_of(place[2 + h] * half, half), half)],
                    out.at[:, :, h * half:(h + 1) * half],
                    sems.at[len(copies)],
                )
            )
    for copy in copies:
        copy.start()
    for copy in copies:
        copy.wait()


def half_swap(values, lane):
    width = values.shape[-1]
    ahead = pltpu.roll(values, width - 32, 1)
    behind = pltpu.roll(values, 32, 1)
    return jnp.where(lane % 64 < 32, ahead, behind)


def signed_tables(cos_ref, sin_ref, index, width, lane):
    cosine = jnp.concatenate([cos_ref[index]] * (width // 128), axis=1)
    sine = jnp.concatenate([sin_ref[index]] * (width // 128), axis=1)
    return cosine, jnp.where(lane % 64 < 32, -sine, sine)


def attend_kernel(
    seg, p0, p1, p2, p3, gain, wa, wb, fv, cos, sin, mix, woa, wob,
    na_o, nb_o, q, k, v, diff_o, att_o, lse_o, keep_o, pass_o, send_o,
    v_t, o_t,
):
    blocks, rows, width = q.shape
    heads = width // 64
    half = wa.shape[1]
    lane_full = lax.broadcasted_iota(jnp.int32, (1, width), 1)
    for b in range(blocks):
        x = jnp.concatenate([p0[b], p1[b], p2[b], p3[b]], axis=0).astype(F32)
        inverse = lax.rsqrt(jnp.mean(x * x, axis=-1, keepdims=True) + EPSILON)
        normed = (x * inverse * gain[...]).astype(BF)
        na, nb = normed[:, :half], normed[:, half:]
        na_o[b] = na
        nb_o[b] = nb
        cosine, sine = signed_tables(cos, sin, b, width, lane_full)
        raw = [dot(na, wa[i]) + dot(nb, wb[i]) for i in range(3)]
        q[b] = (raw[0] * cosine + half_swap(raw[0], lane_full) * sine).astype(BF)
        k[b] = (raw[1] * cosine + half_swap(raw[1], lane_full) * sine).astype(BF)
        first = jnp.concatenate([fv[b, seg[r]] for r in range(4)], axis=0).astype(F32)
        value = mix[...] * raw[2] + (1.0 - mix[...]) * first
        v[b] = value.astype(BF)
        v_t[:, b * rows:(b + 1) * rows] = value.T.astype(BF)
        diff_o[b] = raw[2] - first
    lane = lax.broadcasted_iota(jnp.int32, (1, width), 1) // 64

    def head(h, carry):
        own = lane == h
        for qb in range(blocks):
            qm = jnp.where(own, q[qb], jnp.zeros_like(q[qb]))
            scores = [dot(k[kb], qm, NT) * SCALE for kb in range(qb + 1)]
            top = functools.reduce(jnp.maximum, [jnp.max(s, axis=0, keepdims=True) for s in scores])
            total = jnp.zeros((1, rows), F32)
            out = jnp.zeros((64, rows), F32)
            for kb in range(qb + 1):
                e = jnp.exp(scores[kb] - top)
                total = total + jnp.sum(e, axis=0, keepdims=True)
                out = out + dot(v_t[pl.ds(pl.multiple_of(h * 64, 64), 64), kb * rows:(kb + 1) * rows], e.astype(BF))
            o_t[qb, pl.ds(pl.multiple_of(h * 64, 64), 64), :] = out / total
            lse_o[h, qb:qb + 1, :] = top + jnp.log(total)
        return carry

    lax.fori_loop(0, heads, head, 0)
    quarter = rows // 4
    for qb in range(blocks):
        att = o_t[qb].T.astype(BF)
        att_o[qb] = att
        for lo, w in ((0, woa), (half, wob)):
            part = dot(att, w[...])
            for p, out in enumerate((keep_o, pass_o)):
                out[qb, :, lo:lo + half] = part[p * quarter:(p + 1) * quarter]
            for p in range(2):
                send_o[p, qb, :, lo:lo + half] = part[(2 + p) * quarter:(3 + p) * quarter].astype(BF)


def residual_kernel(x, keep, got_core, got_x, gain, residual_o, normed_o):
    residual = (
        x[0].astype(F32) + keep[0] + got_core[0, 0].astype(F32) + got_x[0].astype(F32)
    )
    inverse = lax.rsqrt(jnp.mean(residual * residual, axis=-1, keepdims=True) + EPSILON)
    residual_o[0] = residual
    normed_o[0] = (residual * inverse * gain[...]).astype(BF)


def mlp_kernel(
    n0, n1, n2, n3, g0, g1, g2, g3, ga, gb, ua, ub, da, la, db, lb,
    na_o, nb_o, la_o, lb_o, hidden_o, dgate_o, dup_o, keep_o, pass_o, send_o,
):
    n = jnp.concatenate([n0[0], n1[0], n2[0], n3[0]], axis=0)
    g = jnp.concatenate([g0[0], g1[0], g2[0], g3[0]], axis=0)
    half = ga.shape[1]
    na, nb = n[:, :half], n[:, half:]
    na_o[0] = na
    nb_o[0] = nb
    la_o[0] = g[:, :half]
    lb_o[0] = g[:, half:]
    gate = dot(na, ga[...], NT) + dot(nb, gb[...], NT)
    up = dot(na, ua[...], NT) + dot(nb, ub[...], NT)
    wa = jnp.concatenate([da[...], la[...]], axis=0)
    wb = jnp.concatenate([db[...], lb[...]], axis=0)
    grad_hidden = dot(g[:, :half], wa, NT) + dot(g[:, half:], wb, NT)
    s = jax.nn.sigmoid(gate)
    active = gate * s
    hidden_o[0] = (active * up).astype(BF)
    dgate = (grad_hidden * up * s * (1.0 + gate * (1.0 - s))).astype(BF)
    dup = (grad_hidden * active).astype(BF)
    dgate_o[0] = dgate
    dup_o[0] = dup
    quarter = n.shape[0] // 4
    for lo, wg, wu in ((0, ga, ua), (half, gb, ub)):
        part = dot(dgate, wg[...]) + dot(dup, wu[...])
        for p, out in enumerate((keep_o, pass_o)):
            out[0, :, lo:lo + half] = part[p * quarter:(p + 1) * quarter]
        for p in range(2):
            send_o[p, 0, :, lo:lo + half] = part[(2 + p) * quarter:(3 + p) * quarter].astype(BF)


def down_kernel(hidden, da, la, db, lb, keep_o, pass_o, send_o):
    half = da.shape[1]
    quarter = hidden.shape[1] // 4
    for lo, w, late in ((0, da, la), (half, db, lb)):
        part = dot(hidden[0], jnp.concatenate([w[...], late[...]], axis=0))
        for p, out in enumerate((keep_o, pass_o)):
            out[0, :, lo:lo + half] = part[p * quarter:(p + 1) * quarter]
        for p in range(2):
            send_o[p, 0, :, lo:lo + half] = part[(2 + p) * quarter:(3 + p) * quarter].astype(BF)


def norm_back_kernel(direct, keep, got_core, got_x, values, gain, grad_o, low_o, gain_o):
    @pl.when(pl.program_id(0) == 0)
    def _():
        gain_o[...] = jnp.zeros_like(gain_o)

    grad = keep[0] + got_core[0, 0].astype(F32) + got_x[0].astype(F32)
    x = values[0].astype(F32)
    inverse = lax.rsqrt(jnp.mean(x * x, axis=-1, keepdims=True) + EPSILON)
    weighted = grad * gain[...]
    gain_o[...] += jnp.sum(grad * x * inverse, axis=0, keepdims=True)
    out = direct[0].astype(F32) + (
        inverse * weighted
        - x * (inverse * inverse * inverse) * jnp.mean(weighted * x, axis=-1, keepdims=True)
    )
    grad_o[0] = out
    low_o[0] = out.astype(BF)


def attend_back_kernel(
    seg, b0, b1, b2, b3, woa, wob, q, k, v, att, lse, cos, sin, mix, diff,
    p0, p1, p2, p3, wa, wb, na, nb, gain_in,
    gf_o, keep_o, pass_o, send_o, own_o, other_o, own2_o, other2_o,
    gat, dmat, k_t, dk, dv, dq_t, og, og2,
):
    blocks, rows, width = q.shape
    heads = width // 64
    half = woa.shape[1]
    lane_full = lax.broadcasted_iota(jnp.int32, (1, width), 1)
    lane = lane_full // 64
    pick = (
        lax.broadcasted_iota(jnp.int32, (8, width), 0)
        == lax.broadcasted_iota(jnp.int32, (8, width), 1) // 64
    ).astype(F32)
    og[...] = jnp.zeros_like(og)
    og2[...] = jnp.zeros_like(og2)
    for b in range(blocks):
        g = jnp.concatenate([b0[b], b1[b], b2[b], b3[b]], axis=0)
        og[:width] += dot(att[b], g, TN)
        ga = (dot(g[:, :half], woa[...], NT) + dot(g[:, half:], wob[...], NT)).astype(BF)
        gat[b] = ga
        prod = ga.astype(F32) * att[b].astype(F32)
        dmat[b] = lax.dot_general(pick, prod, NT, precision=lax.Precision.HIGHEST, preferred_element_type=F32)
        k_t[:, b * rows:(b + 1) * rows] = k[b].astype(F32).T.astype(BF)
    dk[...] = jnp.zeros_like(dk)
    dv[...] = jnp.zeros_like(dv)

    def head(h, carry):
        own = lane == h
        for qb in range(blocks):
            qm = jnp.where(own, q[qb], jnp.zeros_like(q[qb]))
            gm = jnp.where(own, gat[qb], jnp.zeros_like(gat[qb]))
            log_total = lse[h, qb:qb + 1, :]
            row_dot = dmat[qb, pl.ds(h, 1), :]
            acc = jnp.zeros((64, rows), F32)
            for kb in range(qb + 1):
                prob = jnp.exp(dot(k[kb], qm, NT) * SCALE - log_total)
                dprob = dot(v[kb], gm, NT)
                ds = (prob * (dprob - row_dot)).astype(BF)
                dv[kb] += dot(prob.astype(BF), gm)
                dk[kb] += dot(ds, qm)
                acc = acc + dot(k_t[pl.ds(pl.multiple_of(h * 64, 64), 64), kb * rows:(kb + 1) * rows], ds)
            dq_t[qb, pl.ds(pl.multiple_of(h * 64, 64), 64), :] = acc
        return carry

    lax.fori_loop(0, heads, head, 0)
    quarter = rows // 4
    total = jnp.zeros((1, width), F32)
    gains = [jnp.zeros((1, half), F32) for _ in range(2)]
    for b in range(blocks):
        cosine, sine = signed_tables(cos, sin, b, width, lane_full)
        gq = dq_t[b].T * SCALE
        gk = dk[b] * SCALE
        gv = dv[b]
        grads = [
            (gq * cosine - half_swap(gq, lane_full) * sine).astype(BF),
            (gk * cosine - half_swap(gk, lane_full) * sine).astype(BF),
            (mix[...] * gv).astype(BF),
        ]
        for i, n in enumerate((na, nb)):
            lanes = slice(i * half, (i + 1) * half)
            og2[:width, lanes] += dot(grads[0], n[b], TN)
            og2[width:, lanes] += dot(grads[1], n[b], TN)
            og[width:, lanes] += dot(grads[2], n[b], TN)
        x = jnp.concatenate([p0[b], p1[b], p2[b], p3[b]], axis=0).astype(F32)
        x = x * lax.rsqrt(jnp.mean(x * x, axis=-1, keepdims=True) + EPSILON)
        for i, w in enumerate((wa, wb)):
            lanes = slice(i * half, (i + 1) * half)
            part = sum(dot(grad, w[j], NT) for j, grad in enumerate(grads))
            gains[i] = gains[i] + jnp.sum(part * x[:, lanes], axis=0, keepdims=True)
            for p, out in enumerate((keep_o, pass_o)):
                out[b, :, lanes] = part[p * quarter:(p + 1) * quarter]
            for p in range(2):
                send_o[p, b, :, lanes] = part[(2 + p) * quarter:(3 + p) * quarter].astype(BF)
        gf = ((1.0 - mix[...]) * gv).astype(BF)
        for r in range(4):
            gf_o[b, seg[r]] = gf[r * quarter:(r + 1) * quarter]
        total = total + jnp.sum(gv * diff[b], axis=0, keepdims=True)
    row = lax.broadcasted_iota(jnp.int32, (16, half), 0)
    mixed = jnp.concatenate([total, jnp.zeros((1, half - width), F32)], axis=1)
    for i, (out, out2) in enumerate(((own_o, own2_o), (other_o, other2_o))):
        lanes = slice(i * half, (i + 1) * half)
        extra = jnp.where(row == 0, gains[i], jnp.where(row == 1, gain_in[:, lanes], jnp.where(row == 2, mixed, 0.0)))
        out[:2 * width] = og[:, lanes].astype(out.dtype)
        out[2 * width:] = extra.astype(out.dtype)
        out2[...] = og2[:, lanes].astype(out.dtype)


def place_kernel(where, roll, *refs):
    pieces, out = refs[:-1], refs[-1]
    width = out.shape[-1]
    half = width // 2
    for r, piece in enumerate(pieces):
        value = piece[0]
        low, high = value[:, :half], value[:, half:]
        swap = roll[0] == 1
        out[0, where[r], :, :half] = jnp.where(swap, high, low).astype(out.dtype)
        out[0, where[r], :, half:] = jnp.where(swap, low, high).astype(out.dtype)


def first_kernel(got, out):
    out[...] = got[...].astype(out.dtype)


def on_device(
    fsdp, ctx, tp,
    tokens, first_values, out_grad, w_qkv, output_weight, w_gate, w_up, w_down, gain_attn, gain_mlp, mix,
):
    seqs, block, width = tokens.shape
    local = w_qkv.shape[2]
    hidden_width = w_gate.shape[1]
    quarter = block // tp
    half = width // 2
    pair = fsdp == 2
    assert seqs == ctx and ctx == 4 and tp == 4 and local <= half
    y = lax.axis_index("fsdp")
    z = lax.axis_index("ctx")
    t = lax.axis_index("tp")
    swap_y = [(0, 1), (1, 0)]
    by_core = [(i, i ^ 1) for i in range(tp)]
    by_x = [(i, i ^ 2) for i in range(tp)]

    def tie(*values):
        return lax.optimization_barrier(values)

    def core(value):
        return lax.ppermute(value, "tp", by_core)

    def across(value):
        return lax.ppermute(value, "tp", by_x)

    def other_half(value, axis):
        if pair:
            return value, lax.ppermute(value, "fsdp", swap_y)
        whole = lax.all_gather(value, "fsdp", axis=axis, tiled=True)
        return tuple(lax.slice_in_dim(whole, i * half, (i + 1) * half, axis=axis) for i in range(2))

    def added(keep, got):
        return keep + got.astype(F32)

    rows = ctx * block
    smem = pl.BlockSpec(memory_space=pltpu.SMEM)
    piece_spec = pl.BlockSpec((1, quarter, width), lambda b: (b, 0, 0))
    block_local = pl.BlockSpec((1, block, local), lambda b: (b, 0, 0))
    block_half = pl.BlockSpec((1, block, half), lambda b: (b, 0, 0))
    block_hidden = pl.BlockSpec((1, block, hidden_width), lambda b: (b, 0, 0))
    block_table = pl.BlockSpec((1, block, 128), lambda b: (b, 0, 0))
    part_specs = [piece_spec] * 2 + [pl.BlockSpec((2, 1, quarter, width), lambda b: (0, b, 0, 0))]
    first_part = pl.BlockSpec((1, 1, quarter, width), lambda b: (0, b, 0, 0))
    gain_spec = full((1, width))
    send_shape = shape_of((2, ctx, quarter, width), BF)
    own_f32 = shape_of((ctx, quarter, width), F32)
    own_low = shape_of((ctx, quarter, width), BF)
    part_shapes = [own_f32, own_f32, send_shape]
    part_away = [away(own_f32), own_f32, send_shape]
    rows_local = shape_of((ctx, block, local), BF)
    rows_half = shape_of((ctx, block, half), BF)
    rows_hidden = shape_of((ctx, block, hidden_width), BF)
    gain_row = shape_of((1, width), F32)

    seg = jnp.stack([t, t ^ 2, t ^ 1, t ^ 3]).astype(jnp.int32)
    turn = y if pair else y * 0
    roll = jnp.reshape(turn, (1,)).astype(jnp.int32)
    where = jnp.stack([t, t ^ 2, turn, 1 - turn]).astype(jnp.int32)

    def own_rows(value, count):
        return call(
            functools.partial(own_kernel, count),
            [own_low] * count,
            where, value.reshape(seqs, tp, quarter, width),
            in_specs=[smem, pl.BlockSpec(memory_space=pltpu.HBM)],
            scratch=[pltpu.SemaphoreType.DMA((2 * count,))],
            name="own", vmem=4,
        )

    (x_part,) = own_rows(tokens, 1)
    place = (seg[:, None] * quarter + jnp.arange(quarter)[None, :]).reshape(block)
    positions = (jnp.arange(ctx)[:, None] * block + place[None, :]).astype(F32)
    lanes = (jnp.arange(128) % 32).astype(F32)
    table = positions[:, :, None] * (10000.0 ** (-lanes / 32.0))[None, None, :]
    cosine, sine = jnp.cos(table), jnp.sin(table)
    mix_row = jnp.repeat(mix, local // mix.shape[0])[None, :]

    qkv_a, qkv_b = other_half(jnp.transpose(w_qkv, (1, 0, 2)), 1)
    out_a, out_b = other_half(
        jnp.concatenate([output_weight, jnp.stack([gain_attn, gain_mlp])], axis=0), 1
    )
    gate_a, gate_b = other_half(w_gate.T, 1)
    up_a, up_b = other_half(w_up.T, 1)
    early = hidden_width // 4 // 64 * 64
    down_a, down_b = other_half(w_down[:early], 1)
    late_a, late_b = other_half(w_down[early:], 1)

    x_own = lax.all_to_all(x_part, "ctx", 0, 0)
    x_own, qkv_b, cosine, sine, mix_row, g_part, g_late = tie(
        x_own, qkv_b, cosine, sine, mix_row, *own_rows(out_grad, 2)
    )
    x_second = across(x_own)
    fv = lax.all_to_all(first_values, "ctx", 0, 0).reshape(ctx, tp, quarter, local)
    gains = jnp.concatenate([out_a[local:], out_b[local:]], axis=1).astype(F32)
    x_core = core(x_own)
    x_second, out_b, gains = tie(x_second, out_b[:local], gains)
    x_both = core(x_second)
    x_core, x_both, fv, g_part = tie(x_core, x_both, fv, g_part)
    x_pieces = (x_own, x_second, x_core, x_both)
    out_a = output_weight if pair else out_a[:local]
    gain_first, gain_second = gains[0:1], gains[1:2]
    g_first = lax.all_to_all(g_part, "ctx", 0, 0)
    norm_a, norm_b, queries, keys, values, diff, attended, log_total, keep, onward, send = call(
        attend_kernel,
        [away(item) for item in [rows_half] * 2 + [rows_local] * 3 + [
            shape_of((ctx, block, local), F32), rows_local,
        ]] + [shape_of((mix.shape[0], ctx, block), F32)] + part_away,
        seg, *x_pieces, gain_first, qkv_a, qkv_b, fv, cosine, sine, mix_row, out_a, out_b,
        in_specs=[smem] + [pl.BlockSpec(memory_space=pltpu.VMEM)] * 13,
        scratch=[pltpu.VMEM((local, rows), BF), pltpu.VMEM((ctx, local, block), F32)],
        name="attend", vmem=20,
    )
    send, gate_b, g_first, g_late = tie(send, gate_b, g_first, g_late)
    got_core = core(send)
    got_x = across(added(onward, got_core[1]).astype(BF))
    g_second = lax.all_to_all(g_late, "ctx", 0, 0)
    got_x, up_b, down_b, g_second = tie(got_x, up_b, down_b, g_second)
    residual, normed_own = call(
        residual_kernel,
        [own_f32, own_low],
        x_own, keep, got_core, got_x, gain_second,
        grid=(ctx,),
        in_specs=[piece_spec, piece_spec, first_part, piece_spec, gain_spec],
        out_specs=[piece_spec, piece_spec],
        name="residual_norm", vmem=6, us=20,
    )
    down_specs = [full((n, half)) for n in (early, hidden_width - early)] * 2
    n_second = across(normed_own)
    mlp_a, mlp_b, last_a, last_b, hidden, grad_gate, grad_up, keep, onward, send = call(
        mlp_kernel,
        [rows_half] * 4 + [rows_hidden] * 3 + part_shapes,
        normed_own, n_second, core(normed_own), core(n_second), g_first, g_second, core(g_first), core(g_second),
        gate_a, gate_b, up_a, up_b, down_a, late_a, down_b, late_b,
        grid=(ctx,),
        in_specs=[piece_spec] * 8 + [full((hidden_width, half))] * 4 + down_specs,
        out_specs=[block_half] * 4 + [block_hidden] * 3 + part_specs,
        name="mlp", vmem=24, us=10,
    )

    def placed(*pieces):
        *pieces, dtype = pieces
        return call(
            place_kernel,
            [shape_of((seqs, tp, quarter, width), dtype)],
            seg, roll, *pieces,
            grid=(seqs,),
            in_specs=[smem, smem] + [piece_spec] * 4,
            out_specs=[pl.BlockSpec((1, tp, quarter, width), lambda b: (b, 0, 0, 0))],
            name="place", vmem=6,
        )[0].reshape(seqs, block, width)

    def weight_grad(left, right):
        return lax.dot_general(
            left.reshape(rows, -1), right.reshape(rows, -1), TN, preferred_element_type=F32
        )

    def exchange(first, second, axis=1):
        if pair:
            return lax.ppermute(second, "fsdp", swap_y)
        return lax.psum_scatter(
            jnp.concatenate([first.astype(BF), second], axis=axis), "fsdp", scatter_dimension=axis, tiled=True
        )

    def joined(first, received):
        return (first + received.astype(F32)).astype(BF) if pair else received

    def plus(shard, received):
        return (shard.astype(F32) + received.astype(F32)).astype(BF)

    def toward(shard):
        return lax.ppermute(shard, "ctx", [(0, 1), (3, 2)])

    def meet(shard):
        return lax.ppermute(shard, "ctx", [(1, 2), (2, 1)])

    def back(shard):
        return lax.ppermute(shard, "ctx", [(1, 0), (2, 3)])

    def settled(shard, received):
        return jnp.where((z == 0) | (z == 3), received, shard).astype(F32)

    got_core = core(send)
    gate_first = weight_grad(grad_gate, mlp_a)
    gate_second = weight_grad(grad_gate, mlp_b).astype(BF)
    onward = added(onward, got_core[1]).astype(BF)

    onward, gate_first, gate_second, grad_up, hidden = tie(onward, gate_first, gate_second, grad_up, hidden)
    got_x = across(onward)
    gate_got = exchange(gate_first, gate_second)
    up_first = weight_grad(grad_up, mlp_a)
    up_second = weight_grad(grad_up, mlp_b).astype(BF)
    down_first = weight_grad(hidden, last_a)
    down_second = weight_grad(hidden, last_b).astype(BF)
    down_keep, down_onward, down_send = call(
        down_kernel,
        part_shapes,
        hidden, down_a, late_a, down_b, late_b,
        grid=(ctx,),
        in_specs=[block_hidden] + down_specs,
        out_specs=part_specs,
        name="down", vmem=12,
    )
    down_core = core(down_send)
    down_onward = added(down_onward, down_core[1]).astype(BF)
    output_own = residual + added(down_keep, down_core[0])
    grad_residual, branch_own, gain_sum_second = call(
        norm_back_kernel,
        [own_f32, own_low, gain_row],
        g_first, keep, got_core, got_x, residual, gain_second,
        grid=(ctx,),
        in_specs=[piece_spec, piece_spec, first_part, piece_spec, piece_spec, gain_spec],
        out_specs=[piece_spec, piece_spec, gain_spec],
        name="norm_back_mlp", vmem=6, us=20,
    )
    (
        branch_own, grad_residual, gate_got, gate_first, up_first, up_second, down_first, down_second,
        down_onward, output_own,
    ) = tie(
        branch_own, grad_residual, gate_got, gate_first, up_first, up_second, down_first, down_second,
        down_onward, output_own,
    )

    b_second = across(branch_own)
    b_core = core(branch_own)
    b_both = core(b_second)
    up_got = exchange(up_first, up_second)
    gate_shard = joined(gate_first, gate_got)
    gate_more = toward(gate_shard)
    (
        b_second, b_core, b_both, up_got, gate_shard, gate_more, down_onward, output_own, down_second,
    ) = tie(b_second, b_core, b_both, up_got, gate_shard, gate_more, down_onward, output_own, down_second)

    down_x = across(down_onward)
    down_got = exchange(down_first, down_second)
    gate_shard = plus(gate_shard, gate_more)
    gate_more = meet(gate_shard)
    up_shard = joined(up_first, up_got)
    up_more = toward(up_shard)
    payload = [shape_of((2 * local + n, half), kind) for n in (16, 0) for kind in (F32, BF)]
    gf, keep, onward, send, out_first, out_second, qk_first, qk_second = call(
        attend_back_kernel,
        [away(shape_of((ctx, tp, quarter, local), BF)), *part_away, *[away(item) for item in payload]],
        seg, branch_own, b_second, b_core, b_both, out_a, out_b,
        queries, keys, values, attended, log_total, cosine, sine, mix_row, diff,
        *x_pieces, qkv_a, qkv_b, norm_a, norm_b, gain_sum_second,
        in_specs=[smem] + [pl.BlockSpec(memory_space=pltpu.VMEM)] * 24,
        scratch=[
            pltpu.VMEM((ctx, block, local), BF),
            pltpu.VMEM((ctx, 8, block), F32),
            pltpu.VMEM((local, rows), BF),
            pltpu.VMEM((ctx, block, local), F32),
            pltpu.VMEM((ctx, block, local), F32),
            pltpu.VMEM((ctx, local, block), F32),
            pltpu.VMEM((2 * local, width), F32),
            pltpu.VMEM((2 * local, width), F32),
        ],
        name="attend_back", vmem=40, us=30,
    )
    send, down_got, gate_more, up_more, down_x = tie(send, down_got, gate_more, up_more, down_x)
    got_core = core(send)
    onward = added(onward, got_core[1]).astype(BF)
    (
        onward, qk_second, out_second, down_got, gate_shard, gate_more, up_shard, up_more, down_x,
    ) = tie(onward, qk_second, out_second, down_got, gate_shard, gate_more, up_shard, up_more, down_x)

    got_x = across(onward)
    gate_shard = plus(gate_shard, gate_more)
    gate_more = back(gate_shard)
    up_shard = plus(up_shard, up_more)
    up_more = meet(up_shard)
    down_shard = joined(down_first, down_got)
    down_more = toward(down_shard)
    qk_got = exchange(qk_first, qk_second)
    output_own = (output_own + down_x.astype(F32)).astype(BF)
    _, tokens_own, _ = call(
        norm_back_kernel,
        [own_f32, own_low, gain_row],
        grad_residual, keep, got_core, got_x, x_own, gain_first,
        grid=(ctx,),
        in_specs=[piece_spec, piece_spec, first_part, piece_spec, piece_spec, gain_spec],
        out_specs=[piece_spec, piece_spec, gain_spec],
        name="norm_back_attn", vmem=6, us=20,
    )
    tokens_own, output_own, gf, out_second, gate_shard, up_shard, down_shard = tie(
        tokens_own, output_own, gf, out_second, gate_shard, up_shard, down_shard
    )

    tokens_home = lax.all_to_all(tokens_own, "ctx", 0, 0)
    out_got = exchange(out_first, out_second)
    grad_w_gate = settled(gate_shard, gate_more).T
    up_shard = plus(up_shard, up_more)
    down_shard = plus(down_shard, down_more)
    qk_shard = joined(qk_first, qk_got)
    tokens_home, output_own, gf, grad_w_gate, up_shard, down_shard, qk_shard = tie(
        tokens_home, output_own, gf, grad_w_gate, up_shard, down_shard, qk_shard
    )
    tokens_second = across(tokens_home)
    tokens_core = core(tokens_home)
    up_more = back(up_shard)
    down_more = meet(down_shard)
    qk_more = toward(qk_shard)
    out_shard = joined(out_first, out_got)
    tokens_second, out_shard, output_own, gf, up_more, down_more, qk_more = tie(
        tokens_second, out_shard, output_own, gf, up_more, down_more, qk_more
    )
    output_home = lax.all_to_all(output_own, "ctx", 0, 0)
    down_shard = plus(down_shard, down_more)
    down_more = back(down_shard)
    qk_shard = plus(qk_shard, qk_more)
    qk_more = meet(qk_shard)
    out_more = toward(out_shard)
    grad_tokens = placed(tokens_home, tokens_second, tokens_core, core(tokens_second), F32)
    grad_w_up = settled(up_shard, up_more).T
    output_home, gf, grad_tokens, grad_w_up, down_more, qk_more, out_more = tie(
        output_home, gf, grad_tokens, grad_w_up, down_more, qk_more, out_more
    )
    output_second = across(output_home)
    output_core = core(output_home)
    first_home = lax.all_to_all(gf, "ctx", 0, 0)
    qk_shard = plus(qk_shard, qk_more)
    qk_more = back(qk_shard)
    out_shard = plus(out_shard, out_more)
    out_more = meet(out_shard)
    grad_w_down = settled(down_shard, down_more)
    output_second, first_home, grad_w_down, qk_more, out_more = tie(
        output_second, first_home, grad_w_down, qk_more, out_more
    )
    out_shard = plus(out_shard, out_more)
    out_more = back(out_shard)
    output = placed(output_home, output_second, output_core, core(output_second), BF)
    grad_first = first_home.reshape(seqs, block, local).astype(F32)
    qk_full = settled(qk_shard, qk_more).T
    output, grad_first, qk_full, out_more = tie(output, grad_first, qk_full, out_more)
    out_full = settled(out_shard, out_more)
    v_full = out_full[local:2 * local].T
    grad_w_qkv = jnp.stack([qk_full[:, :local], qk_full[:, local:], v_full], axis=1)
    grad_w_out = out_full[:local]

    share = gain_attn.shape[0]
    gain_grads = out_full[2 * local:2 * local + 2]
    for move in (core, across):
        gain_grads = gain_grads + move(gain_grads)
    mixed = out_full[2 * local + 2:2 * local + 3]
    if not pair:
        mixed = lax.all_gather(mixed, "fsdp", axis=1, tiled=True)
    mixed = mixed[:, :local]
    grad_mix = jnp.sum(mixed.reshape(mix.shape[0], -1), axis=1)
    return (
        output, grad_tokens, grad_first, grad_w_qkv, grad_w_out, grad_w_gate, grad_w_up, grad_w_down,
        gain_grads[0, :share], gain_grads[1, :share], grad_mix,
    )


def solution(mesh):
    rows = P("fsdp", "ctx", None)
    in_specs = (
        rows, P("fsdp", "ctx", "tp"), rows, P("fsdp", None, "tp"), P("tp", "fsdp"), P("fsdp", "tp"),
        P("fsdp", "tp"), P("tp", "fsdp"), P("fsdp"), P("fsdp"), P("tp"),
    )
    out_specs = (
        rows, rows, P("fsdp", "ctx", "tp"), P("fsdp", None, "tp"), P("tp", "fsdp"), P("fsdp", "tp"),
        P("fsdp", "tp"), P("tp", "fsdp"), P("fsdp"), P("fsdp"), P("tp"),
    )
    sizes = [mesh.shape[name] for name in ("fsdp", "ctx", "tp")]
    return jax.shard_map(
        functools.partial(on_device, *sizes), mesh=mesh, in_specs=in_specs, out_specs=out_specs,
        check_vma=False,
    )
```

```python
import functools

import jax
import jax.numpy as jnp
from jax import lax
from jax.experimental import pallas as pl
from jax.experimental.pallas import tpu as pltpu
from jax.sharding import PartitionSpec as P

EPSILON = 1e-06
SCALE = 0.125
BF = jnp.bfloat16
F32 = jnp.float32
NN = (((1,), (0,)), ((), ()))
NT = (((1,), (1,)), ((), ()))
TN = (((0,), (0,)), ((), ()))


def dot(a, b, dims=NN):
    return lax.dot_general(a, b, dims, preferred_element_type=F32)


def away(item):
    return pltpu.HBM(item.shape, item.dtype)


def full(shape):
    return pl.BlockSpec(shape, lambda *_: (0,) * len(shape))


def call(kernel, out_shapes, *args, grid=None, in_specs=None, out_specs=None, scratch=(), us=0, name=None, vmem=16):
    keywords = {}
    if grid is not None:
        keywords = dict(grid=grid, in_specs=in_specs, out_specs=out_specs)
    elif in_specs is not None:
        keywords = dict(in_specs=in_specs)
    return pl.pallas_call(
        kernel,
        out_shape=out_shapes,
        scratch_shapes=list(scratch),
        cost_estimate=pl.CostEstimate(flops=int(us * 1e9), bytes_accessed=int(us * 3.4e6), transcendentals=0),
        compiler_params=pltpu.CompilerParams(vmem_limit_bytes=vmem << 20),
        name=name,
        **keywords,
    )(*args)


def shape_of(dims, dtype):
    return jax.ShapeDtypeStruct(dims, dtype)


def own_kernel(count, place, source, *refs):
    outs, sems = refs[:count], refs[count]
    half = outs[0].shape[2] // 2
    copies = []
    for p, out in enumerate(outs):
        for h in range(2):
            copies.append(
                pltpu.make_async_copy(
                    source.at[:, place[p], :, pl.ds(pl.multiple_of(place[2 + h] * half, half), half)],
                    out.at[:, :, h * half:(h + 1) * half],
                    sems.at[len(copies)],
                )
            )
    for copy in copies:
        copy.start()
    for copy in copies:
        copy.wait()


def half_swap(values, lane):
    width = values.shape[-1]
    ahead = pltpu.roll(values, width - 32, 1)
    behind = pltpu.roll(values, 32, 1)
    return jnp.where(lane % 64 < 32, ahead, behind)


def signed_tables(cos_ref, sin_ref, index, width, lane):
    cosine = jnp.concatenate([cos_ref[index]] * (width // 128), axis=1)
    sine = jnp.concatenate([sin_ref[index]] * (width // 128), axis=1)
    return cosine, jnp.where(lane % 64 < 32, -sine, sine)


def attend_kernel(
    seg, p0, p1, p2, p3, gain, wa, wb, fv, cos, sin, mix, woa, wob,
    na_o, nb_o, q, k, v, diff_o, att_o, lse_o, keep_o, pass_o, send_o,
    v_t, o_t,
):
    blocks, rows, width = q.shape
    heads = width // 64
    half = wa.shape[1]
    lane_full = lax.broadcasted_iota(jnp.int32, (1, width), 1)
    for b in range(blocks):
        x = jnp.concatenate([p0[b], p1[b], p2[b], p3[b]], axis=0).astype(F32)
        inverse = lax.rsqrt(jnp.mean(x * x, axis=-1, keepdims=True) + EPSILON)
        normed = (x * inverse * gain[...]).astype(BF)
        na, nb = normed[:, :half], normed[:, half:]
        na_o[b] = na
        nb_o[b] = nb
        cosine, sine = signed_tables(cos, sin, b, width, lane_full)
        raw = [dot(na, wa[i]) + dot(nb, wb[i]) for i in range(3)]
        q[b] = (raw[0] * cosine + half_swap(raw[0], lane_full) * sine).astype(BF)
        k[b] = (raw[1] * cosine + half_swap(raw[1], lane_full) * sine).astype(BF)
        first = jnp.concatenate([fv[b, seg[r]] for r in range(4)], axis=0).astype(F32)
        value = mix[...] * raw[2] + (1.0 - mix[...]) * first
        v[b] = value.astype(BF)
        v_t[:, b * rows:(b + 1) * rows] = value.T.astype(BF)
        diff_o[b] = raw[2] - first
    lane = lax.broadcasted_iota(jnp.int32, (1, width), 1) // 64

    def head(h, carry):
        own = lane == h
        for qb in range(blocks):
            qm = jnp.where(own, q[qb], jnp.zeros_like(q[qb]))
            scores = [dot(k[kb], qm, NT) * SCALE for kb in range(qb + 1)]
            top = functools.reduce(jnp.maximum, [jnp.max(s, axis=0, keepdims=True) for s in scores])
            total = jnp.zeros((1, rows), F32)
            out = jnp.zeros((64, rows), F32)
            for kb in range(qb + 1):
                e = jnp.exp(scores[kb] - top)
                total = total + jnp.sum(e, axis=0, keepdims=True)
                out = out + dot(v_t[pl.ds(pl.multiple_of(h * 64, 64), 64), kb * rows:(kb + 1) * rows], e.astype(BF))
            o_t[qb, pl.ds(pl.multiple_of(h * 64, 64), 64), :] = out / total
            lse_o[h, qb:qb + 1, :] = top + jnp.log(total)
        return carry

    lax.fori_loop(0, heads, head, 0)
    quarter = rows // 4
    for qb in range(blocks):
        att = o_t[qb].T.astype(BF)
        att_o[qb] = att
        for lo, w in ((0, woa), (half, wob)):
            part = dot(att, w[...])
            for p, out in enumerate((keep_o, pass_o)):
                out[qb, :, lo:lo + half] = part[p * quarter:(p + 1) * quarter]
            for p in range(2):
                send_o[p, qb, :, lo:lo + half] = part[(2 + p) * quarter:(3 + p) * quarter].astype(BF)


def residual_kernel(x, keep, got_core, got_x, gain, residual_o, normed_o):
    residual = (
        x[0].astype(F32) + keep[0] + got_core[0, 0].astype(F32) + got_x[0].astype(F32)
    )
    inverse = lax.rsqrt(jnp.mean(residual * residual, axis=-1, keepdims=True) + EPSILON)
    residual_o[0] = residual
    normed_o[0] = (residual * inverse * gain[...]).astype(BF)


def mlp_kernel(
    n0, n1, n2, n3, g0, g1, g2, g3, ga, gb, ua, ub, da, la, db, lb,
    na_o, nb_o, la_o, lb_o, hidden_o, dgate_o, dup_o, keep_o, pass_o, send_o,
):
    n = jnp.concatenate([n0[0], n1[0], n2[0], n3[0]], axis=0)
    g = jnp.concatenate([g0[0], g1[0], g2[0], g3[0]], axis=0)
    half = ga.shape[1]
    na, nb = n[:, :half], n[:, half:]
    na_o[0] = na
    nb_o[0] = nb
    la_o[0] = g[:, :half]
    lb_o[0] = g[:, half:]
    gate = dot(na, ga[...], NT) + dot(nb, gb[...], NT)
    up = dot(na, ua[...], NT) + dot(nb, ub[...], NT)
    wa = jnp.concatenate([da[...], la[...]], axis=0)
    wb = jnp.concatenate([db[...], lb[...]], axis=0)
    grad_hidden = dot(g[:, :half], wa, NT) + dot(g[:, half:], wb, NT)
    s = jax.nn.sigmoid(gate)
    active = gate * s
    hidden_o[0] = (active * up).astype(BF)
    dgate = (grad_hidden * up * s * (1.0 + gate * (1.0 - s))).astype(BF)
    dup = (grad_hidden * active).astype(BF)
    dgate_o[0] = dgate
    dup_o[0] = dup
    quarter = n.shape[0] // 4
    for lo, wg, wu in ((0, ga, ua), (half, gb, ub)):
        part = dot(dgate, wg[...]) + dot(dup, wu[...])
        for p, out in enumerate((keep_o, pass_o)):
            out[0, :, lo:lo + half] = part[p * quarter:(p + 1) * quarter]
        for p in range(2):
            send_o[p, 0, :, lo:lo + half] = part[(2 + p) * quarter:(3 + p) * quarter].astype(BF)


def down_kernel(hidden, da, la, db, lb, keep_o, pass_o, send_o):
    half = da.shape[1]
    quarter = hidden.shape[1] // 4
    for lo, w, late in ((0, da, la), (half, db, lb)):
        part = dot(hidden[0], jnp.concatenate([w[...], late[...]], axis=0))
        for p, out in enumerate((keep_o, pass_o)):
            out[0, :, lo:lo + half] = part[p * quarter:(p + 1) * quarter]
        for p in range(2):
            send_o[p, 0, :, lo:lo + half] = part[(2 + p) * quarter:(3 + p) * quarter].astype(BF)


def norm_back_kernel(direct, keep, got_core, got_x, values, gain, grad_o, low_o, gain_o):
    @pl.when(pl.program_id(0) == 0)
    def _():
        gain_o[...] = jnp.zeros_like(gain_o)

    grad = keep[0] + got_core[0, 0].astype(F32) + got_x[0].astype(F32)
    x = values[0].astype(F32)
    inverse = lax.rsqrt(jnp.mean(x * x, axis=-1, keepdims=True) + EPSILON)
    weighted = grad * gain[...]
    gain_o[...] += jnp.sum(grad * x * inverse, axis=0, keepdims=True)
    out = direct[0].astype(F32) + (
        inverse * weighted
        - x * (inverse * inverse * inverse) * jnp.mean(weighted * x, axis=-1, keepdims=True)
    )
    grad_o[0] = out
    low_o[0] = out.astype(BF)


def attend_back_kernel(
    seg, b0, b1, b2, b3, woa, wob, q, k, v, att, lse, cos, sin, mix, diff,
    p0, p1, p2, p3, wa, wb, na, nb, gain_in,
    gf_o, keep_o, pass_o, send_o, own_o, other_o, own2_o, other2_o,
    gat, dmat, k_t, dk, dv, dq_t, og, og2,
):
    blocks, rows, width = q.shape
    heads = width // 64
    half = woa.shape[1]
    lane_full = lax.broadcasted_iota(jnp.int32, (1, width), 1)
    lane = lane_full // 64
    pick = (
        lax.broadcasted_iota(jnp.int32, (8, width), 0)
        == lax.broadcasted_iota(jnp.int32, (8, width), 1) // 64
    ).astype(F32)
    og[...] = jnp.zeros_like(og)
    og2[...] = jnp.zeros_like(og2)
    for b in range(blocks):
        g = jnp.concatenate([b0[b], b1[b], b2[b], b3[b]], axis=0)
        og[:width] += dot(att[b], g, TN)
        ga = (dot(g[:, :half], woa[...], NT) + dot(g[:, half:], wob[...], NT)).astype(BF)
        gat[b] = ga
        prod = ga.astype(F32) * att[b].astype(F32)
        dmat[b] = lax.dot_general(pick, prod, NT, precision=lax.Precision.HIGHEST, preferred_element_type=F32)
        k_t[:, b * rows:(b + 1) * rows] = k[b].astype(F32).T.astype(BF)
    dk[...] = jnp.zeros_like(dk)
    dv[...] = jnp.zeros_like(dv)

    def head(h, carry):
        own = lane == h
        for qb in range(blocks):
            qm = jnp.where(own, q[qb], jnp.zeros_like(q[qb]))
            gm = jnp.where(own, gat[qb], jnp.zeros_like(gat[qb]))
            log_total = lse[h, qb:qb + 1, :]
            row_dot = dmat[qb, pl.ds(h, 1), :]
            acc = jnp.zeros((64, rows), F32)
            for kb in range(qb + 1):
                prob = jnp.exp(dot(k[kb], qm, NT) * SCALE - log_total)
                dprob = dot(v[kb], gm, NT)
                ds = (prob * (dprob - row_dot)).astype(BF)
                dv[kb] += dot(prob.astype(BF), gm)
                dk[kb] += dot(ds, qm)
                acc = acc + dot(k_t[pl.ds(pl.multiple_of(h * 64, 64), 64), kb * rows:(kb + 1) * rows], ds)
            dq_t[qb, pl.ds(pl.multiple_of(h * 64, 64), 64), :] = acc
        return carry

    lax.fori_loop(0, heads, head, 0)
    quarter = rows // 4
    total = jnp.zeros((1, width), F32)
    gains = [jnp.zeros((1, half), F32) for _ in range(2)]
    for b in range(blocks):
        cosine, sine = signed_tables(cos, sin, b, width, lane_full)
        gq = dq_t[b].T * SCALE
        gk = dk[b] * SCALE
        gv = dv[b]
        grads = [
            (gq * cosine - half_swap(gq, lane_full) * sine).astype(BF),
            (gk * cosine - half_swap(gk, lane_full) * sine).astype(BF),
            (mix[...] * gv).astype(BF),
        ]
        for i, n in enumerate((na, nb)):
            lanes = slice(i * half, (i + 1) * half)
            og2[:width, lanes] += dot(grads[0], n[b], TN)
            og2[width:, lanes] += dot(grads[1], n[b], TN)
            og[width:, lanes] += dot(grads[2], n[b], TN)
        x = jnp.concatenate([p0[b], p1[b], p2[b], p3[b]], axis=0).astype(F32)
        x = x * lax.rsqrt(jnp.mean(x * x, axis=-1, keepdims=True) + EPSILON)
        for i, w in enumerate((wa, wb)):
            lanes = slice(i * half, (i + 1) * half)
            part = sum(dot(grad, w[j], NT) for j, grad in enumerate(grads))
            gains[i] = gains[i] + jnp.sum(part * x[:, lanes], axis=0, keepdims=True)
            for p, out in enumerate((keep_o, pass_o)):
                out[b, :, lanes] = part[p * quarter:(p + 1) * quarter]
            for p in range(2):
                send_o[p, b, :, lanes] = part[(2 + p) * quarter:(3 + p) * quarter].astype(BF)
        gf = ((1.0 - mix[...]) * gv).astype(BF)
        for r in range(4):
            gf_o[b, seg[r]] = gf[r * quarter:(r + 1) * quarter]
        total = total + jnp.sum(gv * diff[b], axis=0, keepdims=True)
    row = lax.broadcasted_iota(jnp.int32, (16, half), 0)
    mixed = jnp.concatenate([total, jnp.zeros((1, half - width), F32)], axis=1)
    for i, (out, out2) in enumerate(((own_o, own2_o), (other_o, other2_o))):
        lanes = slice(i * half, (i + 1) * half)
        extra = jnp.where(row == 0, gains[i], jnp.where(row == 1, gain_in[:, lanes], jnp.where(row == 2, mixed, 0.0)))
        out[:2 * width] = og[:, lanes].astype(out.dtype)
        out[2 * width:] = extra.astype(out.dtype)
        out2[...] = og2[:, lanes].astype(out.dtype)


def place_kernel(where, roll, *refs):
    pieces, out = refs[:-1], refs[-1]
    width = out.shape[-1]
    half = width // 2
    for r, piece in enumerate(pieces):
        value = piece[0]
        low, high = value[:, :half], value[:, half:]
        swap = roll[0] == 1
        out[0, where[r], :, :half] = jnp.where(swap, high, low).astype(out.dtype)
        out[0, where[r], :, half:] = jnp.where(swap, low, high).astype(out.dtype)


def first_kernel(got, out):
    out[...] = got[...].astype(out.dtype)


def on_device(
    fsdp, ctx, tp,
    tokens, first_values, out_grad, w_qkv, output_weight, w_gate, w_up, w_down, gain_attn, gain_mlp, mix,
):
    seqs, block, width = tokens.shape
    local = w_qkv.shape[2]
    hidden_width = w_gate.shape[1]
    quarter = block // tp
    half = width // 2
    pair = fsdp == 2
    assert seqs == ctx and ctx == 4 and tp == 4 and local <= half
    y = lax.axis_index("fsdp")
    z = lax.axis_index("ctx")
    t = lax.axis_index("tp")
    swap_y = [(0, 1), (1, 0)]
    by_core = [(i, i ^ 1) for i in range(tp)]
    by_x = [(i, i ^ 2) for i in range(tp)]

    def tie(*values):
        return lax.optimization_barrier(values)

    def core(value):
        return lax.ppermute(value, "tp", by_core)

    def across(value):
        return lax.ppermute(value, "tp", by_x)

    def other_half(value, axis):
        if pair:
            return value, lax.ppermute(value, "fsdp", swap_y)
        whole = lax.all_gather(value, "fsdp", axis=axis, tiled=True)
        return tuple(lax.slice_in_dim(whole, i * half, (i + 1) * half, axis=axis) for i in range(2))

    def added(keep, got):
        return keep + got.astype(F32)

    rows = ctx * block
    smem = pl.BlockSpec(memory_space=pltpu.SMEM)
    piece_spec = pl.BlockSpec((1, quarter, width), lambda b: (b, 0, 0))
    block_local = pl.BlockSpec((1, block, local), lambda b: (b, 0, 0))
    block_half = pl.BlockSpec((1, block, half), lambda b: (b, 0, 0))
    block_hidden = pl.BlockSpec((1, block, hidden_width), lambda b: (b, 0, 0))
    block_table = pl.BlockSpec((1, block, 128), lambda b: (b, 0, 0))
    part_specs = [piece_spec] * 2 + [pl.BlockSpec((2, 1, quarter, width), lambda b: (0, b, 0, 0))]
    first_part = pl.BlockSpec((1, 1, quarter, width), lambda b: (0, b, 0, 0))
    gain_spec = full((1, width))
    send_shape = shape_of((2, ctx, quarter, width), BF)
    own_f32 = shape_of((ctx, quarter, width), F32)
    own_low = shape_of((ctx, quarter, width), BF)
    part_shapes = [own_f32, own_f32, send_shape]
    part_away = [away(own_f32), own_f32, send_shape]
    rows_local = shape_of((ctx, block, local), BF)
    rows_half = shape_of((ctx, block, half), BF)
    rows_hidden = shape_of((ctx, block, hidden_width), BF)
    gain_row = shape_of((1, width), F32)

    seg = jnp.stack([t, t ^ 2, t ^ 1, t ^ 3]).astype(jnp.int32)
    turn = y if pair else y * 0
    roll = jnp.reshape(turn, (1,)).astype(jnp.int32)
    where = jnp.stack([t, t ^ 2, turn, 1 - turn]).astype(jnp.int32)

    def own_rows(value, count):
        return call(
            functools.partial(own_kernel, count),
            [own_low] * count,
            where, value.reshape(seqs, tp, quarter, width),
            in_specs=[smem, pl.BlockSpec(memory_space=pltpu.HBM)],
            scratch=[pltpu.SemaphoreType.DMA((2 * count,))],
            name="own", vmem=4,
        )

    (x_part,) = own_rows(tokens, 1)
    place = (seg[:, None] * quarter + jnp.arange(quarter)[None, :]).reshape(block)
    positions = (jnp.arange(ctx)[:, None] * block + place[None, :]).astype(F32)
    lanes = (jnp.arange(128) % 32).astype(F32)
    table = positions[:, :, None] * (10000.0 ** (-lanes / 32.0))[None, None, :]
    cosine, sine = jnp.cos(table), jnp.sin(table)
    mix_row = jnp.repeat(mix, local // mix.shape[0])[None, :]

    qkv_a, qkv_b = other_half(jnp.transpose(w_qkv, (1, 0, 2)), 1)
    out_a, out_b = other_half(
        jnp.concatenate([output_weight, jnp.stack([gain_attn, gain_mlp])], axis=0), 1
    )
    gate_a, gate_b = other_half(w_gate.T, 1)
    up_a, up_b = other_half(w_up.T, 1)
    early = hidden_width // 4 // 64 * 64
    down_a, down_b = other_half(w_down[:early], 1)
    late_a, late_b = other_half(w_down[early:], 1)

    x_own = lax.all_to_all(x_part, "ctx", 0, 0)
    x_second = across(x_own)
    x_own, qkv_b, cosine, sine, mix_row, g_part, g_late = tie(
        x_own, qkv_b, cosine, sine, mix_row, *own_rows(out_grad, 2)
    )
    fv = lax.all_to_all(first_values, "ctx", 0, 0).reshape(ctx, tp, quarter, local)
    gains = jnp.concatenate([out_a[local:], out_b[local:]], axis=1).astype(F32)
    x_core = core(x_own)
    x_second, out_b, gains = tie(x_second, out_b[:local], gains)
    x_both = core(x_second)
    x_core, x_both, fv, g_part = tie(x_core, x_both, fv, g_part)
    x_pieces = (x_own, x_second, x_core, x_both)
    out_a = output_weight if pair else out_a[:local]
    gain_first, gain_second = gains[0:1], gains[1:2]
    g_first = lax.all_to_all(g_part, "ctx", 0, 0)
    norm_a, norm_b, queries, keys, values, diff, attended, log_total, keep, onward, send = call(
        attend_kernel,
        [away(item) for item in [rows_half] * 2 + [rows_local] * 3 + [
            shape_of((ctx, block, local), F32), rows_local,
        ]] + [shape_of((mix.shape[0], ctx, block), F32)] + part_away,
        seg, *x_pieces, gain_first, qkv_a, qkv_b, fv, cosine, sine, mix_row, out_a, out_b,
        in_specs=[smem] + [pl.BlockSpec(memory_space=pltpu.VMEM)] * 13,
        scratch=[pltpu.VMEM((local, rows), BF), pltpu.VMEM((ctx, local, block), F32)],
        name="attend", vmem=20,
    )
    send, gate_b, g_first, g_late = tie(send, gate_b, g_first, g_late)
    got_core = core(send)
    got_x = across(added(onward, got_core[1]).astype(BF))
    g_second = lax.all_to_all(g_late, "ctx", 0, 0)
    got_x, up_b, down_b, g_second = tie(got_x, up_b, down_b, g_second)
    residual, normed_own = call(
        residual_kernel,
        [own_f32, own_low],
        x_own, keep, got_core, got_x, gain_second,
        grid=(ctx,),
        in_specs=[piece_spec, piece_spec, first_part, piece_spec, gain_spec],
        out_specs=[piece_spec, piece_spec],
        name="residual_norm", vmem=6, us=20,
    )
    down_specs = [full((n, half)) for n in (early, hidden_width - early)] * 2
    n_second = across(normed_own)
    mlp_a, mlp_b, last_a, last_b, hidden, grad_gate, grad_up, keep, onward, send = call(
        mlp_kernel,
        [rows_half] * 4 + [rows_hidden] * 3 + part_shapes,
        normed_own, n_second, core(normed_own), core(n_second), g_first, g_second, core(g_first), core(g_second),
        gate_a, gate_b, up_a, up_b, down_a, late_a, down_b, late_b,
        grid=(ctx,),
        in_specs=[piece_spec] * 8 + [full((hidden_width, half))] * 4 + down_specs,
        out_specs=[block_half] * 4 + [block_hidden] * 3 + part_specs,
        name="mlp", vmem=24, us=10,
    )

    def placed(*pieces):
        *pieces, dtype = pieces
        return call(
            place_kernel,
            [shape_of((seqs, tp, quarter, width), dtype)],
            seg, roll, *pieces,
            grid=(seqs,),
            in_specs=[smem, smem] + [piece_spec] * 4,
            out_specs=[pl.BlockSpec((1, tp, quarter, width), lambda b: (b, 0, 0, 0))],
            name="place", vmem=6,
        )[0].reshape(seqs, block, width)

    def weight_grad(left, right):
        return lax.dot_general(
            left.reshape(rows, -1), right.reshape(rows, -1), TN, preferred_element_type=F32
        )

    def exchange(first, second, axis=1):
        if pair:
            return lax.ppermute(second, "fsdp", swap_y)
        return lax.psum_scatter(
            jnp.concatenate([first.astype(BF), second], axis=axis), "fsdp", scatter_dimension=axis, tiled=True
        )

    def joined(first, received):
        return (first + received.astype(F32)).astype(BF) if pair else received

    def plus(shard, received):
        return (shard.astype(F32) + received.astype(F32)).astype(BF)

    def toward(shard):
        return lax.ppermute(shard, "ctx", [(0, 1), (3, 2)])

    def meet(shard):
        return lax.ppermute(shard, "ctx", [(1, 2), (2, 1)])

    def back(shard):
        return lax.ppermute(shard, "ctx", [(1, 0), (2, 3)])

    def settled(shard, received):
        return jnp.where((z == 0) | (z == 3), received, shard).astype(F32)

    got_core = core(send)
    gate_first = weight_grad(grad_gate, mlp_a)
    gate_second = weight_grad(grad_gate, mlp_b).astype(BF)
    onward = added(onward, got_core[1]).astype(BF)

    onward, gate_first, gate_second, grad_up, hidden = tie(onward, gate_first, gate_second, grad_up, hidden)
    got_x = across(onward)
    gate_got = exchange(gate_first, gate_second)
    up_first = weight_grad(grad_up, mlp_a)
    up_second = weight_grad(grad_up, mlp_b).astype(BF)
    down_first = weight_grad(hidden, last_a)
    down_second = weight_grad(hidden, last_b).astype(BF)
    down_keep, down_onward, down_send = call(
        down_kernel,
        part_shapes,
        hidden, down_a, late_a, down_b, late_b,
        grid=(ctx,),
        in_specs=[block_hidden] + down_specs,
        out_specs=part_specs,
        name="down", vmem=12,
    )
    down_core = core(down_send)
    down_onward = added(down_onward, down_core[1]).astype(BF)
    grad_residual, branch_own, gain_sum_second = call(
        norm_back_kernel,
        [own_f32, own_low, gain_row],
        g_first, keep, got_core, got_x, residual, gain_second,
        grid=(ctx,),
        in_specs=[piece_spec, piece_spec, first_part, piece_spec, piece_spec, gain_spec],
        out_specs=[piece_spec, piece_spec, gain_spec],
        name="norm_back_mlp", vmem=6, us=20,
    )
    (
        branch_own, grad_residual, gate_got, gate_first, up_first, up_second, down_first, down_second,
        down_onward,
    ) = tie(
        branch_own, grad_residual, gate_got, gate_first, up_first, up_second, down_first, down_second,
        down_onward,
    )

    b_second = across(branch_own)
    b_core = core(branch_own)
    b_both = core(b_second)
    up_got = exchange(up_first, up_second)
    gate_shard = joined(gate_first, gate_got)
    gate_more = toward(gate_shard)
    (
        b_second, b_core, b_both, up_got, gate_shard, gate_more, down_onward, down_second,
    ) = tie(b_second, b_core, b_both, up_got, gate_shard, gate_more, down_onward, down_second)

    down_x = across(down_onward)
    down_got = exchange(down_first, down_second)
    gate_shard = plus(gate_shard, gate_more)
    gate_more = meet(gate_shard)
    up_shard = joined(up_first, up_got)
    up_more = toward(up_shard)
    payload = [shape_of((2 * local + n, half), kind) for n in (16, 0) for kind in (F32, BF)]
    gf, keep, onward, send, out_first, out_second, qk_first, qk_second = call(
        attend_back_kernel,
        [away(shape_of((ctx, tp, quarter, local), BF)), *part_away, *[away(item) for item in payload]],
        seg, branch_own, b_second, b_core, b_both, out_a, out_b,
        queries, keys, values, attended, log_total, cosine, sine, mix_row, diff,
        *x_pieces, qkv_a, qkv_b, norm_a, norm_b, gain_sum_second,
        in_specs=[smem] + [pl.BlockSpec(memory_space=pltpu.VMEM)] * 24,
        scratch=[
            pltpu.VMEM((ctx, block, local), BF),
            pltpu.VMEM((ctx, 8, block), F32),
            pltpu.VMEM((local, rows), BF),
            pltpu.VMEM((ctx, block, local), F32),
            pltpu.VMEM((ctx, block, local), F32),
            pltpu.VMEM((ctx, local, block), F32),
            pltpu.VMEM((2 * local, width), F32),
            pltpu.VMEM((2 * local, width), F32),
        ],
        name="attend_back", vmem=40, us=30,
    )
    send, down_got, gate_more, up_more, down_x = tie(send, down_got, gate_more, up_more, down_x)
    got_core = core(send)
    onward = added(onward, got_core[1]).astype(BF)
    (
        onward, qk_second, out_second, down_got, gate_shard, gate_more, up_shard, up_more, down_x,
    ) = tie(onward, qk_second, out_second, down_got, gate_shard, gate_more, up_shard, up_more, down_x)

    got_x = across(onward)
    gate_shard = plus(gate_shard, gate_more)
    gate_more = back(gate_shard)
    up_shard = plus(up_shard, up_more)
    up_more = meet(up_shard)
    down_shard = joined(down_first, down_got)
    down_more = toward(down_shard)
    qk_got = exchange(qk_first, qk_second)
    output_own = (residual + added(down_keep, down_core[0]) + down_x.astype(F32)).astype(BF)
    _, tokens_own, _ = call(
        norm_back_kernel,
        [own_f32, own_low, gain_row],
        grad_residual, keep, got_core, got_x, x_own, gain_first,
        grid=(ctx,),
        in_specs=[piece_spec, piece_spec, first_part, piece_spec, piece_spec, gain_spec],
        out_specs=[piece_spec, piece_spec, gain_spec],
        name="norm_back_attn", vmem=6, us=20,
    )
    tokens_own, output_own, gf, out_second, gate_shard, up_shard, down_shard = tie(
        tokens_own, output_own, gf, out_second, gate_shard, up_shard, down_shard
    )

    tokens_home = lax.all_to_all(tokens_own, "ctx", 0, 0)
    out_got = exchange(out_first, out_second)
    grad_w_gate = settled(gate_shard, gate_more).T
    up_shard = plus(up_shard, up_more)
    down_shard = plus(down_shard, down_more)
    qk_shard = joined(qk_first, qk_got)
    tokens_home, output_own, gf, grad_w_gate, up_shard, down_shard, qk_shard = tie(
        tokens_home, output_own, gf, grad_w_gate, up_shard, down_shard, qk_shard
    )
    tokens_second = across(tokens_home)
    tokens_core = core(tokens_home)
    up_more = back(up_shard)
    down_more = meet(down_shard)
    qk_more = toward(qk_shard)
    out_shard = joined(out_first, out_got)
    tokens_second, out_shard, output_own, gf, up_more, down_more, qk_more = tie(
        tokens_second, out_shard, output_own, gf, up_more, down_more, qk_more
    )
    output_home = lax.all_to_all(output_own, "ctx", 0, 0)
    down_shard = plus(down_shard, down_more)
    down_more = back(down_shard)
    qk_shard = plus(qk_shard, qk_more)
    qk_more = meet(qk_shard)
    out_more = toward(out_shard)
    grad_tokens = placed(tokens_home, tokens_second, tokens_core, core(tokens_second), F32)
    grad_w_up = settled(up_shard, up_more).T
    output_home, gf, grad_tokens, grad_w_up = tie(output_home, gf, grad_tokens, grad_w_up)
    output_second = across(output_home)
    output_core = core(output_home)
    first_home = lax.all_to_all(gf, "ctx", 0, 0)
    qk_shard = plus(qk_shard, qk_more)
    qk_more = back(qk_shard)
    out_shard = plus(out_shard, out_more)
    out_more = meet(out_shard)
    grad_w_down = settled(down_shard, down_more)
    out_shard = plus(out_shard, out_more)
    out_more = back(out_shard)
    output = placed(output_home, output_second, output_core, core(output_second), BF)
    grad_first = first_home.reshape(seqs, block, local).astype(F32)
    qk_full = settled(qk_shard, qk_more).T
    output, grad_first, grad_w_down, qk_full, out_more = tie(output, grad_first, grad_w_down, qk_full, out_more)
    out_full = settled(out_shard, out_more)
    v_full = out_full[local:2 * local].T
    grad_w_qkv = jnp.stack([qk_full[:, :local], qk_full[:, local:], v_full], axis=1)
    grad_w_out = out_full[:local]

    share = gain_attn.shape[0]
    gain_grads = out_full[2 * local:2 * local + 2]
    for move in (core, across):
        gain_grads = gain_grads + move(gain_grads)
    mixed = out_full[2 * local + 2:2 * local + 3]
    if not pair:
        mixed = lax.all_gather(mixed, "fsdp", axis=1, tiled=True)
    mixed = mixed[:, :local]
    grad_mix = jnp.sum(mixed.reshape(mix.shape[0], -1), axis=1)
    return (
        output, grad_tokens, grad_first, grad_w_qkv, grad_w_out, grad_w_gate, grad_w_up, grad_w_down,
        gain_grads[0, :share], gain_grads[1, :share], grad_mix,
    )


def solution(mesh):
    rows = P("fsdp", "ctx", None)
    in_specs = (
        rows, P("fsdp", "ctx", "tp"), rows, P("fsdp", None, "tp"), P("tp", "fsdp"), P("fsdp", "tp"),
        P("fsdp", "tp"), P("tp", "fsdp"), P("fsdp"), P("fsdp"), P("tp"),
    )
    out_specs = (
        rows, rows, P("fsdp", "ctx", "tp"), P("fsdp", None, "tp"), P("tp", "fsdp"), P("fsdp", "tp"),
        P("fsdp", "tp"), P("tp", "fsdp"), P("fsdp"), P("fsdp"), P("tp"),
    )
    sizes = [mesh.shape[name] for name in ("fsdp", "ctx", "tp")]
    return jax.shard_map(
        functools.partial(on_device, *sizes), mesh=mesh, in_specs=in_specs, out_specs=out_specs,
        check_vma=False,
    )
```

```python
import functools

import jax
import jax.numpy as jnp
from jax import lax
from jax.experimental import pallas as pl
from jax.experimental.pallas import tpu as pltpu
from jax.sharding import PartitionSpec as P

EPSILON = 1e-06
SCALE = 0.125
BF = jnp.bfloat16
F32 = jnp.float32
NN = (((1,), (0,)), ((), ()))
NT = (((1,), (1,)), ((), ()))
TN = (((0,), (0,)), ((), ()))


def dot(a, b, dims=NN):
    return lax.dot_general(a, b, dims, preferred_element_type=F32)


def away(item):
    return pltpu.HBM(item.shape, item.dtype)


def full(shape):
    return pl.BlockSpec(shape, lambda *_: (0,) * len(shape))


def call(kernel, out_shapes, *args, grid=None, in_specs=None, out_specs=None, scratch=(), us=0, name=None, vmem=16):
    keywords = {}
    if grid is not None:
        keywords = dict(grid=grid, in_specs=in_specs, out_specs=out_specs)
    elif in_specs is not None:
        keywords = dict(in_specs=in_specs)
    return pl.pallas_call(
        kernel,
        out_shape=out_shapes,
        scratch_shapes=list(scratch),
        cost_estimate=pl.CostEstimate(flops=int(us * 1e9), bytes_accessed=int(us * 3.4e6), transcendentals=0),
        compiler_params=pltpu.CompilerParams(vmem_limit_bytes=vmem << 20),
        name=name,
        **keywords,
    )(*args)


def shape_of(dims, dtype):
    return jax.ShapeDtypeStruct(dims, dtype)


def own_kernel(count, place, source, *refs):
    outs, sems = refs[:count], refs[count]
    half = outs[0].shape[2] // 2
    copies = []
    for p, out in enumerate(outs):
        for h in range(2):
            copies.append(
                pltpu.make_async_copy(
                    source.at[:, place[p], :, pl.ds(pl.multiple_of(place[2 + h] * half, half), half)],
                    out.at[:, :, h * half:(h + 1) * half],
                    sems.at[len(copies)],
                )
            )
    for copy in copies:
        copy.start()
    for copy in copies:
        copy.wait()


def half_swap(values, lane):
    width = values.shape[-1]
    ahead = pltpu.roll(values, width - 32, 1)
    behind = pltpu.roll(values, 32, 1)
    return jnp.where(lane % 64 < 32, ahead, behind)


def signed_tables(cos_ref, sin_ref, index, width, lane):
    cosine = jnp.concatenate([cos_ref[index]] * (width // 128), axis=1)
    sine = jnp.concatenate([sin_ref[index]] * (width // 128), axis=1)
    return cosine, jnp.where(lane % 64 < 32, -sine, sine)


def attend_kernel(
    seg, p0, p1, p2, p3, gain, wa, wb, fv, cos, sin, mix, woa, wob,
    na_o, nb_o, q, k, v, diff_o, att_o, lse_o, keep_o, pass_o, send_o,
    v_t, o_t,
):
    blocks, rows, width = q.shape
    heads = width // 64
    half = wa.shape[1]
    lane_full = lax.broadcasted_iota(jnp.int32, (1, width), 1)
    for b in range(blocks):
        x = jnp.concatenate([p0[b], p1[b], p2[b], p3[b]], axis=0).astype(F32)
        inverse = lax.rsqrt(jnp.mean(x * x, axis=-1, keepdims=True) + EPSILON)
        normed = (x * inverse * gain[...]).astype(BF)
        na, nb = normed[:, :half], normed[:, half:]
        na_o[b] = na
        nb_o[b] = nb
        cosine, sine = signed_tables(cos, sin, b, width, lane_full)
        raw = [dot(na, wa[i]) + dot(nb, wb[i]) for i in range(3)]
        q[b] = (raw[0] * cosine + half_swap(raw[0], lane_full) * sine).astype(BF)
        k[b] = (raw[1] * cosine + half_swap(raw[1], lane_full) * sine).astype(BF)
        first = jnp.concatenate([fv[b, seg[r]] for r in range(4)], axis=0).astype(F32)
        value = mix[...] * raw[2] + (1.0 - mix[...]) * first
        v[b] = value.astype(BF)
        v_t[:, b * rows:(b + 1) * rows] = value.T.astype(BF)
        diff_o[b] = raw[2] - first
    lane = lax.broadcasted_iota(jnp.int32, (1, width), 1) // 64

    def head(h, carry):
        own = lane == h
        for qb in range(blocks):
            qm = jnp.where(own, q[qb], jnp.zeros_like(q[qb]))
            scores = [dot(k[kb], qm, NT) * SCALE for kb in range(qb + 1)]
            top = functools.reduce(jnp.maximum, [jnp.max(s, axis=0, keepdims=True) for s in scores])
            total = jnp.zeros((1, rows), F32)
            out = jnp.zeros((64, rows), F32)
            for kb in range(qb + 1):
                e = jnp.exp(scores[kb] - top)
                total = total + jnp.sum(e, axis=0, keepdims=True)
                out = out + dot(v_t[pl.ds(pl.multiple_of(h * 64, 64), 64), kb * rows:(kb + 1) * rows], e.astype(BF))
            o_t[qb, pl.ds(pl.multiple_of(h * 64, 64), 64), :] = out / total
            lse_o[h, qb:qb + 1, :] = top + jnp.log(total)
        return carry

    lax.fori_loop(0, heads, head, 0)
    quarter = rows // 4
    for qb in range(blocks):
        att = o_t[qb].T.astype(BF)
        att_o[qb] = att
        for lo, w in ((0, woa), (half, wob)):
            part = dot(att, w[...])
            for p, out in enumerate((keep_o, pass_o)):
                out[qb, :, lo:lo + half] = part[p * quarter:(p + 1) * quarter]
            for p in range(2):
                send_o[p, qb, :, lo:lo + half] = part[(2 + p) * quarter:(3 + p) * quarter].astype(BF)


def residual_kernel(x, keep, got_core, got_x, gain, residual_o, normed_o):
    residual = (
        x[0].astype(F32) + keep[0] + got_core[0, 0].astype(F32) + got_x[0].astype(F32)
    )
    inverse = lax.rsqrt(jnp.mean(residual * residual, axis=-1, keepdims=True) + EPSILON)
    residual_o[0] = residual
    normed_o[0] = (residual * inverse * gain[...]).astype(BF)


def mlp_kernel(
    n0, n1, n2, n3, g0, g1, g2, g3, ga, gb, ua, ub, da, la, db, lb,
    na_o, nb_o, la_o, lb_o, hidden_o, dgate_o, dup_o, keep_o, pass_o, send_o,
):
    n = jnp.concatenate([n0[0], n1[0], n2[0], n3[0]], axis=0)
    g = jnp.concatenate([g0[0], g1[0], g2[0], g3[0]], axis=0)
    half = ga.shape[1]
    na, nb = n[:, :half], n[:, half:]
    na_o[0] = na
    nb_o[0] = nb
    la_o[0] = g[:, :half]
    lb_o[0] = g[:, half:]
    gate = dot(na, ga[...], NT) + dot(nb, gb[...], NT)
    up = dot(na, ua[...], NT) + dot(nb, ub[...], NT)
    wa = jnp.concatenate([da[...], la[...]], axis=0)
    wb = jnp.concatenate([db[...], lb[...]], axis=0)
    grad_hidden = dot(g[:, :half], wa, NT) + dot(g[:, half:], wb, NT)
    s = jax.nn.sigmoid(gate)
    active = gate * s
    hidden_o[0] = (active * up).astype(BF)
    dgate = (grad_hidden * up * s * (1.0 + gate * (1.0 - s))).astype(BF)
    dup = (grad_hidden * active).astype(BF)
    dgate_o[0] = dgate
    dup_o[0] = dup
    quarter = n.shape[0] // 4
    for lo, wg, wu in ((0, ga, ua), (half, gb, ub)):
        part = dot(dgate, wg[...]) + dot(dup, wu[...])
        for p, out in enumerate((keep_o, pass_o)):
            out[0, :, lo:lo + half] = part[p * quarter:(p + 1) * quarter]
        for p in range(2):
            send_o[p, 0, :, lo:lo + half] = part[(2 + p) * quarter:(3 + p) * quarter].astype(BF)


def down_kernel(hidden, da, la, db, lb, keep_o, pass_o, send_o):
    half = da.shape[1]
    quarter = hidden.shape[1] // 4
    for lo, w, late in ((0, da, la), (half, db, lb)):
        part = dot(hidden[0], jnp.concatenate([w[...], late[...]], axis=0))
        for p, out in enumerate((keep_o, pass_o)):
            out[0, :, lo:lo + half] = part[p * quarter:(p + 1) * quarter]
        for p in range(2):
            send_o[p, 0, :, lo:lo + half] = part[(2 + p) * quarter:(3 + p) * quarter].astype(BF)


def norm_back_kernel(direct, keep, got_core, got_x, values, gain, grad_o, low_o, gain_o):
    @pl.when(pl.program_id(0) == 0)
    def _():
        gain_o[...] = jnp.zeros_like(gain_o)

    grad = keep[0] + got_core[0, 0].astype(F32) + got_x[0].astype(F32)
    x = values[0].astype(F32)
    inverse = lax.rsqrt(jnp.mean(x * x, axis=-1, keepdims=True) + EPSILON)
    weighted = grad * gain[...]
    gain_o[...] += jnp.sum(grad * x * inverse, axis=0, keepdims=True)
    out = direct[0].astype(F32) + (
        inverse * weighted
        - x * (inverse * inverse * inverse) * jnp.mean(weighted * x, axis=-1, keepdims=True)
    )
    grad_o[0] = out
    low_o[0] = out.astype(BF)


def attend_back_kernel(
    seg, b0, b1, b2, b3, woa, wob, q, k, v, att, lse, cos, sin, mix, diff,
    p0, p1, p2, p3, wa, wb, na, nb, gain_in,
    gf_o, keep_o, pass_o, send_o, own_o, other_o, own2_o, other2_o,
    gat, dmat, k_t, dk, dv, dq_t, og, og2,
):
    blocks, rows, width = q.shape
    heads = width // 64
    half = woa.shape[1]
    lane_full = lax.broadcasted_iota(jnp.int32, (1, width), 1)
    lane = lane_full // 64
    pick = (
        lax.broadcasted_iota(jnp.int32, (8, width), 0)
        == lax.broadcasted_iota(jnp.int32, (8, width), 1) // 64
    ).astype(F32)
    og[...] = jnp.zeros_like(og)
    og2[...] = jnp.zeros_like(og2)
    for b in range(blocks):
        g = jnp.concatenate([b0[b], b1[b], b2[b], b3[b]], axis=0)
        og[:width] += dot(att[b], g, TN)
        ga = (dot(g[:, :half], woa[...], NT) + dot(g[:, half:], wob[...], NT)).astype(BF)
        gat[b] = ga
        prod = ga.astype(F32) * att[b].astype(F32)
        dmat[b] = lax.dot_general(pick, prod, NT, precision=lax.Precision.HIGHEST, preferred_element_type=F32)
        k_t[:, b * rows:(b + 1) * rows] = k[b].astype(F32).T.astype(BF)
    dk[...] = jnp.zeros_like(dk)
    dv[...] = jnp.zeros_like(dv)

    def head(h, carry):
        own = lane == h
        for qb in range(blocks):
            qm = jnp.where(own, q[qb], jnp.zeros_like(q[qb]))
            gm = jnp.where(own, gat[qb], jnp.zeros_like(gat[qb]))
            log_total = lse[h, qb:qb + 1, :]
            row_dot = dmat[qb, pl.ds(h, 1), :]
            acc = jnp.zeros((64, rows), F32)
            for kb in range(qb + 1):
                prob = jnp.exp(dot(k[kb], qm, NT) * SCALE - log_total)
                dprob = dot(v[kb], gm, NT)
                ds = (prob * (dprob - row_dot)).astype(BF)
                dv[kb] += dot(prob.astype(BF), gm)
                dk[kb] += dot(ds, qm)
                acc = acc + dot(k_t[pl.ds(pl.multiple_of(h * 64, 64), 64), kb * rows:(kb + 1) * rows], ds)
            dq_t[qb, pl.ds(pl.multiple_of(h * 64, 64), 64), :] = acc
        return carry

    lax.fori_loop(0, heads, head, 0)
    quarter = rows // 4
    total = jnp.zeros((1, width), F32)
    gains = [jnp.zeros((1, half), F32) for _ in range(2)]
    for b in range(blocks):
        cosine, sine = signed_tables(cos, sin, b, width, lane_full)
        gq = dq_t[b].T * SCALE
        gk = dk[b] * SCALE
        gv = dv[b]
        grads = [
            (gq * cosine - half_swap(gq, lane_full) * sine).astype(BF),
            (gk * cosine - half_swap(gk, lane_full) * sine).astype(BF),
            (mix[...] * gv).astype(BF),
        ]
        for i, n in enumerate((na, nb)):
            lanes = slice(i * half, (i + 1) * half)
            og2[:width, lanes] += dot(grads[0], n[b], TN)
            og2[width:, lanes] += dot(grads[1], n[b], TN)
            og[width:, lanes] += dot(grads[2], n[b], TN)
        x = jnp.concatenate([p0[b], p1[b], p2[b], p3[b]], axis=0).astype(F32)
        x = x * lax.rsqrt(jnp.mean(x * x, axis=-1, keepdims=True) + EPSILON)
        for i, w in enumerate((wa, wb)):
            lanes = slice(i * half, (i + 1) * half)
            part = sum(dot(grad, w[j], NT) for j, grad in enumerate(grads))
            gains[i] = gains[i] + jnp.sum(part * x[:, lanes], axis=0, keepdims=True)
            for p, out in enumerate((keep_o, pass_o)):
                out[b, :, lanes] = part[p * quarter:(p + 1) * quarter]
            for p in range(2):
                send_o[p, b, :, lanes] = part[(2 + p) * quarter:(3 + p) * quarter].astype(BF)
        gf = ((1.0 - mix[...]) * gv).astype(BF)
        for r in range(4):
            gf_o[b, seg[r]] = gf[r * quarter:(r + 1) * quarter]
        total = total + jnp.sum(gv * diff[b], axis=0, keepdims=True)
    row = lax.broadcasted_iota(jnp.int32, (16, half), 0)
    mixed = jnp.concatenate([total, jnp.zeros((1, half - width), F32)], axis=1)
    for i, (out, out2) in enumerate(((own_o, own2_o), (other_o, other2_o))):
        lanes = slice(i * half, (i + 1) * half)
        extra = jnp.where(row == 0, gains[i], jnp.where(row == 1, gain_in[:, lanes], jnp.where(row == 2, mixed, 0.0)))
        out[:2 * width] = og[:, lanes].astype(out.dtype)
        out[2 * width:] = extra.astype(out.dtype)
        out2[...] = og2[:, lanes].astype(out.dtype)


def place_kernel(where, roll, *refs):
    pieces, out = refs[:-1], refs[-1]
    width = out.shape[-1]
    half = width // 2
    for r, piece in enumerate(pieces):
        value = piece[0]
        low, high = value[:, :half], value[:, half:]
        swap = roll[0] == 1
        out[0, where[r], :, :half] = jnp.where(swap, high, low).astype(out.dtype)
        out[0, where[r], :, half:] = jnp.where(swap, low, high).astype(out.dtype)


def first_kernel(got, out):
    out[...] = got[...].astype(out.dtype)


def on_device(
    fsdp, ctx, tp,
    tokens, first_values, out_grad, w_qkv, output_weight, w_gate, w_up, w_down, gain_attn, gain_mlp, mix,
):
    seqs, block, width = tokens.shape
    local = w_qkv.shape[2]
    hidden_width = w_gate.shape[1]
    quarter = block // tp
    half = width // 2
    pair = fsdp == 2
    assert seqs == ctx and ctx == 4 and tp == 4 and local <= half
    y = lax.axis_index("fsdp")
    z = lax.axis_index("ctx")
    t = lax.axis_index("tp")
    swap_y = [(0, 1), (1, 0)]
    by_core = [(i, i ^ 1) for i in range(tp)]
    by_x = [(i, i ^ 2) for i in range(tp)]

    def tie(*values):
        return lax.optimization_barrier(values)

    def core(value):
        return lax.ppermute(value, "tp", by_core)

    def across(value):
        return lax.ppermute(value, "tp", by_x)

    def other_half(value, axis):
        if pair:
            return value, lax.ppermute(value, "fsdp", swap_y)
        whole = lax.all_gather(value, "fsdp", axis=axis, tiled=True)
        return tuple(lax.slice_in_dim(whole, i * half, (i + 1) * half, axis=axis) for i in range(2))

    def added(keep, got):
        return keep + got.astype(F32)

    rows = ctx * block
    smem = pl.BlockSpec(memory_space=pltpu.SMEM)
    piece_spec = pl.BlockSpec((1, quarter, width), lambda b: (b, 0, 0))
    block_local = pl.BlockSpec((1, block, local), lambda b: (b, 0, 0))
    block_half = pl.BlockSpec((1, block, half), lambda b: (b, 0, 0))
    block_hidden = pl.BlockSpec((1, block, hidden_width), lambda b: (b, 0, 0))
    block_table = pl.BlockSpec((1, block, 128), lambda b: (b, 0, 0))
    part_specs = [piece_spec] * 2 + [pl.BlockSpec((2, 1, quarter, width), lambda b: (0, b, 0, 0))]
    first_part = pl.BlockSpec((1, 1, quarter, width), lambda b: (0, b, 0, 0))
    gain_spec = full((1, width))
    send_shape = shape_of((2, ctx, quarter, width), BF)
    own_f32 = shape_of((ctx, quarter, width), F32)
    own_low = shape_of((ctx, quarter, width), BF)
    part_shapes = [own_f32, own_f32, send_shape]
    part_away = [away(own_f32), own_f32, send_shape]
    rows_local = shape_of((ctx, block, local), BF)
    rows_half = shape_of((ctx, block, half), BF)
    rows_hidden = shape_of((ctx, block, hidden_width), BF)
    gain_row = shape_of((1, width), F32)

    seg = jnp.stack([t, t ^ 2, t ^ 1, t ^ 3]).astype(jnp.int32)
    turn = y if pair else y * 0
    roll = jnp.reshape(turn, (1,)).astype(jnp.int32)
    where = jnp.stack([t, t ^ 2, turn, 1 - turn]).astype(jnp.int32)

    def own_rows(value, count):
        return call(
            functools.partial(own_kernel, count),
            [own_low] * count,
            where, value.reshape(seqs, tp, quarter, width),
            in_specs=[smem, pl.BlockSpec(memory_space=pltpu.HBM)],
            scratch=[pltpu.SemaphoreType.DMA((2 * count,))],
            name="own", vmem=4,
        )

    (x_part,) = own_rows(tokens, 1)
    place = (seg[:, None] * quarter + jnp.arange(quarter)[None, :]).reshape(block)
    positions = (jnp.arange(ctx)[:, None] * block + place[None, :]).astype(F32)
    lanes = (jnp.arange(128) % 32).astype(F32)
    table = positions[:, :, None] * (10000.0 ** (-lanes / 32.0))[None, None, :]
    cosine, sine = jnp.cos(table), jnp.sin(table)
    mix_row = jnp.repeat(mix, local // mix.shape[0])[None, :]

    qkv_a, qkv_b = other_half(jnp.transpose(w_qkv, (1, 0, 2)), 1)
    out_a, out_b = other_half(
        jnp.concatenate([output_weight, jnp.stack([gain_attn, gain_mlp])], axis=0), 1
    )
    gate_a, gate_b = other_half(w_gate.T, 1)
    up_a, up_b = other_half(w_up.T, 1)
    early = hidden_width // 4 // 64 * 64
    down_a, down_b = other_half(w_down[:early], 1)
    late_a, late_b = other_half(w_down[early:], 1)

    x_own = lax.all_to_all(x_part, "ctx", 0, 0)
    x_second = across(x_own)
    x_own, qkv_b, cosine, sine, mix_row, g_part, g_late = tie(
        x_own, qkv_b, cosine, sine, mix_row, *own_rows(out_grad, 2)
    )
    fv = lax.all_to_all(first_values, "ctx", 0, 0).reshape(ctx, tp, quarter, local)
    gains = jnp.concatenate([out_a[local:], out_b[local:]], axis=1).astype(F32)
    x_core = core(x_own)
    x_second, out_b, gains = tie(x_second, out_b[:local], gains)
    x_both = core(x_second)
    x_core, x_both, fv, g_part = tie(x_core, x_both, fv, g_part)
    x_pieces = (x_own, x_second, x_core, x_both)
    out_a = output_weight if pair else out_a[:local]
    gain_first, gain_second = gains[0:1], gains[1:2]
    g_first = lax.all_to_all(g_part, "ctx", 0, 0)
    norm_a, norm_b, queries, keys, values, diff, attended, log_total, keep, onward, send = call(
        attend_kernel,
        [away(item) for item in [rows_half] * 2 + [rows_local] * 3 + [
            shape_of((ctx, block, local), F32), rows_local,
        ]] + [shape_of((mix.shape[0], ctx, block), F32)] + part_away,
        seg, *x_pieces, gain_first, qkv_a, qkv_b, fv, cosine, sine, mix_row, out_a, out_b,
        in_specs=[smem] + [pl.BlockSpec(memory_space=pltpu.VMEM)] * 13,
        scratch=[pltpu.VMEM((local, rows), BF), pltpu.VMEM((ctx, local, block), F32)],
        name="attend", vmem=20,
    )
    send, gate_b, g_first, g_late = tie(send, gate_b, g_first, g_late)
    got_core = core(send)
    got_x = across(added(onward, got_core[1]).astype(BF))
    g_second = lax.all_to_all(g_late, "ctx", 0, 0)
    got_x, up_b, down_b, g_second = tie(got_x, up_b, down_b, g_second)
    residual, normed_own = call(
        residual_kernel,
        [own_f32, own_low],
        x_own, keep, got_core, got_x, gain_second,
        grid=(ctx,),
        in_specs=[piece_spec, piece_spec, first_part, piece_spec, gain_spec],
        out_specs=[piece_spec, piece_spec],
        name="residual_norm", vmem=6, us=20,
    )
    down_specs = [full((n, half)) for n in (early, hidden_width - early)] * 2
    n_second = across(normed_own)
    mlp_a, mlp_b, last_a, last_b, hidden, grad_gate, grad_up, keep, onward, send = call(
        mlp_kernel,
        [rows_half] * 4 + [rows_hidden] * 3 + part_shapes,
        normed_own, n_second, core(normed_own), core(n_second), g_first, g_second, core(g_first), core(g_second),
        gate_a, gate_b, up_a, up_b, down_a, late_a, down_b, late_b,
        grid=(ctx,),
        in_specs=[piece_spec] * 8 + [full((hidden_width, half))] * 4 + down_specs,
        out_specs=[block_half] * 4 + [block_hidden] * 3 + part_specs,
        name="mlp", vmem=24, us=10,
    )

    def placed(*pieces):
        *pieces, dtype = pieces
        return call(
            place_kernel,
            [shape_of((seqs, tp, quarter, width), dtype)],
            seg, roll, *pieces,
            grid=(seqs,),
            in_specs=[smem, smem] + [piece_spec] * 4,
            out_specs=[pl.BlockSpec((1, tp, quarter, width), lambda b: (b, 0, 0, 0))],
            name="place", vmem=6,
        )[0].reshape(seqs, block, width)

    def weight_grad(left, right):
        return lax.dot_general(
            left.reshape(rows, -1), right.reshape(rows, -1), TN, preferred_element_type=F32
        )

    def exchange(first, second, axis=1):
        if pair:
            return lax.ppermute(second, "fsdp", swap_y)
        return lax.psum_scatter(
            jnp.concatenate([first.astype(BF), second], axis=axis), "fsdp", scatter_dimension=axis, tiled=True
        )

    def joined(first, received):
        return (first + received.astype(F32)).astype(BF) if pair else received

    def plus(shard, received):
        return (shard.astype(F32) + received.astype(F32)).astype(BF)

    def toward(shard):
        return lax.ppermute(shard, "ctx", [(0, 1), (3, 2)])

    def meet(shard):
        return lax.ppermute(shard, "ctx", [(1, 2), (2, 1)])

    def back(shard):
        return lax.ppermute(shard, "ctx", [(1, 0), (2, 3)])

    def settled(shard, received):
        return jnp.where((z == 0) | (z == 3), received, shard).astype(F32)

    got_core = core(send)
    gate_first = weight_grad(grad_gate, mlp_a)
    gate_second = weight_grad(grad_gate, mlp_b).astype(BF)
    onward = added(onward, got_core[1]).astype(BF)

    onward, gate_first, gate_second, grad_up, hidden = tie(onward, gate_first, gate_second, grad_up, hidden)
    got_x = across(onward)
    gate_got = exchange(gate_first, gate_second)
    up_first = weight_grad(grad_up, mlp_a)
    up_second = weight_grad(grad_up, mlp_b).astype(BF)
    down_first = weight_grad(hidden, last_a)
    down_second = weight_grad(hidden, last_b).astype(BF)
    down_keep, down_onward, down_send = call(
        down_kernel,
        part_shapes,
        hidden, down_a, late_a, down_b, late_b,
        grid=(ctx,),
        in_specs=[block_hidden] + down_specs,
        out_specs=part_specs,
        name="down", vmem=12,
    )
    down_core = core(down_send)
    down_onward = added(down_onward, down_core[1]).astype(BF)
    grad_residual, branch_own, gain_sum_second = call(
        norm_back_kernel,
        [own_f32, own_low, gain_row],
        g_first, keep, got_core, got_x, residual, gain_second,
        grid=(ctx,),
        in_specs=[piece_spec, piece_spec, first_part, piece_spec, piece_spec, gain_spec],
        out_specs=[piece_spec, piece_spec, gain_spec],
        name="norm_back_mlp", vmem=6, us=20,
    )
    (
        branch_own, grad_residual, gate_got, gate_first, up_first, up_second, down_first, down_second,
        down_onward,
    ) = tie(
        branch_own, grad_residual, gate_got, gate_first, up_first, up_second, down_first, down_second,
        down_onward,
    )

    b_second = across(branch_own)
    b_core = core(branch_own)
    b_both = core(b_second)
    up_got = exchange(up_first, up_second)
    gate_shard = joined(gate_first, gate_got)
    gate_more = toward(gate_shard)
    (
        b_second, b_core, b_both, up_got, gate_shard, gate_more, down_onward, down_second,
    ) = tie(b_second, b_core, b_both, up_got, gate_shard, gate_more, down_onward, down_second)

    down_x = across(down_onward)
    down_got = exchange(down_first, down_second)
    gate_shard = plus(gate_shard, gate_more)
    gate_more = meet(gate_shard)
    up_shard = joined(up_first, up_got)
    up_more = toward(up_shard)
    payload = [shape_of((2 * local + n, half), kind) for n in (16, 0) for kind in (F32, BF)]
    gf, keep, onward, send, out_first, out_second, qk_first, qk_second = call(
        attend_back_kernel,
        [away(shape_of((ctx, tp, quarter, local), BF)), *part_away, *[away(item) for item in payload]],
        seg, branch_own, b_second, b_core, b_both, out_a, out_b,
        queries, keys, values, attended, log_total, cosine, sine, mix_row, diff,
        *x_pieces, qkv_a, qkv_b, norm_a, norm_b, gain_sum_second,
        in_specs=[smem] + [pl.BlockSpec(memory_space=pltpu.VMEM)] * 24,
        scratch=[
            pltpu.VMEM((ctx, block, local), BF),
            pltpu.VMEM((ctx, 8, block), F32),
            pltpu.VMEM((local, rows), BF),
            pltpu.VMEM((ctx, block, local), F32),
            pltpu.VMEM((ctx, block, local), F32),
            pltpu.VMEM((ctx, local, block), F32),
            pltpu.VMEM((2 * local, width), F32),
            pltpu.VMEM((2 * local, width), F32),
        ],
        name="attend_back", vmem=40, us=30,
    )
    send, down_got, gate_more, up_more, down_x = tie(send, down_got, gate_more, up_more, down_x)
    got_core = core(send)
    onward = added(onward, got_core[1]).astype(BF)
    gate_shard = plus(gate_shard, gate_more)
    up_shard = plus(up_shard, up_more)
    down_shard = joined(down_first, down_got)
    onward, qk_second, out_second, gate_shard, up_shard, down_shard, down_x = tie(
        onward, qk_second, out_second, gate_shard, up_shard, down_shard, down_x
    )

    got_x = across(onward)
    gate_more = back(gate_shard)
    up_more = meet(up_shard)
    down_more = toward(down_shard)
    qk_got = exchange(qk_first, qk_second)
    output_own = (residual + added(down_keep, down_core[0]) + down_x.astype(F32)).astype(BF)
    _, tokens_own, _ = call(
        norm_back_kernel,
        [own_f32, own_low, gain_row],
        grad_residual, keep, got_core, got_x, x_own, gain_first,
        grid=(ctx,),
        in_specs=[piece_spec, piece_spec, first_part, piece_spec, piece_spec, gain_spec],
        out_specs=[piece_spec, piece_spec, gain_spec],
        name="norm_back_attn", vmem=6, us=20,
    )
    tokens_own, output_own, gf, out_second, gate_shard, up_shard, down_shard = tie(
        tokens_own, output_own, gf, out_second, gate_shard, up_shard, down_shard
    )

    tokens_home = lax.all_to_all(tokens_own, "ctx", 0, 0)
    out_got = exchange(out_first, out_second)
    grad_w_gate = settled(gate_shard, gate_more).T
    up_shard = plus(up_shard, up_more)
    down_shard = plus(down_shard, down_more)
    qk_shard = joined(qk_first, qk_got)
    tokens_home, output_own, gf, grad_w_gate, up_shard, down_shard, qk_shard = tie(
        tokens_home, output_own, gf, grad_w_gate, up_shard, down_shard, qk_shard
    )
    tokens_second = across(tokens_home)
    tokens_core = core(tokens_home)
    up_more = back(up_shard)
    down_more = meet(down_shard)
    qk_more = toward(qk_shard)
    out_shard = joined(out_first, out_got)
    out_more = toward(out_shard)
    tokens_second, output_own, gf, up_more, down_more, qk_more = tie(
        tokens_second, output_own, gf, up_more, down_more, qk_more
    )
    output_home = lax.all_to_all(output_own, "ctx", 0, 0)
    down_shard = plus(down_shard, down_more)
    down_more = back(down_shard)
    qk_shard = plus(qk_shard, qk_more)
    qk_more = meet(qk_shard)
    grad_tokens = placed(tokens_home, tokens_second, tokens_core, core(tokens_second), F32)
    grad_w_up = settled(up_shard, up_more).T
    output_home, gf, grad_tokens, grad_w_up, out_more = tie(output_home, gf, grad_tokens, grad_w_up, out_more)
    output_second = across(output_home)
    output_core = core(output_home)
    first_home = lax.all_to_all(gf, "ctx", 0, 0)
    qk_shard = plus(qk_shard, qk_more)
    qk_more = back(qk_shard)
    out_shard = plus(out_shard, out_more)
    out_more = meet(out_shard)
    grad_w_down = settled(down_shard, down_more)
    out_shard = plus(out_shard, out_more)
    out_more = back(out_shard)
    output = placed(output_home, output_second, output_core, core(output_second), BF)
    grad_first = first_home.reshape(seqs, block, local).astype(F32)
    qk_full = settled(qk_shard, qk_more).T
    output, grad_first, grad_w_down, qk_full, out_more = tie(output, grad_first, grad_w_down, qk_full, out_more)
    out_full = settled(out_shard, out_more)
    v_full = out_full[local:2 * local].T
    grad_w_qkv = jnp.stack([qk_full[:, :local], qk_full[:, local:], v_full], axis=1)
    grad_w_out = out_full[:local]

    share = gain_attn.shape[0]
    gain_grads = out_full[2 * local:2 * local + 2]
    for move in (core, across):
        gain_grads = gain_grads + move(gain_grads)
    mixed = out_full[2 * local + 2:2 * local + 3]
    if not pair:
        mixed = lax.all_gather(mixed, "fsdp", axis=1, tiled=True)
    mixed = mixed[:, :local]
    grad_mix = jnp.sum(mixed.reshape(mix.shape[0], -1), axis=1)
    return (
        output, grad_tokens, grad_first, grad_w_qkv, grad_w_out, grad_w_gate, grad_w_up, grad_w_down,
        gain_grads[0, :share], gain_grads[1, :share], grad_mix,
    )


def solution(mesh):
    rows = P("fsdp", "ctx", None)
    in_specs = (
        rows, P("fsdp", "ctx", "tp"), rows, P("fsdp", None, "tp"), P("tp", "fsdp"), P("fsdp", "tp"),
        P("fsdp", "tp"), P("tp", "fsdp"), P("fsdp"), P("fsdp"), P("tp"),
    )
    out_specs = (
        rows, rows, P("fsdp", "ctx", "tp"), P("fsdp", None, "tp"), P("tp", "fsdp"), P("fsdp", "tp"),
        P("fsdp", "tp"), P("tp", "fsdp"), P("fsdp"), P("fsdp"), P("tp"),
    )
    sizes = [mesh.shape[name] for name in ("fsdp", "ctx", "tp")]
    return jax.shard_map(
        functools.partial(on_device, *sizes), mesh=mesh, in_specs=in_specs, out_specs=out_specs,
        check_vma=False,
    )
```

```python
import functools

import jax
import jax.numpy as jnp
from jax import lax
from jax.experimental import pallas as pl
from jax.experimental.pallas import tpu as pltpu
from jax.sharding import PartitionSpec as P

EPSILON = 1e-06
SCALE = 0.125
BF = jnp.bfloat16
F32 = jnp.float32
NN = (((1,), (0,)), ((), ()))
NT = (((1,), (1,)), ((), ()))
TN = (((0,), (0,)), ((), ()))


def dot(a, b, dims=NN):
    return lax.dot_general(a, b, dims, preferred_element_type=F32)


def away(item):
    return pltpu.HBM(item.shape, item.dtype)


def full(shape):
    return pl.BlockSpec(shape, lambda *_: (0,) * len(shape))


def call(kernel, out_shapes, *args, grid=None, in_specs=None, out_specs=None, scratch=(), us=0, name=None, vmem=16):
    keywords = {}
    if grid is not None:
        keywords = dict(grid=grid, in_specs=in_specs, out_specs=out_specs)
    elif in_specs is not None:
        keywords = dict(in_specs=in_specs)
    return pl.pallas_call(
        kernel,
        out_shape=out_shapes,
        scratch_shapes=list(scratch),
        cost_estimate=pl.CostEstimate(flops=int(us * 1e9), bytes_accessed=int(us * 3.4e6), transcendentals=0),
        compiler_params=pltpu.CompilerParams(vmem_limit_bytes=vmem << 20),
        name=name,
        **keywords,
    )(*args)


def shape_of(dims, dtype):
    return jax.ShapeDtypeStruct(dims, dtype)


def own_kernel(count, place, source, *refs):
    outs, sems = refs[:count], refs[count]
    half = outs[0].shape[2] // 2
    copies = []
    for p, out in enumerate(outs):
        for h in range(2):
            copies.append(
                pltpu.make_async_copy(
                    source.at[:, place[p], :, pl.ds(pl.multiple_of(place[2 + h] * half, half), half)],
                    out.at[:, :, h * half:(h + 1) * half],
                    sems.at[len(copies)],
                )
            )
    for copy in copies:
        copy.start()
    for copy in copies:
        copy.wait()


def half_swap(values, lane):
    width = values.shape[-1]
    ahead = pltpu.roll(values, width - 32, 1)
    behind = pltpu.roll(values, 32, 1)
    return jnp.where(lane % 64 < 32, ahead, behind)


def signed_tables(cos_ref, sin_ref, index, width, lane):
    cosine = jnp.concatenate([cos_ref[index]] * (width // 128), axis=1)
    sine = jnp.concatenate([sin_ref[index]] * (width // 128), axis=1)
    return cosine, jnp.where(lane % 64 < 32, -sine, sine)


def attend_kernel(
    seg, p0, p1, p2, p3, gain, wa, wb, fv, cos, sin, mix, woa, wob,
    na_o, nb_o, q, k, v, diff_o, att_o, lse_o, keep_o, pass_o, send_o,
    v_t, o_t,
):
    blocks, rows, width = q.shape
    heads = width // 64
    half = wa.shape[1]
    lane_full = lax.broadcasted_iota(jnp.int32, (1, width), 1)
    for b in range(blocks):
        x = jnp.concatenate([p0[b], p1[b], p2[b], p3[b]], axis=0).astype(F32)
        inverse = lax.rsqrt(jnp.mean(x * x, axis=-1, keepdims=True) + EPSILON)
        normed = (x * inverse * gain[...]).astype(BF)
        na, nb = normed[:, :half], normed[:, half:]
        na_o[b] = na
        nb_o[b] = nb
        cosine, sine = signed_tables(cos, sin, b, width, lane_full)
        raw = [dot(na, wa[i]) + dot(nb, wb[i]) for i in range(3)]
        q[b] = (raw[0] * cosine + half_swap(raw[0], lane_full) * sine).astype(BF)
        k[b] = (raw[1] * cosine + half_swap(raw[1], lane_full) * sine).astype(BF)
        first = jnp.concatenate([fv[b, seg[r]] for r in range(4)], axis=0).astype(F32)
        value = mix[...] * raw[2] + (1.0 - mix[...]) * first
        v[b] = value.astype(BF)
        v_t[:, b * rows:(b + 1) * rows] = value.T.astype(BF)
        diff_o[b] = raw[2] - first
    lane = lax.broadcasted_iota(jnp.int32, (1, width), 1) // 64

    def head(h, carry):
        own = lane == h
        for qb in range(blocks):
            qm = jnp.where(own, q[qb], jnp.zeros_like(q[qb]))
            scores = [dot(k[kb], qm, NT) * SCALE for kb in range(qb + 1)]
            top = functools.reduce(jnp.maximum, [jnp.max(s, axis=0, keepdims=True) for s in scores])
            total = jnp.zeros((1, rows), F32)
            out = jnp.zeros((64, rows), F32)
            for kb in range(qb + 1):
                e = jnp.exp(scores[kb] - top)
                total = total + jnp.sum(e, axis=0, keepdims=True)
                out = out + dot(v_t[pl.ds(pl.multiple_of(h * 64, 64), 64), kb * rows:(kb + 1) * rows], e.astype(BF))
            o_t[qb, pl.ds(pl.multiple_of(h * 64, 64), 64), :] = out / total
            lse_o[h, qb:qb + 1, :] = top + jnp.log(total)
        return carry

    lax.fori_loop(0, heads, head, 0)
    quarter = rows // 4
    for qb in range(blocks):
        att = o_t[qb].T.astype(BF)
        att_o[qb] = att
        for lo, w in ((0, woa), (half, wob)):
            part = dot(att, w[...])
            for p, out in enumerate((keep_o, pass_o)):
                out[qb, :, lo:lo + half] = part[p * quarter:(p + 1) * quarter]
            for p in range(2):
                send_o[p, qb, :, lo:lo + half] = part[(2 + p) * quarter:(3 + p) * quarter].astype(BF)


def residual_kernel(x, keep, got_core, got_x, gain, residual_o, normed_o):
    residual = (
        x[0].astype(F32) + keep[0] + got_core[0, 0].astype(F32) + got_x[0].astype(F32)
    )
    inverse = lax.rsqrt(jnp.mean(residual * residual, axis=-1, keepdims=True) + EPSILON)
    residual_o[0] = residual
    normed_o[0] = (residual * inverse * gain[...]).astype(BF)


def mlp_kernel(
    n0, n1, n2, n3, g0, g1, g2, g3, ga, gb, ua, ub, da, la, db, lb,
    na_o, nb_o, la_o, lb_o, hidden_o, dgate_o, dup_o, keep_o, pass_o, send_o,
):
    n = jnp.concatenate([n0[0], n1[0], n2[0], n3[0]], axis=0)
    g = jnp.concatenate([g0[0], g1[0], g2[0], g3[0]], axis=0)
    half = ga.shape[1]
    na, nb = n[:, :half], n[:, half:]
    na_o[0] = na
    nb_o[0] = nb
    la_o[0] = g[:, :half]
    lb_o[0] = g[:, half:]
    gate = dot(na, ga[...], NT) + dot(nb, gb[...], NT)
    up = dot(na, ua[...], NT) + dot(nb, ub[...], NT)
    wa = jnp.concatenate([da[...], la[...]], axis=0)
    wb = jnp.concatenate([db[...], lb[...]], axis=0)
    grad_hidden = dot(g[:, :half], wa, NT) + dot(g[:, half:], wb, NT)
    s = jax.nn.sigmoid(gate)
    active = gate * s
    hidden_o[0] = (active * up).astype(BF)
    dgate = (grad_hidden * up * s * (1.0 + gate * (1.0 - s))).astype(BF)
    dup = (grad_hidden * active).astype(BF)
    dgate_o[0] = dgate
    dup_o[0] = dup
    quarter = n.shape[0] // 4
    for lo, wg, wu in ((0, ga, ua), (half, gb, ub)):
        part = dot(dgate, wg[...]) + dot(dup, wu[...])
        for p, out in enumerate((keep_o, pass_o)):
            out[0, :, lo:lo + half] = part[p * quarter:(p + 1) * quarter]
        for p in range(2):
            send_o[p, 0, :, lo:lo + half] = part[(2 + p) * quarter:(3 + p) * quarter].astype(BF)


def down_kernel(hidden, da, la, db, lb, keep_o, pass_o, send_o):
    half = da.shape[1]
    quarter = hidden.shape[1] // 4
    for lo, w, late in ((0, da, la), (half, db, lb)):
        part = dot(hidden[0], jnp.concatenate([w[...], late[...]], axis=0))
        for p, out in enumerate((keep_o, pass_o)):
            out[0, :, lo:lo + half] = part[p * quarter:(p + 1) * quarter]
        for p in range(2):
            send_o[p, 0, :, lo:lo + half] = part[(2 + p) * quarter:(3 + p) * quarter].astype(BF)


def norm_back_kernel(direct, keep, got_core, got_x, values, gain, grad_o, low_o, gain_o):
    @pl.when(pl.program_id(0) == 0)
    def _():
        gain_o[...] = jnp.zeros_like(gain_o)

    grad = keep[0] + got_core[0, 0].astype(F32) + got_x[0].astype(F32)
    x = values[0].astype(F32)
    inverse = lax.rsqrt(jnp.mean(x * x, axis=-1, keepdims=True) + EPSILON)
    weighted = grad * gain[...]
    gain_o[...] += jnp.sum(grad * x * inverse, axis=0, keepdims=True)
    out = direct[0].astype(F32) + (
        inverse * weighted
        - x * (inverse * inverse * inverse) * jnp.mean(weighted * x, axis=-1, keepdims=True)
    )
    grad_o[0] = out
    low_o[0] = out.astype(BF)


def attend_back_kernel(
    seg, b0, b1, b2, b3, woa, wob, q, k, v, att, lse, cos, sin, mix, diff,
    p0, p1, p2, p3, wa, wb, na, nb, gain_in,
    gf_o, keep_o, pass_o, send_o, own_o, other_o, own2_o, other2_o,
    gat, dmat, k_t, dk, dv, dq_t, og, og2,
):
    blocks, rows, width = q.shape
    heads = width // 64
    half = woa.shape[1]
    lane_full = lax.broadcasted_iota(jnp.int32, (1, width), 1)
    lane = lane_full // 64
    pick = (
        lax.broadcasted_iota(jnp.int32, (8, width), 0)
        == lax.broadcasted_iota(jnp.int32, (8, width), 1) // 64
    ).astype(F32)
    og[...] = jnp.zeros_like(og)
    og2[...] = jnp.zeros_like(og2)
    for b in range(blocks):
        g = jnp.concatenate([b0[b], b1[b], b2[b], b3[b]], axis=0)
        og[:width] += dot(att[b], g, TN)
        ga = (dot(g[:, :half], woa[...], NT) + dot(g[:, half:], wob[...], NT)).astype(BF)
        gat[b] = ga
        prod = ga.astype(F32) * att[b].astype(F32)
        dmat[b] = lax.dot_general(pick, prod, NT, precision=lax.Precision.HIGHEST, preferred_element_type=F32)
        k_t[:, b * rows:(b + 1) * rows] = k[b].astype(F32).T.astype(BF)
    dk[...] = jnp.zeros_like(dk)
    dv[...] = jnp.zeros_like(dv)

    def head(h, carry):
        own = lane == h
        for qb in range(blocks):
            qm = jnp.where(own, q[qb], jnp.zeros_like(q[qb]))
            gm = jnp.where(own, gat[qb], jnp.zeros_like(gat[qb]))
            log_total = lse[h, qb:qb + 1, :]
            row_dot = dmat[qb, pl.ds(h, 1), :]
            acc = jnp.zeros((64, rows), F32)
            for kb in range(qb + 1):
                prob = jnp.exp(dot(k[kb], qm, NT) * SCALE - log_total)
                dprob = dot(v[kb], gm, NT)
                ds = (prob * (dprob - row_dot)).astype(BF)
                dv[kb] += dot(prob.astype(BF), gm)
                dk[kb] += dot(ds, qm)
                acc = acc + dot(k_t[pl.ds(pl.multiple_of(h * 64, 64), 64), kb * rows:(kb + 1) * rows], ds)
            dq_t[qb, pl.ds(pl.multiple_of(h * 64, 64), 64), :] = acc
        return carry

    lax.fori_loop(0, heads, head, 0)
    quarter = rows // 4
    total = jnp.zeros((1, width), F32)
    gains = [jnp.zeros((1, half), F32) for _ in range(2)]
    for b in range(blocks):
        cosine, sine = signed_tables(cos, sin, b, width, lane_full)
        gq = dq_t[b].T * SCALE
        gk = dk[b] * SCALE
        gv = dv[b]
        grads = [
            (gq * cosine - half_swap(gq, lane_full) * sine).astype(BF),
            (gk * cosine - half_swap(gk, lane_full) * sine).astype(BF),
            (mix[...] * gv).astype(BF),
        ]
        for i, n in enumerate((na, nb)):
            lanes = slice(i * half, (i + 1) * half)
            og2[:width, lanes] += dot(grads[0], n[b], TN)
            og2[width:, lanes] += dot(grads[1], n[b], TN)
            og[width:, lanes] += dot(grads[2], n[b], TN)
        x = jnp.concatenate([p0[b], p1[b], p2[b], p3[b]], axis=0).astype(F32)
        x = x * lax.rsqrt(jnp.mean(x * x, axis=-1, keepdims=True) + EPSILON)
        for i, w in enumerate((wa, wb)):
            lanes = slice(i * half, (i + 1) * half)
            part = sum(dot(grad, w[j], NT) for j, grad in enumerate(grads))
            gains[i] = gains[i] + jnp.sum(part * x[:, lanes], axis=0, keepdims=True)
            for p, out in enumerate((keep_o, pass_o)):
                out[b, :, lanes] = part[p * quarter:(p + 1) * quarter]
            for p in range(2):
                send_o[p, b, :, lanes] = part[(2 + p) * quarter:(3 + p) * quarter].astype(BF)
        gf = ((1.0 - mix[...]) * gv).astype(BF)
        for r in range(4):
            gf_o[b, seg[r]] = gf[r * quarter:(r + 1) * quarter]
        total = total + jnp.sum(gv * diff[b], axis=0, keepdims=True)
    row = lax.broadcasted_iota(jnp.int32, (16, half), 0)
    mixed = jnp.concatenate([total, jnp.zeros((1, half - width), F32)], axis=1)
    for i, (out, out2) in enumerate(((own_o, own2_o), (other_o, other2_o))):
        lanes = slice(i * half, (i + 1) * half)
        extra = jnp.where(row == 0, gains[i], jnp.where(row == 1, gain_in[:, lanes], jnp.where(row == 2, mixed, 0.0)))
        out[:2 * width] = og[:, lanes].astype(out.dtype)
        out[2 * width:] = extra.astype(out.dtype)
        out2[...] = og2[:, lanes].astype(out.dtype)


def place_kernel(where, roll, *refs):
    pieces, out = refs[:-1], refs[-1]
    width = out.shape[-1]
    half = width // 2
    for r, piece in enumerate(pieces):
        value = piece[0]
        low, high = value[:, :half], value[:, half:]
        swap = roll[0] == 1
        out[0, where[r], :, :half] = jnp.where(swap, high, low).astype(out.dtype)
        out[0, where[r], :, half:] = jnp.where(swap, low, high).astype(out.dtype)


def first_kernel(got, out):
    out[...] = got[...].astype(out.dtype)


def on_device(
    fsdp, ctx, tp,
    tokens, first_values, out_grad, w_qkv, output_weight, w_gate, w_up, w_down, gain_attn, gain_mlp, mix,
):
    seqs, block, width = tokens.shape
    local = w_qkv.shape[2]
    hidden_width = w_gate.shape[1]
    quarter = block // tp
    half = width // 2
    pair = fsdp == 2
    assert seqs == ctx and ctx == 4 and tp == 4 and local <= half
    y = lax.axis_index("fsdp")
    z = lax.axis_index("ctx")
    t = lax.axis_index("tp")
    swap_y = [(0, 1), (1, 0)]
    by_core = [(i, i ^ 1) for i in range(tp)]
    by_x = [(i, i ^ 2) for i in range(tp)]

    def tie(*values):
        return lax.optimization_barrier(values)

    def core(value):
        return lax.ppermute(value, "tp", by_core)

    def across(value):
        return lax.ppermute(value, "tp", by_x)

    def other_half(value, axis):
        if pair:
            return value, lax.ppermute(value, "fsdp", swap_y)
        whole = lax.all_gather(value, "fsdp", axis=axis, tiled=True)
        return tuple(lax.slice_in_dim(whole, i * half, (i + 1) * half, axis=axis) for i in range(2))

    def added(keep, got):
        return keep + got.astype(F32)

    rows = ctx * block
    smem = pl.BlockSpec(memory_space=pltpu.SMEM)
    piece_spec = pl.BlockSpec((1, quarter, width), lambda b: (b, 0, 0))
    block_local = pl.BlockSpec((1, block, local), lambda b: (b, 0, 0))
    block_half = pl.BlockSpec((1, block, half), lambda b: (b, 0, 0))
    block_hidden = pl.BlockSpec((1, block, hidden_width), lambda b: (b, 0, 0))
    block_table = pl.BlockSpec((1, block, 128), lambda b: (b, 0, 0))
    part_specs = [piece_spec] * 2 + [pl.BlockSpec((2, 1, quarter, width), lambda b: (0, b, 0, 0))]
    first_part = pl.BlockSpec((1, 1, quarter, width), lambda b: (0, b, 0, 0))
    gain_spec = full((1, width))
    send_shape = shape_of((2, ctx, quarter, width), BF)
    own_f32 = shape_of((ctx, quarter, width), F32)
    own_low = shape_of((ctx, quarter, width), BF)
    part_shapes = [own_f32, own_f32, send_shape]
    part_away = [away(own_f32), own_f32, send_shape]
    rows_local = shape_of((ctx, block, local), BF)
    rows_half = shape_of((ctx, block, half), BF)
    rows_hidden = shape_of((ctx, block, hidden_width), BF)
    gain_row = shape_of((1, width), F32)

    seg = jnp.stack([t, t ^ 2, t ^ 1, t ^ 3]).astype(jnp.int32)
    turn = y if pair else y * 0
    roll = jnp.reshape(turn, (1,)).astype(jnp.int32)
    where = jnp.stack([t, t ^ 2, turn, 1 - turn]).astype(jnp.int32)

    def own_rows(value, count):
        return call(
            functools.partial(own_kernel, count),
            [own_low] * count,
            where, value.reshape(seqs, tp, quarter, width),
            in_specs=[smem, pl.BlockSpec(memory_space=pltpu.HBM)],
            scratch=[pltpu.SemaphoreType.DMA((2 * count,))],
            name="own", vmem=4,
        )

    (x_part,) = own_rows(tokens, 1)
    place = (seg[:, None] * quarter + jnp.arange(quarter)[None, :]).reshape(block)
    positions = (jnp.arange(ctx)[:, None] * block + place[None, :]).astype(F32)
    lanes = (jnp.arange(128) % 32).astype(F32)
    table = positions[:, :, None] * (10000.0 ** (-lanes / 32.0))[None, None, :]
    cosine, sine = jnp.cos(table), jnp.sin(table)
    mix_row = jnp.repeat(mix, local // mix.shape[0])[None, :]

    qkv_a, qkv_b = other_half(jnp.transpose(w_qkv, (1, 0, 2)), 1)
    out_a, out_b = other_half(
        jnp.concatenate([output_weight, jnp.stack([gain_attn, gain_mlp])], axis=0), 1
    )
    gate_a, gate_b = other_half(w_gate.T, 1)
    up_a, up_b = other_half(w_up.T, 1)
    early = hidden_width // 4 // 64 * 64
    down_a, down_b = other_half(w_down[:early], 1)
    late_a, late_b = other_half(w_down[early:], 1)

    x_own = lax.all_to_all(x_part, "ctx", 0, 0)
    x_second = across(x_own)
    x_own, qkv_b, cosine, sine, mix_row, g_part, g_late = tie(
        x_own, qkv_b, cosine, sine, mix_row, *own_rows(out_grad, 2)
    )
    fv = lax.all_to_all(first_values, "ctx", 0, 0).reshape(ctx, tp, quarter, local)
    gains = jnp.concatenate([out_a[local:], out_b[local:]], axis=1).astype(F32)
    x_core = core(x_own)
    x_second, out_b, gains = tie(x_second, out_b[:local], gains)
    x_both = core(x_second)
    x_core, x_both, fv, g_part = tie(x_core, x_both, fv, g_part)
    x_pieces = (x_own, x_second, x_core, x_both)
    out_a = output_weight if pair else out_a[:local]
    gain_first, gain_second = gains[0:1], gains[1:2]
    g_first = lax.all_to_all(g_part, "ctx", 0, 0)
    norm_a, norm_b, queries, keys, values, diff, attended, log_total, keep, onward, send = call(
        attend_kernel,
        [away(item) for item in [rows_half] * 2 + [rows_local] * 3 + [
            shape_of((ctx, block, local), F32), rows_local,
        ]] + [shape_of((mix.shape[0], ctx, block), F32)] + part_away,
        seg, *x_pieces, gain_first, qkv_a, qkv_b, fv, cosine, sine, mix_row, out_a, out_b,
        in_specs=[smem] + [pl.BlockSpec(memory_space=pltpu.VMEM)] * 13,
        scratch=[pltpu.VMEM((local, rows), BF), pltpu.VMEM((ctx, local, block), F32)],
        name="attend", vmem=16,
    )
    send, gate_b, g_first, g_late = tie(send, gate_b, g_first, g_late)
    got_core = core(send)
    got_x = across(added(onward, got_core[1]).astype(BF))
    g_second = lax.all_to_all(g_late, "ctx", 0, 0)
    got_x, up_b, down_b, g_second = tie(got_x, up_b, down_b, g_second)
    residual, normed_own = call(
        residual_kernel,
        [own_f32, own_low],
        x_own, keep, got_core, got_x, gain_second,
        grid=(ctx,),
        in_specs=[piece_spec, piece_spec, first_part, piece_spec, gain_spec],
        out_specs=[piece_spec, piece_spec],
        name="residual_norm", vmem=6, us=20,
    )
    down_specs = [full((n, half)) for n in (early, hidden_width - early)] * 2
    n_second = across(normed_own)
    mlp_a, mlp_b, last_a, last_b, hidden, grad_gate, grad_up, keep, onward, send = call(
        mlp_kernel,
        [rows_half] * 4 + [rows_hidden] * 3 + part_shapes,
        normed_own, n_second, core(normed_own), core(n_second), g_first, g_second, core(g_first), core(g_second),
        gate_a, gate_b, up_a, up_b, down_a, late_a, down_b, late_b,
        grid=(ctx,),
        in_specs=[piece_spec] * 8 + [full((hidden_width, half))] * 4 + down_specs,
        out_specs=[block_half] * 4 + [block_hidden] * 3 + part_specs,
        name="mlp", vmem=24, us=10,
    )

    def placed(*pieces):
        *pieces, dtype = pieces
        return call(
            place_kernel,
            [shape_of((seqs, tp, quarter, width), dtype)],
            seg, roll, *pieces,
            grid=(seqs,),
            in_specs=[smem, smem] + [piece_spec] * 4,
            out_specs=[pl.BlockSpec((1, tp, quarter, width), lambda b: (b, 0, 0, 0))],
            name="place", vmem=6,
        )[0].reshape(seqs, block, width)

    def weight_grad(left, right):
        return lax.dot_general(
            left.reshape(rows, -1), right.reshape(rows, -1), TN, preferred_element_type=F32
        )

    def exchange(first, second, axis=1):
        if pair:
            return lax.ppermute(second, "fsdp", swap_y)
        return lax.psum_scatter(
            jnp.concatenate([first.astype(BF), second], axis=axis), "fsdp", scatter_dimension=axis, tiled=True
        )

    def joined(first, received):
        return (first + received.astype(F32)).astype(BF) if pair else received

    def plus(shard, received):
        return (shard.astype(F32) + received.astype(F32)).astype(BF)

    def toward(shard):
        return lax.ppermute(shard, "ctx", [(0, 1), (3, 2)])

    def meet(shard):
        return lax.ppermute(shard, "ctx", [(1, 2), (2, 1)])

    def back(shard):
        return lax.ppermute(shard, "ctx", [(1, 0), (2, 3)])

    def settled(shard, received):
        return jnp.where((z == 0) | (z == 3), received, shard).astype(F32)

    got_core = core(send)
    gate_first = weight_grad(grad_gate, mlp_a)
    gate_second = weight_grad(grad_gate, mlp_b).astype(BF)
    onward = added(onward, got_core[1]).astype(BF)

    onward, gate_first, gate_second, grad_up, hidden = tie(onward, gate_first, gate_second, grad_up, hidden)
    got_x = across(onward)
    gate_got = exchange(gate_first, gate_second)
    up_first = weight_grad(grad_up, mlp_a)
    up_second = weight_grad(grad_up, mlp_b).astype(BF)
    down_first = weight_grad(hidden, last_a)
    down_second = weight_grad(hidden, last_b).astype(BF)
    down_keep, down_onward, down_send = call(
        down_kernel,
        part_shapes,
        hidden, down_a, late_a, down_b, late_b,
        grid=(ctx,),
        in_specs=[block_hidden] + down_specs,
        out_specs=part_specs,
        name="down", vmem=12,
    )
    down_core = core(down_send)
    down_onward = added(down_onward, down_core[1]).astype(BF)
    grad_residual, branch_own, gain_sum_second = call(
        norm_back_kernel,
        [own_f32, own_low, gain_row],
        g_first, keep, got_core, got_x, residual, gain_second,
        grid=(ctx,),
        in_specs=[piece_spec, piece_spec, first_part, piece_spec, piece_spec, gain_spec],
        out_specs=[piece_spec, piece_spec, gain_spec],
        name="norm_back_mlp", vmem=6, us=20,
    )
    (
        branch_own, grad_residual, gate_first, up_first, up_second, down_first, down_second, down_onward,
    ) = tie(
        branch_own, grad_residual, gate_first, up_first, up_second, down_first, down_second, down_onward,
    )
    grad_residual, gate_got = tie(grad_residual, gate_got)

    b_second = across(branch_own)
    b_core = core(branch_own)
    b_both = core(b_second)
    up_got = exchange(up_first, up_second)
    gate_shard = joined(gate_first, gate_got)
    gate_more = toward(gate_shard)
    (
        b_second, b_core, b_both, up_got, gate_shard, gate_more, down_onward, down_second,
    ) = tie(b_second, b_core, b_both, up_got, gate_shard, gate_more, down_onward, down_second)

    down_x = across(down_onward)
    down_got = exchange(down_first, down_second)
    gate_shard = plus(gate_shard, gate_more)
    gate_more = meet(gate_shard)
    up_shard = joined(up_first, up_got)
    up_more = toward(up_shard)
    payload = [shape_of((2 * local + n, half), kind) for n in (16, 0) for kind in (F32, BF)]
    gf, keep, onward, send, out_first, out_second, qk_first, qk_second = call(
        attend_back_kernel,
        [away(shape_of((ctx, tp, quarter, local), BF)), *part_away, *[away(item) for item in payload]],
        seg, branch_own, b_second, b_core, b_both, out_a, out_b,
        queries, keys, values, attended, log_total, cosine, sine, mix_row, diff,
        *x_pieces, qkv_a, qkv_b, norm_a, norm_b, gain_sum_second,
        in_specs=[smem] + [pl.BlockSpec(memory_space=pltpu.VMEM)] * 24,
        scratch=[
            pltpu.VMEM((ctx, block, local), BF),
            pltpu.VMEM((ctx, 8, block), F32),
            pltpu.VMEM((local, rows), BF),
            pltpu.VMEM((ctx, block, local), F32),
            pltpu.VMEM((ctx, block, local), F32),
            pltpu.VMEM((ctx, local, block), F32),
            pltpu.VMEM((2 * local, width), F32),
            pltpu.VMEM((2 * local, width), F32),
        ],
        name="attend_back", vmem=30, us=30,
    )
    send, down_got, gate_more, up_more, down_x = tie(send, down_got, gate_more, up_more, down_x)
    got_core = core(send)
    onward = added(onward, got_core[1]).astype(BF)
    gate_shard = plus(gate_shard, gate_more)
    up_shard = plus(up_shard, up_more)
    down_shard = joined(down_first, down_got)
    onward, qk_second, out_second, gate_shard, up_shard, down_shard, down_x = tie(
        onward, qk_second, out_second, gate_shard, up_shard, down_shard, down_x
    )

    got_x = across(onward)
    gate_more = back(gate_shard)
    up_more = meet(up_shard)
    down_more = toward(down_shard)
    qk_got = exchange(qk_first, qk_second)
    output_own = (residual + added(down_keep, down_core[0]) + down_x.astype(F32)).astype(BF)
    _, tokens_own, _ = call(
        norm_back_kernel,
        [own_f32, own_low, gain_row],
        grad_residual, keep, got_core, got_x, x_own, gain_first,
        grid=(ctx,),
        in_specs=[piece_spec, piece_spec, first_part, piece_spec, piece_spec, gain_spec],
        out_specs=[piece_spec, piece_spec, gain_spec],
        name="norm_back_attn", vmem=6, us=20,
    )
    tokens_own, output_own, gf, out_second, gate_shard, up_shard, down_shard = tie(
        tokens_own, output_own, gf, out_second, gate_shard, up_shard, down_shard
    )

    tokens_home = lax.all_to_all(tokens_own, "ctx", 0, 0)
    out_got = exchange(out_first, out_second)
    grad_w_gate = settled(gate_shard, gate_more).T
    up_shard = plus(up_shard, up_more)
    down_shard = plus(down_shard, down_more)
    qk_shard = joined(qk_first, qk_got)
    tokens_home, output_own, gf, grad_w_gate, up_shard, down_shard, qk_shard = tie(
        tokens_home, output_own, gf, grad_w_gate, up_shard, down_shard, qk_shard
    )
    tokens_second = across(tokens_home)
    tokens_core = core(tokens_home)
    up_more = back(up_shard)
    down_more = meet(down_shard)
    qk_more = toward(qk_shard)
    out_shard = joined(out_first, out_got)
    out_more = toward(out_shard)
    tokens_second, output_own, gf, up_more, down_more, qk_more = tie(
        tokens_second, output_own, gf, up_more, down_more, qk_more
    )
    output_home = lax.all_to_all(output_own, "ctx", 0, 0)
    down_shard = plus(down_shard, down_more)
    down_more = back(down_shard)
    qk_shard = plus(qk_shard, qk_more)
    qk_more = meet(qk_shard)
    grad_tokens = placed(tokens_home, tokens_second, tokens_core, core(tokens_second), F32)
    grad_w_up = settled(up_shard, up_more).T
    output_home, gf, grad_tokens, grad_w_up, out_more = tie(output_home, gf, grad_tokens, grad_w_up, out_more)
    output_second = across(output_home)
    output_core = core(output_home)
    first_home = lax.all_to_all(gf, "ctx", 0, 0)
    qk_shard = plus(qk_shard, qk_more)
    qk_more = back(qk_shard)
    out_shard = plus(out_shard, out_more)
    out_more = meet(out_shard)
    grad_w_down = settled(down_shard, down_more)
    out_shard = plus(out_shard, out_more)
    out_more = back(out_shard)
    output = placed(output_home, output_second, output_core, core(output_second), BF)
    grad_first = first_home.reshape(seqs, block, local).astype(F32)
    qk_full = settled(qk_shard, qk_more).T
    output, grad_first, grad_w_down, qk_full, out_more = tie(output, grad_first, grad_w_down, qk_full, out_more)
    out_full = settled(out_shard, out_more)
    v_full = out_full[local:2 * local].T
    grad_w_qkv = jnp.stack([qk_full[:, :local], qk_full[:, local:], v_full], axis=1)
    grad_w_out = out_full[:local]

    share = gain_attn.shape[0]
    gain_grads = out_full[2 * local:2 * local + 2]
    for move in (core, across):
        gain_grads = gain_grads + move(gain_grads)
    mixed = out_full[2 * local + 2:2 * local + 3]
    if not pair:
        mixed = lax.all_gather(mixed, "fsdp", axis=1, tiled=True)
    mixed = mixed[:, :local]
    grad_mix = jnp.sum(mixed.reshape(mix.shape[0], -1), axis=1)
    return (
        output, grad_tokens, grad_first, grad_w_qkv, grad_w_out, grad_w_gate, grad_w_up, grad_w_down,
        gain_grads[0, :share], gain_grads[1, :share], grad_mix,
    )


def solution(mesh):
    rows = P("fsdp", "ctx", None)
    in_specs = (
        rows, P("fsdp", "ctx", "tp"), rows, P("fsdp", None, "tp"), P("tp", "fsdp"), P("fsdp", "tp"),
        P("fsdp", "tp"), P("tp", "fsdp"), P("fsdp"), P("fsdp"), P("tp"),
    )
    out_specs = (
        rows, rows, P("fsdp", "ctx", "tp"), P("fsdp", None, "tp"), P("tp", "fsdp"), P("fsdp", "tp"),
        P("fsdp", "tp"), P("tp", "fsdp"), P("fsdp"), P("fsdp"), P("tp"),
    )
    sizes = [mesh.shape[name] for name in ("fsdp", "ctx", "tp")]
    return jax.shard_map(
        functools.partial(on_device, *sizes), mesh=mesh, in_specs=in_specs, out_specs=out_specs,
        check_vma=False,
    )
```
